512 devices in a mesh: ctx: 32 (over y_lo, z), fsdp: 16 (over y_hi, x, core).
Axes of the slice: x: 4, y: 4 (y_hi: 2, y_lo: 2; y = y_hi * 2 + y_lo), z: 16, core: 2. Of those that a mesh axis runs over, the one named last changes fastest.
Arguments:
- sig_raw: bfloat16 [4096, 8192], P('ctx', 'fsdp'), may hold values from -6 to 6
- map_raw: bfloat16 [4096, 2048], P('ctx'), may hold values from -1.796875 to 1.796875
- step_size_logits: float32 [4096, 128], P('ctx', 'fsdp'), may hold values from -5.4 to 21.5
- d_out: bfloat16 [4096, 8192], P('ctx', 'fsdp'), may hold values from -6 to 6
- sig_taps: float32 [4, 8192], P(None, 'fsdp'), may hold values from -3 to 3
- map_taps: float32 [4, 2048], P(None, 'fsdp'), may hold values from -3 to 3
- sig_bias: float32 [8192], P('fsdp'), may hold values from -3 to 3
- map_bias: float32 [2048], P('fsdp'), may hold values from -0.6 to 0.6
- a_log: float32 [128], P('fsdp'), as said below
- dt_bias: float32 [128], P('fsdp'), may hold values from -5 to -4.2
- skip_gain: float32 [128], P('fsdp'), may hold values from 0.1 to 3
Outputs:
- d_sig: float32 [4096, 8192], P('ctx', 'fsdp')
- d_map: float32 [4096, 2048], P('ctx', 'fsdp')
- d_dt: float32 [4096, 128], P('ctx', 'fsdp')
- d_sig_taps: float32 [4, 8192], P(None, 'fsdp')
- d_map_taps: float32 [4, 2048], P(None, 'fsdp')
- d_sig_bias: float32 [8192], P('fsdp')
- d_map_bias: float32 [2048], P('fsdp')
- d_a_log: float32 [128], P('fsdp')
- scaled_timestep_shift_grad: float32 [128], P('fsdp')
- d_skip: float32 [128], P('fsdp')
The draws below stay inside these ranges and needn't reach their ends.
Inputs may be any that keep to these rules, and one draw needn't show every extreme that they name: Each head's rate exp(a_log) lies either between 2 and 4 or between 30 / 4096 and 200 / 4096.
All inputs are finite; a program needn't handle non-finite values.
Results may differ from the reference program's by a relative error of at most 0.0066.
Values may be sent and summed in bfloat16 or wider, within the bound.
A program may use at most 128 MiB of HBM per device.

```python
import math
import jax
import jax.numpy as jnp
import numpy as np
from jax import lax

HEADS = 128
HDIM = 64
STATE = 128
GROUPS = 8
KSIZE = 4
BLK = 64
TOKEN_COUNT = 4096
CH = 10240
N_CTX = 32


def draw_a_log(key, part):
    kind_key, slow_key, quick_key = jax.random.split(key, 3)
    quick = jax.random.randint(kind_key, (HEADS,), 0, 2) == 0
    span = 0.01 * TOKEN_COUNT
    slow_log = jax.random.uniform(slow_key, (HEADS,), jnp.float32, jnp.log(0.3 / span), jnp.log(2.0 / span))
    quick_log = jax.random.uniform(quick_key, (HEADS,), jnp.float32, jnp.log(2.0), jnp.log(4.0))
    return jnp.where(quick, quick_log, slow_log)


def draw_step_size_logits(key, part):
    base_key, place_lookup, height_key = jax.random.split(key, 3)
    starting_shift = jnp.clip(0.5 * jax.random.normal(base_key, (TOKEN_COUNT, HEADS), jnp.float32), -1.5, 1.5)
    spike_place = jax.random.randint(place_lookup, (TOKEN_COUNT, HEADS), 0, 1024) == 0
    raised_by = jax.random.uniform(height_key, (TOKEN_COUNT, HEADS), jnp.float32, 10.0, 20.0)
    return starting_shift + jnp.where(spike_place, raised_by, 0.0)


def block_scale(own_key, shape, cuts, low, top_value):
    def one(dim, blocks):
        steps = jax.random.uniform(jax.random.fold_in(jax.random.fold_in(own_key, 6), dim), (blocks,), jnp.float32, low / len(cuts), top_value / len(cuts))
        return jnp.repeat(jnp.exp(steps), shape[dim] // blocks).reshape((-1,) + (1,) * (len(shape) - dim - 1))

    factor_of = one(*cuts[0])
    for cut in cuts[1:]:
        factor_of = factor_of * one(*cut)
    return factor_of


def gaussian(own_key, shape, deviation, bound, cuts=(), kind=jnp.bfloat16):
    drawn = deviation * jax.random.normal(own_key, shape, jnp.float32)
    if cuts:
        drawn = drawn * block_scale(own_key, shape, cuts, -0.22, 0.18)
    return jnp.clip(drawn, -bound, bound).astype(kind)


def setup_inputs(seed: int = 0) -> dict:
    key_list = jax.random.split(jax.random.key(seed), 12)
    sig_raw = gaussian(key_list[0], (TOKEN_COUNT, HEADS * HDIM), 1.0, 6.0, ((0, 32), (1, 16)))
    map_raw = gaussian(key_list[1], (TOKEN_COUNT, 2 * GROUPS * STATE), 0.3, 1.796875, ((0, 32),))
    step_size_logits = draw_step_size_logits(jax.random.fold_in(key_list[11], 71), 0)
    d_out = gaussian(key_list[3], (TOKEN_COUNT, HEADS * HDIM), 1.0, 6.0, ((0, 32), (1, 16)))
    sig_taps = gaussian(key_list[4], (KSIZE, HEADS * HDIM), KSIZE ** -0.5, 3.0, ((1, 16),), jnp.float32)
    map_taps = gaussian(key_list[5], (KSIZE, 2 * GROUPS * STATE), KSIZE ** -0.5, 3.0, ((1, 16),), jnp.float32)
    sig_bias = gaussian(key_list[6], (HEADS * HDIM,), 0.5, 3.0, ((0, 16),), jnp.float32)
    map_bias = gaussian(key_list[7], (2 * GROUPS * STATE,), 0.1, 0.6, ((0, 16),), jnp.float32)
    a_log = draw_a_log(jax.random.fold_in(key_list[11], 71), 0)
    dt_bias = jnp.clip(-5.0 + 0.8000002 * jax.random.uniform(key_list[9], (HEADS,), jnp.float32) ** block_scale(key_list[9], (HEADS,), ((0, 16),), -0.2, 0.2), -5.0, -4.2)
    skip_gain = jnp.clip(jnp.exp(math.log(3.0) - 3.4011974 * jax.random.uniform(key_list[10], (HEADS,), jnp.float32) ** block_scale(key_list[10], (HEADS,), ((0, 16),), -0.2, 0.2)), 0.1, 3.0)
    return {"sig_raw": sig_raw, "map_raw": map_raw, "step_size_logits": step_size_logits, "d_out": d_out, "sig_taps": sig_taps, "map_taps": map_taps, "sig_bias": sig_bias, "map_bias": map_bias, "a_log": a_log, "dt_bias": dt_bias, "skip_gain": skip_gain}


def ein(form, left, right):
    return jnp.einsum(form, left.astype(jnp.float32), right.astype(jnp.float32))

def silu_slope(value):
    sig = jax.nn.sigmoid(value)
    return sig * (1.0 + value * (1.0 - sig))

def block_parts(activated, dt_rows, a_log, dt_bias, groups):
    length = activated.shape[0]
    heads = dt_rows.shape[1]
    inner = heads * HDIM
    shared = groups * STATE
    ratio = heads // groups
    signal = activated[:, :inner].reshape(length, heads, HDIM)
    input_map = activated[:, inner:inner + shared].reshape(length, groups, STATE)
    output_map = activated[:, inner + shared:].reshape(length, groups, STATE)
    input_heads = jnp.repeat(input_map, ratio, axis=1)
    output_heads = jnp.repeat(output_map, ratio, axis=1)
    step = jax.nn.softplus(dt_rows + dt_bias)
    rate = -jnp.exp(a_log)
    row_ids = lax.broadcasted_iota(jnp.int32, (length, length), 0)
    col_ids = lax.broadcasted_iota(jnp.int32, (length, length), 1)
    lower = (row_ids >= col_ids).astype(jnp.float32)
    decay_sum = jnp.dot(lower, step * rate, precision=lax.Precision.HIGHEST)
    to_end = jnp.exp(decay_sum[-1][None, :] - decay_sum)
    scaled = (signal.astype(jnp.float32) * step[:, :, None]).astype(jnp.bfloat16)
    weighted = (scaled.astype(jnp.float32) * to_end[:, :, None]).astype(jnp.bfloat16)
    local = ein('qhp,qhn->hpn', weighted, input_heads)
    return (signal, input_map, output_map, input_heads, output_heads, step, rate, lower, decay_sum, scaled, to_end, weighted, local)

def entry_grad(parts, d_rows):
    decay_sum = parts[8]
    output_heads = parts[4]
    scaled_grad = (d_rows.astype(jnp.float32) * jnp.exp(decay_sum)[:, :, None]).astype(jnp.bfloat16)
    return (scaled_grad, ein('thp,thn->hpn', scaled_grad, output_heads))

def block_grads(parts, d_rows, scaled_grad, h_in, carried, skip_gain, dt_rows, dt_bias):
    signal, input_map, output_map, input_heads, output_heads, step, rate, lower, decay_sum, scaled, to_end, weighted, local = parts
    length = d_rows.shape[0]
    heads = d_rows.shape[1]
    groups = input_map.shape[1]
    width_state = input_map.shape[2]
    ratio = heads // groups
    grad_f = d_rows.astype(jnp.float32)
    signal_f = signal.astype(jnp.float32)
    grad_skip = lax.optimization_barrier(jnp.sum(grad_f * signal_f, axis=(0, 2)))
    h_low = h_in.astype(jnp.bfloat16)
    carried_low = carried.astype(jnp.bfloat16)
    offset = jnp.exp(decay_sum)[:, :, None] * ein('thn,hpn->thp', output_heads, h_low)
    grad_sum = lax.optimization_barrier(jnp.sum(grad_f * offset, axis=2))
    out_heads_grad = ein('thp,hpn->thn', scaled_grad, h_low)
    grad_weighted = ein('shn,hpn->shp', input_heads, carried_low)
    in_heads_grad = ein('shp,hpn->shn', weighted, carried_low)
    back = lax.optimization_barrier(jnp.sum(grad_weighted * scaled.astype(jnp.float32), axis=2)) * to_end
    end_term = jnp.exp(decay_sum[-1]) * lax.optimization_barrier(jnp.sum(h_in * carried, axis=(1, 2)))
    last_row = (lax.broadcasted_iota(jnp.int32, (length, 1), 0) == length - 1).astype(jnp.float32)
    grad_sum = grad_sum - back + last_row * (lax.optimization_barrier(jnp.sum(back, axis=0)) + end_term)[None, :]
    spread = decay_sum.T[:, :, None] - decay_sum.T[:, None, :]
    decay = jnp.where(lower[None] > 0, jnp.exp(jnp.minimum(spread, 0.0)), 0.0)
    score = ein('tgn,sgn->gts', output_map, input_map)
    mix = jnp.repeat(score, ratio, axis=0) * decay
    grad_mix = ein('thp,shp->hts', d_rows, scaled)
    grad_scaled = grad_weighted * to_end[:, :, None] + ein('hts,thp->shp', mix.astype(jnp.bfloat16), d_rows)
    product = grad_mix * mix
    grad_sum = grad_sum + (lax.optimization_barrier(jnp.sum(product, axis=2)) - lax.optimization_barrier(jnp.sum(product, axis=1))).T
    grad_score = lax.optimization_barrier(jnp.sum((grad_mix * decay).reshape(groups, ratio, length, length), axis=1)).astype(jnp.bfloat16)
    grad_outmap = ein('gts,sgn->tgn', grad_score, input_map) + lax.optimization_barrier(jnp.sum(out_heads_grad.reshape(length, groups, ratio, width_state), axis=2))
    grad_in = ein('gts,tgn->sgn', grad_score, output_map) + lax.optimization_barrier(jnp.sum(in_heads_grad.reshape(length, groups, ratio, width_state), axis=2))
    grad_log = jnp.dot(lower.T, grad_sum, precision=lax.Precision.HIGHEST)
    descent_increment = grad_log * rate + lax.optimization_barrier(jnp.sum(grad_scaled * signal_f, axis=2))
    grad_signal = skip_gain[None, :, None] * grad_f + grad_scaled * step[:, :, None]
    grad_dt = descent_increment * jax.nn.sigmoid(dt_rows + dt_bias)
    decay_log_gradient = lax.optimization_barrier(jnp.sum(grad_log * step, axis=0)) * rate
    grad_act = jnp.concatenate([grad_signal.reshape(length, heads * HDIM), grad_in.reshape(length, groups * width_state), grad_outmap.reshape(length, groups * width_state)], axis=1)
    return (grad_act, grad_dt, decay_log_gradient, lax.optimization_barrier(jnp.sum(grad_dt, axis=0)), grad_skip)

def reference(sig_raw, map_raw, step_size_logits, d_out, sig_taps, map_taps, sig_bias, map_bias, a_log, dt_bias, skip_gain):
    blocks = 2 * N_CTX
    order = np.array([2 * p if p < N_CTX else 2 * (blocks - 1 - p) + 1 for p in range(blocks)], dtype=np.int32)
    back_order = np.argsort(order).astype(np.int32)

    def unzig(array):
        return array.reshape((blocks, BLK) + array.shape[1:])[order].reshape(array.shape)

    def rezig(array):
        return array.reshape((blocks, BLK) + array.shape[1:])[back_order].reshape(array.shape)
    sig_width = HEADS * HDIM
    raw_rows = jnp.concatenate([unzig(sig_raw), unzig(map_raw)], axis=1)
    conv_weight = jnp.concatenate([sig_taps, map_taps], axis=1)
    conv_bias = jnp.concatenate([sig_bias, map_bias], axis=0)
    dt_rows = unzig(step_size_logits)
    grad_rows = unzig(d_out)
    padded = jnp.concatenate([jnp.zeros((KSIZE - 1, CH), jnp.float32), raw_rows.astype(jnp.float32)], axis=0)
    preact = conv_bias[None, :] + jnp.zeros((TOKEN_COUNT, CH), jnp.float32)
    for tap in range(KSIZE):
        preact = preact + conv_weight[tap][None, :] * padded[tap:tap + TOKEN_COUNT]
    activated = jax.nn.silu(preact).astype(jnp.bfloat16)
    act_blocks = activated.reshape(blocks, BLK, CH)
    step_size_blocks = dt_rows.reshape(blocks, BLK, HEADS)
    grad_blocks = grad_rows.reshape(blocks, BLK, HEADS, HDIM)

    def first_pass(entry):
        parts = block_parts(entry[0], entry[1], a_log, dt_bias, GROUPS)
        scaled_grad, state_grad = entry_grad(parts, entry[2])
        return (parts[8][-1], parts[12], state_grad)
    ends, locals_all, state_grads = lax.map(first_pass, (act_blocks, step_size_blocks, grad_blocks))
    zero_state = jnp.zeros((HEADS, HDIM, STATE), jnp.float32)

    def forward_link(state, entry):
        return (jnp.exp(entry[0])[:, None, None] * state + entry[1], state)
    _, h_ins = lax.scan(forward_link, zero_state, (ends, locals_all))

    def backward_link(state, entry):
        return (entry[1] + jnp.exp(entry[0])[:, None, None] * state, state)
    _, carried = lax.scan(backward_link, zero_state, (ends, state_grads), reverse=True)

    def second_pass(entry):
        parts = block_parts(entry[0], entry[1], a_log, dt_bias, GROUPS)
        scaled_grad, state_grad = entry_grad(parts, entry[2])
        return block_grads(parts, entry[2], scaled_grad, entry[3], entry[4], skip_gain, entry[1], dt_bias)
    grad_act, grad_dt, decay_log_gradient, grad_dtb, grad_skip = lax.map(second_pass, (act_blocks, step_size_blocks, grad_blocks, h_ins, carried))
    grad_pre = grad_act.reshape(TOKEN_COUNT, CH) * silu_slope(preact)
    padded_next = jnp.concatenate([grad_pre, jnp.zeros((KSIZE - 1, CH), jnp.float32)], axis=0)
    grad_raw = jnp.zeros((TOKEN_COUNT, CH), jnp.float32)
    for tap in range(KSIZE):
        grad_raw = grad_raw + conv_weight[tap][None, :] * padded_next[KSIZE - 1 - tap:KSIZE - 1 - tap + TOKEN_COUNT]
    grad_taps = jnp.stack([lax.optimization_barrier(jnp.sum(grad_pre * padded[tap:tap + TOKEN_COUNT], axis=0)) for tap in range(KSIZE)])
    bias_grad = lax.optimization_barrier(jnp.sum(grad_pre, axis=0))
    stored = rezig(grad_raw)
    scale = 1.0 / np.sqrt(float(TOKEN_COUNT))
    return (stored[:, :sig_width], stored[:, sig_width:], rezig(grad_dt.reshape(TOKEN_COUNT, HEADS)), grad_taps[:, :sig_width] * scale, grad_taps[:, sig_width:] * scale, bias_grad[:sig_width] * scale, bias_grad[sig_width:] * scale, lax.optimization_barrier(jnp.sum(decay_log_gradient, axis=0)) * scale, lax.optimization_barrier(jnp.sum(grad_dtb, axis=0)) * scale, lax.optimization_barrier(jnp.sum(grad_skip, axis=0)) * scale)
```

```python
import functools
import math

import jax
import jax.numpy as jnp
from jax import lax
from jax.experimental import pallas as pl
from jax.experimental.pallas import tpu as pltpu
from jax.sharding import PartitionSpec as P

HEADS = 128
HDIM = 64
STATE = 128
GROUPS = 8
MESH = pl.DeviceIdType.MESH
VM = pl.BlockSpec(memory_space=pltpu.VMEM)


def ein(form, left, right):
    return jnp.einsum(form, left, right, preferred_element_type=jnp.float32)


def silu_slope(value):
    sig = jax.nn.sigmoid(value)
    return sig * (1.0 + value * (1.0 - sig))


def block_parts(activated, dt_rows, a_log, dt_bias, groups):
    length = activated.shape[0]
    heads = dt_rows.shape[1]
    inner = heads * HDIM
    shared = groups * STATE
    ratio = heads // groups
    signal = activated[:, :inner].reshape(length, heads, HDIM)
    input_map = activated[:, inner : inner + shared].reshape(length, groups, STATE)
    output_map = activated[:, inner + shared :].reshape(length, groups, STATE)
    input_heads = jnp.repeat(input_map, ratio, axis=1)
    output_heads = jnp.repeat(output_map, ratio, axis=1)
    step = jax.nn.softplus(dt_rows + dt_bias)
    rate = -jnp.exp(a_log)
    row_ids = lax.broadcasted_iota(jnp.int32, (length, length), 0)
    col_ids = lax.broadcasted_iota(jnp.int32, (length, length), 1)
    lower = (row_ids >= col_ids).astype(jnp.float32)
    decay_sum = jnp.dot(lower, step * rate, precision=lax.Precision.HIGHEST)
    to_end = jnp.exp(decay_sum[-1][None, :] - decay_sum)
    scaled = (signal.astype(jnp.float32) * step[:, :, None]).astype(jnp.bfloat16)
    weighted = (scaled.astype(jnp.float32) * to_end[:, :, None]).astype(jnp.bfloat16)
    local = ein("qhp,qhn->hpn", weighted, input_heads)
    return (
        signal,
        input_map,
        output_map,
        input_heads,
        output_heads,
        step,
        rate,
        lower,
        decay_sum,
        scaled,
        to_end,
        weighted,
        local,
    )


def entry_grad(parts, d_rows):
    decay_sum = parts[8]
    output_heads = parts[4]
    scaled_grad = (d_rows.astype(jnp.float32) * jnp.exp(decay_sum)[:, :, None]).astype(jnp.bfloat16)
    return (scaled_grad, ein("thp,thn->hpn", scaled_grad, output_heads))


def block_grads(parts, d_rows, scaled_grad, h_in, carried, skip_gain, dt_rows, dt_bias):
    (
        signal,
        input_map,
        output_map,
        input_heads,
        output_heads,
        step,
        rate,
        lower,
        decay_sum,
        scaled,
        to_end,
        weighted,
        local,
    ) = parts
    length = d_rows.shape[0]
    heads = d_rows.shape[1]
    groups = input_map.shape[1]
    width_state = input_map.shape[2]
    ratio = heads // groups
    grad_f = d_rows.astype(jnp.float32)
    signal_f = signal.astype(jnp.float32)
    grad_skip = jnp.sum(grad_f * signal_f, axis=(0, 2))
    h_low = h_in.astype(jnp.bfloat16)
    carried_low = carried.astype(jnp.bfloat16)
    offset = jnp.exp(decay_sum)[:, :, None] * ein("thn,hpn->thp", output_heads, h_low)
    grad_sum = jnp.sum(grad_f * offset, axis=2)
    out_heads_grad = ein("thp,hpn->thn", scaled_grad, h_low)
    grad_weighted = ein("shn,hpn->shp", input_heads, carried_low)
    in_heads_grad = ein("shp,hpn->shn", weighted, carried_low)
    back = jnp.sum(grad_weighted * scaled.astype(jnp.float32), axis=2) * to_end
    end_term = jnp.exp(decay_sum[-1]) * jnp.sum(h_in * carried, axis=(1, 2))
    last_row = (lax.broadcasted_iota(jnp.int32, (length, 1), 0) == length - 1).astype(jnp.float32)
    grad_sum = grad_sum - back + last_row * (jnp.sum(back, axis=0) + end_term)[None, :]
    spread = decay_sum.T[:, :, None] - decay_sum.T[:, None, :]
    decay = jnp.where(lower[None] > 0, jnp.exp(jnp.minimum(spread, 0.0)), 0.0)
    score = ein("tgn,sgn->gts", output_map, input_map)
    mix = jnp.repeat(score, ratio, axis=0) * decay
    grad_mix = ein("thp,shp->hts", d_rows, scaled)
    grad_scaled = grad_weighted * to_end[:, :, None] + ein(
        "hts,thp->shp", mix.astype(jnp.bfloat16), d_rows
    )
    product = grad_mix * mix
    grad_sum = grad_sum + (jnp.sum(product, axis=2) - jnp.sum(product, axis=1)).T
    grad_score = jnp.sum((grad_mix * decay).reshape(groups, ratio, length, length), axis=1).astype(
        jnp.bfloat16
    )
    grad_outmap = ein("gts,sgn->tgn", grad_score, input_map) + jnp.sum(
        out_heads_grad.reshape(length, groups, ratio, width_state), axis=2
    )
    grad_in = ein("gts,tgn->sgn", grad_score, output_map) + jnp.sum(
        in_heads_grad.reshape(length, groups, ratio, width_state), axis=2
    )
    grad_log = jnp.dot(lower.T, grad_sum, precision=lax.Precision.HIGHEST)
    descent_increment = grad_log * rate + jnp.sum(grad_scaled * signal_f, axis=2)
    grad_signal = skip_gain[None, :, None] * grad_f + grad_scaled * step[:, :, None]
    grad_dt = descent_increment * jax.nn.sigmoid(dt_rows + dt_bias)
    decay_log_gradient = jnp.sum(grad_log * step, axis=0) * rate
    grad_act = jnp.concatenate(
        [
            grad_signal.reshape(length, heads * HDIM),
            grad_in.reshape(length, groups * width_state),
            grad_outmap.reshape(length, groups * width_state),
        ],
        axis=1,
    )
    return (grad_act, grad_dt, decay_log_gradient, jnp.sum(grad_dt, axis=0), grad_skip)


def signal(sem, **where):
    pl.semaphore_signal(sem, inc=1, device_id=where, device_id_type=MESH)


def remote(src, dst, send_sem, recv_sem, **where):
    return pltpu.make_async_remote_copy(
        src_ref=src,
        dst_ref=dst,
        send_sem=send_sem,
        recv_sem=recv_sem,
        device_id=where,
        device_id_type=MESH,
    )


def entry_kernel(
    n_ctx, half, tail_ref, taps_ref, halo_ref, got_ref, halo_send, halo_recv, tap_send, tap_recv
):
    c = lax.axis_index("ctx")
    f = lax.axis_index("fsdp")
    up, down = lax.rem(c + 1, n_ctx), lax.rem(c + n_ctx - 1, n_ctx)
    slot = f // half
    first = 2 * (f - slot * half)
    group = f // 2
    barrier = pltpu.get_barrier_semaphore()
    signal(barrier, ctx=up)
    signal(barrier, ctx=down)
    for k in range(2):
        source = group + k * half

        @pl.when(source != f)
        def _():
            signal(barrier, fsdp=source)

    selves = jnp.where(first == f, 1, 0) + jnp.where(first + 1 == f, 1, 0)
    pl.semaphore_wait(barrier, 4 - selves)
    to_up = remote(tail_ref.at[0], halo_ref.at[0], halo_send.at[0], halo_recv.at[0], ctx=up)
    to_down = remote(tail_ref.at[1], halo_ref.at[1], halo_send.at[1], halo_recv.at[1], ctx=down)
    to_up.start()
    to_down.start()
    for k in range(2):

        @pl.when(first + k != f)
        def _():
            remote(
                taps_ref, got_ref.at[slot], tap_send.at[k], tap_recv.at[slot], fsdp=first + k
            ).start()

    for k in range(2):

        @pl.when(group + k * half == f)
        def _():
            got_ref[k] = taps_ref[...]

    for k in range(2):

        @pl.when(group + k * half != f)
        def _():
            remote(
                taps_ref, got_ref.at[k], tap_send.at[k], tap_recv.at[k], fsdp=group + k * half
            ).wait_recv()

        @pl.when(first + k != f)
        def _():
            remote(
                taps_ref, got_ref.at[slot], tap_send.at[k], tap_recv.at[slot], fsdp=first + k
            ).wait_send()

    to_up.wait()
    to_down.wait()


def entry(tails, taps):
    n_ctx = lax.axis_size("ctx")
    half = lax.axis_size("fsdp") // 2
    return pl.pallas_call(
        functools.partial(entry_kernel, n_ctx, half),
        out_shape=(
            jax.ShapeDtypeStruct(tails.shape, tails.dtype),
            jax.ShapeDtypeStruct((2,) + taps.shape, taps.dtype),
        ),
        in_specs=[VM] * 2,
        out_specs=(VM, VM),
        scratch_shapes=[pltpu.SemaphoreType.DMA((2,))] * 4,
        compiler_params=pltpu.CompilerParams(collective_id=0, has_side_effects=True),
        name="entry",
    )(tails, taps)


def exchange_kernel(
    n, rows, x_ref, g_ref, e_ref, y_ref, xr, gr, er, yo,
    xs_sem, xr_sem, gs_sem, gr_sem, es_sem, er_sem, ys_sem, yr_sem
):
    me = lax.axis_index("ctx")
    barrier = pltpu.get_barrier_semaphore()

    def other(i):
        return lax.rem(me + i, n)

    def mine(d):
        return pl.ds(pl.multiple_of(d * rows, rows), rows)

    def greet(i, _):
        signal(barrier, ctx=other(i))
        return 0

    lax.fori_loop(1, n, greet, 0)
    pl.semaphore_wait(barrier, n - 1)

    def x_copy(d):
        return remote(x_ref.at[:, mine(d)], xr.at[me], xs_sem.at[d], xr_sem.at[me], ctx=d)

    def g_copy(d):
        return remote(g_ref.at[:, mine(d)], gr.at[me], gs_sem.at[d], gr_sem.at[me], ctx=d)

    def e_copy(d):
        return remote(e_ref.at[d], er.at[me], es_sem.at[d], er_sem.at[me], ctx=d)

    def y_copy(d):
        return remote(yo.at[d], y_ref.at[:, mine(me)], ys_sem.at[d], yr_sem.at[me], ctx=d)

    def send(i, _):
        d = other(i)
        e_copy(d).start()
        g_copy(d).start()
        x_copy(d).start()
        return 0

    lax.fori_loop(1, n, send, 0)
    xr[me] = x_ref[:, mine(me)]
    gr[me] = g_ref[:, mine(me)]
    er[me] = e_ref[me]

    def arrived(i, _):
        s = other(i)
        remote(e_ref.at[s], er.at[s], es_sem.at[s], er_sem.at[s], ctx=s).wait_recv()
        remote(x_ref.at[:, mine(s)], xr.at[s], xs_sem.at[s], xr_sem.at[s], ctx=s).wait_recv()
        remote(g_ref.at[:, mine(s)], gr.at[s], gs_sem.at[s], gr_sem.at[s], ctx=s).wait_recv()
        return 0

    lax.fori_loop(1, n, arrived, 0)
    zero = jnp.zeros((rows, STATE), jnp.float32)

    def first(i, state):
        h, g = state
        yo[i, 0] = h.astype(yo.dtype)
        yo[i, 3] = g.astype(yo.dtype)
        h = er[i, 0:1, :] * h + xr[i, 0].astype(jnp.float32)
        g = er[i, 1:2, :] * g + gr[i, 1]
        return h, g

    def second(i, state):
        h, g = state
        j = n - 1 - i
        yo[j, 1] = h.astype(yo.dtype)
        yo[j, 2] = g.astype(yo.dtype)
        h = er[j, 1:2, :] * h + xr[j, 1].astype(jnp.float32)
        g = er[j, 0:1, :] * g + gr[j, 0]
        return h, g

    lax.fori_loop(0, n, second, lax.fori_loop(0, n, first, (zero, zero)))

    def back(i, _):
        y_copy(other(i)).start()
        return 0

    lax.fori_loop(1, n, back, 0)
    y_ref[:, mine(me)] = yo[me]

    def finish(i, _):
        d = other(i)
        e_copy(d).wait_send()
        g_copy(d).wait_send()
        x_copy(d).wait_send()
        y_copy(d).wait_send()
        remote(yo.at[d], y_ref.at[:, mine(d)], ys_sem.at[d], yr_sem.at[d], ctx=d).wait_recv()
        return 0

    lax.fori_loop(1, n, finish, 0)


def exchange(x, g, e):
    n = lax.axis_size("ctx")
    _, total, width = x.shape
    rows = total // n
    return pl.pallas_call(
        functools.partial(exchange_kernel, n, rows),
        out_shape=jax.ShapeDtypeStruct((4, total, width), x.dtype),
        in_specs=[VM] * 3,
        out_specs=VM,
        scratch_shapes=[
            pltpu.VMEM((n, 2, rows, width), x.dtype),
            pltpu.VMEM((n, 2, rows, width), jnp.float32),
            pltpu.VMEM((n, 2, width), jnp.float32),
            pltpu.VMEM((n, 4, rows, width), x.dtype),
        ]
        + [pltpu.SemaphoreType.DMA((n,))] * 8,
        compiler_params=pltpu.CompilerParams(
            collective_id=1, has_side_effects=True, vmem_limit_bytes=32 * 1024 * 1024
        ),
        name="exchange",
    )(x, g, e)


def owners_kernel(half, g_ref, got_ref, send_sem, recv_sem):
    f = lax.axis_index("fsdp")
    slot = f // half
    first = 2 * (f - slot * half)
    group = f // 2
    side = f - 2 * group
    barrier = pltpu.get_barrier_semaphore()
    for k in range(2):

        @pl.when(first + k != f)
        def _():
            signal(barrier, fsdp=first + k)

    selves = jnp.where(group == f, 1, 0) + jnp.where(group + half == f, 1, 0)
    pl.semaphore_wait(barrier, 2 - selves)
    for k in range(2):

        @pl.when(group + k * half != f)
        def _():
            remote(
                g_ref.at[k], got_ref.at[side], send_sem.at[k], recv_sem.at[side], fsdp=group + k * half
            ).start()

        @pl.when(group + k * half == f)
        def _():
            got_ref[side] = g_ref[k]

    for k in range(2):

        @pl.when(first + k != f)
        def _():
            remote(
                g_ref.at[k], got_ref.at[k], send_sem.at[k], recv_sem.at[k], fsdp=first + k
            ).wait_recv()

        @pl.when(group + k * half != f)
        def _():
            remote(
                g_ref.at[k], got_ref.at[side], send_sem.at[k], recv_sem.at[side], fsdp=group + k * half
            ).wait_send()


def to_owners(g):
    half = lax.axis_size("fsdp") // 2
    return pl.pallas_call(
        functools.partial(owners_kernel, half),
        out_shape=jax.ShapeDtypeStruct(g.shape, g.dtype),
        in_specs=[VM],
        out_specs=VM,
        scratch_shapes=[pltpu.SemaphoreType.DMA((2,))] * 2,
        compiler_params=pltpu.CompilerParams(collective_id=2, has_side_effects=True),
        name="owners",
    )(g)


def finish_kernel(
    n, rim_ref, part_ref, halo_ref, total_ref, parts, mine_sum,
    halo_send, halo_recv, ps_sem, pr_sem, ts_sem, tr_sem
):
    me = lax.axis_index("ctx")
    barrier = pltpu.get_barrier_semaphore()

    def other(i):
        return lax.rem(me + i, n)

    def greet(i, _):
        signal(barrier, ctx=other(i))
        return 0

    lax.fori_loop(1, n, greet, 0)
    pl.semaphore_wait(barrier, n - 1)
    up, down = other(1), other(n - 1)
    to_down = remote(rim_ref.at[0], halo_ref.at[0], halo_send.at[0], halo_recv.at[0], ctx=down)
    to_up = remote(rim_ref.at[1], halo_ref.at[1], halo_send.at[1], halo_recv.at[1], ctx=up)
    to_down.start()
    to_up.start()

    def p_copy(d):
        return remote(part_ref.at[d], parts.at[me], ps_sem.at[d], pr_sem.at[me], ctx=d)

    def t_copy(d):
        return remote(mine_sum, total_ref.at[me], ts_sem.at[d], tr_sem.at[me], ctx=d)

    def send(i, _):
        p_copy(other(i)).start()
        return 0

    lax.fori_loop(1, n, send, 0)
    parts[me] = part_ref[me]

    def arrived(i, _):
        s = other(i)
        remote(part_ref.at[s], parts.at[s], ps_sem.at[s], pr_sem.at[s], ctx=s).wait_recv()
        return 0

    lax.fori_loop(1, n, arrived, 0)
    mine_sum[...] = jnp.sum(parts[...], axis=0)

    def spread(i, _):
        t_copy(other(i)).start()
        return 0

    lax.fori_loop(1, n, spread, 0)
    total_ref[me] = mine_sum[...]

    def done(i, _):
        d = other(i)
        p_copy(d).wait_send()
        t_copy(d).wait_send()
        remote(mine_sum, total_ref.at[d], ts_sem.at[d], tr_sem.at[d], ctx=d).wait_recv()
        return 0

    lax.fori_loop(1, n, done, 0)
    to_down.wait()
    to_up.wait()


def finish(rims, part):
    n = lax.axis_size("ctx")
    return pl.pallas_call(
        functools.partial(finish_kernel, n),
        out_shape=(
            jax.ShapeDtypeStruct(rims.shape, rims.dtype),
            jax.ShapeDtypeStruct(part.shape, part.dtype),
        ),
        in_specs=[VM] * 2,
        out_specs=(VM, VM),
        scratch_shapes=[
            pltpu.VMEM(part.shape, part.dtype),
            pltpu.VMEM(part.shape[1:], part.dtype),
        ]
        + [pltpu.SemaphoreType.DMA((2,))] * 2
        + [pltpu.SemaphoreType.DMA((n,))] * 4,
        compiler_params=pltpu.CompilerParams(collective_id=3, has_side_effects=True),
        name="finish",
    )(rims, part)


def conv(rows, before, taps, bias):
    rim = before.shape[1]
    length = rows.shape[1]
    padded = jnp.concatenate([before, rows], axis=1)
    preact = bias[None, None, :] + jnp.zeros(rows.shape, jnp.float32)
    for tap in range(rim + 1):
        preact = preact + taps[tap][None, None, :] * padded[:, tap : tap + length]
    return padded, preact


def shards(
    sig_raw,
    map_raw,
    step_size_logits,
    d_out,
    sig_taps,
    map_taps,
    sig_bias,
    map_bias,
    a_log,
    dt_bias,
    skip_gain,
):
    kernel = sig_taps.shape[0]
    rim = kernel - 1
    length = sig_raw.shape[0] // 2
    sig_width = sig_raw.shape[1]
    map_width = map_raw.shape[1]
    heads_here = step_size_logits.shape[1]
    ratio = HEADS // GROUPS
    fsdp = lax.axis_index("fsdp")
    owned = map_width // lax.axis_size("fsdp")
    group_start = fsdp * heads_here // ratio * STATE
    map_start = fsdp * owned
    ctx = lax.axis_index("ctx")
    n_ctx = lax.axis_size("ctx")
    at_end = ctx == n_ctx - 1

    raw = jnp.concatenate(
        [
            sig_raw,
            lax.dynamic_slice_in_dim(map_raw, group_start, STATE, 1),
            lax.dynamic_slice_in_dim(map_raw, map_width // 2 + group_start, STATE, 1),
            lax.dynamic_slice_in_dim(map_raw, map_start, owned, 1),
        ],
        axis=1,
    )
    width = raw.shape[1]
    raw = raw.reshape(2, length, width).astype(jnp.float32)
    own_taps8 = jnp.concatenate(
        [map_taps, map_bias[None, :], jnp.zeros((8 - kernel - 1, owned), jnp.float32)], axis=0
    )
    halo, group_taps = entry(raw[:, length - 8 :], own_taps8)
    halo = halo[:, 8 - rim :]
    before = jnp.stack(
        [
            jnp.where(ctx == 0, 0.0, halo[0]),
            jnp.where(at_end, raw[0, length - rim :], halo[1]),
        ]
    )
    taps = jnp.concatenate(
        [sig_taps, group_taps[0, :kernel], group_taps[1, :kernel], map_taps], axis=1
    )
    bias = jnp.concatenate([sig_bias, group_taps[0, kernel], group_taps[1, kernel], map_bias])
    padded, preact = conv(raw, before, taps, bias)
    act_width = sig_width + 2 * STATE
    local_act = jax.nn.silu(preact[:, :, :act_width]).astype(jnp.bfloat16)
    dt_rows = step_size_logits.reshape(2, length, heads_here)
    grad_rows = d_out.reshape(2, length, heads_here, HDIM)

    def parts_of(act_block, dt_block):
        return block_parts(act_block, dt_block, a_log, dt_bias, 1)

    parts = jax.vmap(parts_of)(local_act, dt_rows)
    scaled_grad, state_grad = jax.vmap(entry_grad)(parts, grad_rows)
    ends = jnp.exp(parts[8][:, -1])
    local = parts[12].astype(jnp.bfloat16).reshape(2, heads_here * HDIM, STATE)
    state_grad = state_grad.reshape(2, heads_here * HDIM, STATE)
    decays = jnp.repeat(ends.T, n_ctx // heads_here, axis=0)[:, :, None]
    decays = jnp.broadcast_to(decays, (n_ctx, 2, STATE))
    linked = exchange(local, state_grad, decays).reshape(2, 2, heads_here, HDIM, STATE)
    h_ins = linked[0].astype(jnp.float32)
    carried = linked[1].astype(jnp.float32)
    grad_act, grad_dt, decay_log_gradient, grad_dtb, grad_skip = jax.vmap(
        block_grads, in_axes=(0, 0, 0, 0, 0, None, 0, None)
    )(parts, grad_rows, scaled_grad, h_ins, carried, skip_gain, dt_rows, dt_bias)
    map_grads = jnp.stack(
        [grad_act[:, :, sig_width : sig_width + STATE], grad_act[:, :, sig_width + STATE :]]
    )
    got = to_owners(map_grads.reshape(2, 2 * length, STATE))
    map_owned = (got[0] + got[1]).reshape(2, length, owned)
    own = jnp.concatenate([preact[:, :, :sig_width], preact[:, :, act_width:]], axis=2)
    own_padded = jnp.concatenate([padded[:, :, :sig_width], padded[:, :, act_width:]], axis=2)
    own_taps = jnp.concatenate([sig_taps, map_taps], axis=1)
    grad_pre = jnp.concatenate([grad_act[:, :, :sig_width], map_owned], axis=2) * silu_slope(own)
    own_width = sig_width + owned
    tap_grads = [
        jnp.sum(grad_pre * own_padded[:, tap : tap + length], axis=(0, 1)) for tap in range(kernel)
    ]
    tap_grads.append(jnp.sum(grad_pre, axis=(0, 1)))
    small = jnp.concatenate(
        [
            jnp.sum(decay_log_gradient, axis=0),
            jnp.sum(grad_dtb, axis=0),
            jnp.sum(grad_skip, axis=0),
        ]
    )
    flat = jnp.concatenate(tap_grads + [small])
    flat = jnp.pad(flat, (0, n_ctx * 128 - flat.shape[0])).reshape(n_ctx, 1, 128)
    rims, total = finish(grad_pre[:, :8], flat)
    after = jnp.stack(
        [
            jnp.where(at_end, grad_pre[1, :rim], rims[0, :rim]),
            jnp.where(ctx == 0, 0.0, rims[1, :rim]),
        ]
    )
    padded_next = jnp.concatenate([grad_pre, after], axis=1)
    grad_raw = jnp.zeros(grad_pre.shape, jnp.float32)
    for tap in range(kernel):
        grad_raw = (
            grad_raw
            + own_taps[tap][None, None, :] * padded_next[:, rim - tap : rim - tap + length]
        )
    scale = 1.0 / math.sqrt(float(n_ctx * 2 * length))
    total = total.reshape(-1) * scale
    body = (kernel + 1) * own_width
    table = total[:body].reshape(kernel + 1, own_width)
    tail = total[body : body + 3 * heads_here].reshape(3, heads_here)
    return (
        grad_raw[:, :, :sig_width].reshape(2 * length, sig_width),
        grad_raw[:, :, sig_width:].reshape(2 * length, owned),
        grad_dt.reshape(2 * length, heads_here),
        table[:kernel, :sig_width],
        table[:kernel, sig_width:],
        table[kernel, :sig_width],
        table[kernel, sig_width:],
        tail[0],
        tail[1],
        tail[2],
    )


def solution(mesh):
    return jax.shard_map(
        shards,
        mesh=mesh,
        in_specs=(
            P("ctx", "fsdp"),
            P("ctx", None),
            P("ctx", "fsdp"),
            P("ctx", "fsdp"),
            P(None, "fsdp"),
            P(None, "fsdp"),
            P("fsdp"),
            P("fsdp"),
            P("fsdp"),
            P("fsdp"),
            P("fsdp"),
        ),
        out_specs=(
            P("ctx", "fsdp"),
            P("ctx", "fsdp"),
            P("ctx", "fsdp"),
            P(None, "fsdp"),
            P(None, "fsdp"),
            P("fsdp"),
            P("fsdp"),
            P("fsdp"),
            P("fsdp"),
            P("fsdp"),
        ),
        check_vma=False,
    )
```

```python
import functools
import math

import jax
import jax.numpy as jnp
from jax import lax
from jax.experimental import pallas as pl
from jax.experimental.pallas import tpu as pltpu
from jax.sharding import PartitionSpec as P

HEADS = 128
HDIM = 64
STATE = 128
GROUPS = 8
HERE = 8
KSIZE = 4
RIM = KSIZE - 1
BLK = 64
ROWS = 2 * BLK
SIG = HERE * HDIM
WIDE = SIG + 3 * STATE
OWN = SIG + STATE
EDGE = 8
TAIL = (KSIZE + 1) * OWN // STATE
MESH = pl.DeviceIdType.MESH
VM = pl.BlockSpec(memory_space=pltpu.VMEM)
HIGH = lax.Precision.HIGHEST
F32 = jnp.float32
BF16 = jnp.bfloat16


def signal(sem, **where):
    pl.semaphore_signal(sem, inc=1, device_id=where, device_id_type=MESH)


def remote(src, dst, send_sem, recv_sem, **where):
    return pltpu.make_async_remote_copy(
        src_ref=src,
        dst_ref=dst,
        send_sem=send_sem,
        recv_sem=recv_sem,
        device_id=where,
        device_id_type=MESH,
    )


def other(me, i, n):
    off = jnp.where(lax.rem(i, 2) == 1, (i + 1) // 2, n - i // 2)
    return lax.rem(me + off, n)


def columns(start):
    return pl.ds(pl.multiple_of(start * STATE, STATE), STATE)


def nn(a, b, precision=None):
    return lax.dot_general(
        a, b, (((1,), (0,)), ((), ())), precision=precision, preferred_element_type=F32
    )


def nt(a, b, precision=None):
    return lax.dot_general(
        a, b, (((1,), (1,)), ((), ())), precision=precision, preferred_element_type=F32
    )


def tn(a, b):
    return lax.dot_general(a, b, (((0,), (0,)), ((), ())), preferred_element_type=F32)


def sigmoid(v):
    return 1.0 / (1.0 + jnp.exp(-v))


def log1p_small(e):
    series = e * (
        1.0 + e * (-1.0 / 2 + e * (1.0 / 3 + e * (-1.0 / 4 + e * (1.0 / 5 + e * (-1.0 / 6)))))
    )
    return jnp.where(e < 0.03, series, jnp.log(1.0 + e))


def entry_kernel(
    n_ctx, half, sig_ref, map_ref, taps_in, bias_in, halo_ref, got_ref,
    tail_ref, taps_ref, halo_send, halo_recv, tap_send, tap_recv
):
    c = lax.axis_index("ctx")
    f = lax.axis_index("fsdp")
    up, down = lax.rem(c + 1, n_ctx), lax.rem(c + n_ctx - 1, n_ctx)
    slot = f // half
    first = 2 * (f - slot * half)
    group = f // 2
    barrier = pltpu.get_barrier_semaphore()
    signal(barrier, ctx=up)
    signal(barrier, ctx=down)
    for k in range(2):
        source = group + k * half

        @pl.when(source != f)
        def _():
            signal(barrier, fsdp=source)

    for b in range(2):
        rows = slice(b * BLK + BLK - EDGE, b * BLK + BLK)
        tail_ref[b, :, :SIG] = sig_ref[rows, :].astype(F32)
        for k, start in enumerate((group, GROUPS + group, f)):
            tail_ref[b, :, SIG + k * STATE : SIG + (k + 1) * STATE] = map_ref[
                rows, columns(start)
            ].astype(F32)
    taps_ref[0:KSIZE] = taps_in[...]
    taps_ref[KSIZE : KSIZE + 1] = bias_in[...]
    taps_ref[KSIZE + 1 :] = jnp.zeros((EDGE - KSIZE - 1, STATE), F32)
    selves = jnp.where(first == f, 1, 0) + jnp.where(first + 1 == f, 1, 0)
    pl.semaphore_wait(barrier, 4 - selves)
    to_up = remote(tail_ref.at[0], halo_ref.at[0], halo_send.at[0], halo_recv.at[0], ctx=up)
    to_down = remote(tail_ref.at[1], halo_ref.at[1], halo_send.at[1], halo_recv.at[1], ctx=down)
    for k in range(2):

        @pl.when(first + k != f)
        def _():
            remote(
                taps_ref, got_ref.at[slot], tap_send.at[k], tap_recv.at[slot], fsdp=first + k
            ).start()

    to_up.start()
    to_down.start()
    for k in range(2):

        @pl.when(group + k * half == f)
        def _():
            got_ref[k] = taps_ref[...]

    for k in range(2):

        @pl.when(group + k * half != f)
        def _():
            remote(
                taps_ref, got_ref.at[k], tap_send.at[k], tap_recv.at[k], fsdp=group + k * half
            ).wait_recv()

        @pl.when(first + k != f)
        def _():
            remote(
                taps_ref, got_ref.at[slot], tap_send.at[k], tap_recv.at[slot], fsdp=first + k
            ).wait_send()

    to_up.wait()
    to_down.wait()


def entry(sig_raw, map_raw, map_taps, map_bias):
    n_ctx = lax.axis_size("ctx")
    half = lax.axis_size("fsdp") // 2
    return pl.pallas_call(
        functools.partial(entry_kernel, n_ctx, half),
        out_shape=(
            jax.ShapeDtypeStruct((2, EDGE, WIDE), F32),
            jax.ShapeDtypeStruct((2, EDGE, STATE), F32),
        ),
        in_specs=[VM] * 4,
        out_specs=(VM, VM),
        scratch_shapes=[
            pltpu.VMEM((2, EDGE, WIDE), F32),
            pltpu.VMEM((EDGE, STATE), F32),
        ]
        + [pltpu.SemaphoreType.DMA((2,))] * 4,
        compiler_params=pltpu.CompilerParams(
            collective_id=0, has_side_effects=True, vmem_limit_bytes=32 * 1024 * 1024
        ),
        name="entry",
    )(sig_raw, map_raw, map_taps, map_bias)


def main_kernel(
    n, half, sig_ref, map_ref, dt_ref, dout_ref, taps_ref, bias_ref, mtaps_ref, mbias_ref,
    alog_ref, dtb_ref, skip_ref, halo_ref, gtaps_ref,
    gp, rims, total, ddt_ref,
    pad, slope, signal_ref, scaled_ref, weighted_ref, sgrad_ref, imap_ref, omap_ref, wide3, intra,
    oh, gw, drow, xs, gs, es, xr, gr, er, yo, lk, mg, mgot, part, parts, mine_sum,
    xs_sem, xr_sem, gs_sem, gr_sem, es_sem, er_sem, ys_sem, yr_sem, ms_sem, mr_sem,
    hs_sem, hr_sem, ps_sem, pr_sem, ts_sem, tr_sem
):
    me = lax.axis_index("ctx")
    f = lax.axis_index("fsdp")
    slot = f // half
    first = 2 * (f - slot * half)
    group = f // 2
    side = f - 2 * group
    share = HERE * HDIM // n
    per_head = n // HERE
    barrier = pltpu.get_barrier_semaphore()

    def greet(i, _):
        signal(barrier, ctx=other(me, i, n))
        return 0

    lax.fori_loop(1, n, greet, 0)
    for k in range(2):

        @pl.when(first + k != f)
        def _():
            signal(barrier, fsdp=first + k)

    lane = lax.broadcasted_iota(jnp.int32, (HERE, ROWS), 1)
    row_id = lax.broadcasted_iota(jnp.int32, (ROWS, ROWS), 0)
    col_id = lax.broadcasted_iota(jnp.int32, (ROWS, ROWS), 1)
    lower = ((row_id >= BLK) == (col_id >= BLK)) & (col_id <= row_id)
    lower_f = jnp.where(lower, 1.0, 0.0).astype(F32)
    eye = jnp.where(row_id == col_id, 1.0, 0.0).astype(F32)
    eye8 = eye[:HERE, :HERE]
    ones8 = jnp.ones((HERE, ROWS), F32)
    head3 = lax.broadcasted_iota(jnp.int32, (3 * HERE, 3 * SIG), 0)
    spread3 = jnp.where(
        lax.broadcasted_iota(jnp.int32, (3 * HERE, 3 * SIG), 1) // HDIM == head3, 1.0, 0.0
    ).astype(F32)
    spread1 = spread3[:HERE, :SIG]

    def in_rows(ref):
        return nt(eye8, jnp.broadcast_to(ref[...], (ROWS, HERE)), HIGH)

    def per_row(y):
        return nt(spread1, y, HIGH)

    logits = nt(eye8, dt_ref[...], HIGH) + in_rows(dtb_ref)
    rate = -jnp.exp(in_rows(alog_ref))
    step = jnp.maximum(logits, 0.0) + log1p_small(jnp.exp(-jnp.abs(logits)))
    ds = nt(step * rate, lower_f, HIGH)
    end_low = jnp.exp(ds[:, BLK - 1 : BLK])
    end_high = jnp.exp(ds[:, ROWS - 1 : ROWS])
    end = jnp.where(lane < BLK, ds[:, BLK - 1 : BLK], ds[:, ROWS - 1 : ROWS])
    to_end = jnp.exp(end - ds)
    col4 = nt(eye, jnp.concatenate([step, to_end, jnp.exp(ds), ds], axis=0), HIGH)
    ds_col = col4[:, 3 * HERE :]
    wide3[...] = nn(col4[:, : 3 * HERE], spread3, HIGH)
    end_low8 = jnp.broadcast_to(end_low, (HERE, STATE))
    end_high8 = jnp.broadcast_to(end_high, (HERE, STATE))
    for h in range(HERE):
        es[h, 0:1, :] = end_low8[h : h + 1]
        es[h, 1:2, :] = end_high8[h : h + 1]

    keep = jnp.where(me == 0, 0.0, 1.0).astype(F32)
    for b in range(2):
        rows = slice(b * BLK, (b + 1) * BLK)
        pad[b, EDGE:, :SIG] = sig_ref[rows, :].astype(F32)
        for k, start in enumerate((group, GROUPS + group, f)):
            pad[b, EDGE:, SIG + k * STATE : SIG + (k + 1) * STATE] = map_ref[
                rows, columns(start)
            ].astype(F32)
    pad[0, :EDGE] = halo_ref[0] * keep
    pad[1, :EDGE] = jnp.where(me == n - 1, pad[0, BLK:], halo_ref[1])

    def preact(b, cols, taps, bias):
        acc = bias
        for k in range(KSIZE):
            start = EDGE - RIM + k
            acc = acc + taps[k : k + 1] * pad[b, start : start + BLK, cols]
        return acc

    for b in range(2):
        rows = slice(b * BLK, (b + 1) * BLK)
        for q in range(SIG // STATE):
            cols = slice(q * STATE, (q + 1) * STATE)
            v = preact(b, cols, taps_ref[:, cols], bias_ref[:, cols])
            s = sigmoid(v)
            slope[rows, cols] = s * (1.0 + v * (1.0 - s))
            signal_b = (v * s).astype(BF16)
            signal_ref[rows, cols] = signal_b
            scaled_b = (signal_b.astype(F32) * wide3[rows, cols]).astype(BF16)
            scaled_ref[rows, cols] = scaled_b
            cols2 = slice(SIG + q * STATE, SIG + (q + 1) * STATE)
            cols3 = slice(2 * SIG + q * STATE, 2 * SIG + (q + 1) * STATE)
            weighted_ref[rows, cols] = (scaled_b.astype(F32) * wide3[rows, cols2]).astype(BF16)
            sgrad_ref[rows, cols] = (
                dout_ref[rows, cols].astype(F32) * wide3[rows, cols3]
            ).astype(BF16)
        for k, out in enumerate((imap_ref, omap_ref)):
            cols = slice(SIG + k * STATE, SIG + (k + 1) * STATE)
            v = preact(b, cols, gtaps_ref[k, :KSIZE], gtaps_ref[k, KSIZE : KSIZE + 1])
            out[rows, :] = (v * sigmoid(v)).astype(BF16)
        v = preact(b, slice(SIG + 2 * STATE, WIDE), mtaps_ref[...], mbias_ref[...])
        s = sigmoid(v)
        slope[rows, SIG:] = s * (1.0 + v * (1.0 - s))
        gs[b] = tn(sgrad_ref[rows, :], omap_ref[rows, :])
        xs[b] = tn(weighted_ref[rows, :], imap_ref[rows, :]).astype(BF16)

    def mine(d):
        return pl.ds(pl.multiple_of(d * share, share), share)

    def x_copy(d):
        return remote(xs.at[:, mine(d)], xr.at[me], xs_sem.at[d], xr_sem.at[me], ctx=d)

    def g_copy(d):
        return remote(gs.at[:, mine(d)], gr.at[me], gs_sem.at[d], gr_sem.at[me], ctx=d)

    def e_copy(d):
        return remote(es.at[d // per_head], er.at[me], es_sem.at[d], er_sem.at[me], ctx=d)

    def y_copy(d):
        return remote(yo.at[d], lk.at[:, mine(me)], ys_sem.at[d], yr_sem.at[me], ctx=d)

    selves = jnp.where(group == f, 1, 0) + jnp.where(group + half == f, 1, 0)
    pl.semaphore_wait(barrier, n - 1 + 2 - selves)

    def send(i, _):
        d = other(me, i, n)
        g_copy(d).start()
        x_copy(d).start()
        e_copy(d).start()
        return 0

    lax.fori_loop(1, n, send, 0)
    xr[me] = xs[:, mine(me)]
    gr[me] = gs[:, mine(me)]
    er[me] = es[me // per_head]

    score = nt(omap_ref[...], imap_ref[...])
    lane_row = lax.broadcasted_iota(jnp.int32, (ROWS, STATE), 1)
    grad_score = jnp.zeros((ROWS, ROWS), F32)
    for q in range(HERE // 2):
        cols = slice(q * STATE, (q + 1) * STATE)
        d_pair = dout_ref[:, cols].astype(F32)
        d_two = jnp.concatenate(
            [jnp.where(lane_row < HDIM, d_pair, 0.0), jnp.where(lane_row < HDIM, 0.0, d_pair)],
            axis=0,
        ).astype(BF16)
        grad_mix2 = nt(d_two, scaled_ref[:, cols])
        mixes = []
        for k in range(2):
            h = 2 * q + k
            grad_mix = grad_mix2[k * ROWS : (k + 1) * ROWS]
            gap = jnp.minimum(ds_col[:, h : h + 1] - ds[h : h + 1, :], 0.0)
            decay = jnp.where(lower, jnp.exp(gap), 0.0)
            mix = score * decay
            mixes.append(mix.astype(BF16))
            grad_score = grad_score + grad_mix * decay
            product = grad_mix * mix
            drow[h : h + 1, :] = nt(ones8, product, HIGH)[0:1] - jnp.sum(
                product, axis=0, keepdims=True
            )
        intra[:, cols] = tn(jnp.concatenate(mixes, axis=0), d_two)
    grad_score = grad_score.astype(BF16)
    mg[0] = tn(grad_score, omap_ref[...])
    mg[1] = nn(grad_score, imap_ref[...])

    def arrived(i, _):
        s = other(me, i, n)
        remote(es.at[s // per_head], er.at[s], es_sem.at[s], er_sem.at[s], ctx=s).wait_recv()
        remote(xs.at[:, mine(s)], xr.at[s], xs_sem.at[s], xr_sem.at[s], ctx=s).wait_recv()
        remote(gs.at[:, mine(s)], gr.at[s], gs_sem.at[s], gr_sem.at[s], ctx=s).wait_recv()
        return 0

    lax.fori_loop(1, n, arrived, 0)
    zero = jnp.zeros((share, STATE), F32)

    def out_and_up(i, state):
        h, g = state
        yo[i, 0] = h.astype(BF16)
        yo[i, 3] = g.astype(BF16)
        h = er[i, 0:1, :] * h + xr[i, 0].astype(F32)
        g = er[i, 1:2, :] * g + gr[i, 1]
        return h, g

    def out_and_down(i, state):
        h, g = state
        j = n - 1 - i
        yo[j, 1] = h.astype(BF16)
        yo[j, 2] = g.astype(BF16)
        h = er[j, 1:2, :] * h + xr[j, 1].astype(F32)
        g = er[j, 0:1, :] * g + gr[j, 0]
        return h, g

    lax.fori_loop(0, n, out_and_down, lax.fori_loop(0, n, out_and_up, (zero, zero)))

    def back(i, _):
        y_copy(other(me, i, n)).start()
        return 0

    lax.fori_loop(1, n, back, 0)
    lk[:, mine(me)] = yo[me]

    def linked(i, _):
        d = other(me, i, n)
        g_copy(d).wait_send()
        x_copy(d).wait_send()
        e_copy(d).wait_send()
        remote(yo.at[d], lk.at[:, mine(d)], ys_sem.at[d], yr_sem.at[d], ctx=d).wait_recv()
        return 0

    lax.fori_loop(1, n, linked, 0)

    for b in range(2):
        rows = slice(b * BLK, (b + 1) * BLK)
        mg[0, rows, :] = mg[0, rows, :] + nn(weighted_ref[rows, :], lk[2 + b])
        mg[1, rows, :] = mg[1, rows, :] + nn(sgrad_ref[rows, :], lk[b])

    def m_copy(k):
        return remote(
            mg.at[k], mgot.at[side], ms_sem.at[k], mr_sem.at[side], fsdp=group + k * half
        )

    for k in range(2):

        @pl.when(group + k * half != f)
        def _():
            m_copy(k).start()

        @pl.when(group + k * half == f)
        def _():
            mgot[side] = mg[k]

    end_terms = []
    for b in range(2):
        rows = slice(b * BLK, (b + 1) * BLK)
        oh[rows, :] = nt(omap_ref[rows, :], lk[b])
        gw[rows, :] = nt(imap_ref[rows, :], lk[2 + b])
        both = lk[b].astype(F32) * lk[2 + b].astype(F32)
        both = jnp.sum(both.reshape(HERE, HDIM, STATE), axis=1)
        end_terms.append(jnp.sum(both, axis=1, keepdims=True))
    step_w = wide3[:, :SIG]
    end_w = wide3[:, SIG : 2 * SIG]
    exp_w = wide3[:, 2 * SIG :]
    d_f = dout_ref[...].astype(F32)
    signal_f = signal_ref[...].astype(F32)
    gw_v = gw[...]
    back_row = per_row(gw_v * scaled_ref[...].astype(F32)) * to_end
    grad_sum = per_row(d_f * exp_w * oh[...]) - back_row + drow[...]
    back_low = jnp.sum(jnp.where(lane < BLK, back_row, 0.0), axis=1, keepdims=True)
    back_high = jnp.sum(jnp.where(lane < BLK, 0.0, back_row), axis=1, keepdims=True)
    last_low = back_low + end_low * end_terms[0]
    last_high = back_high + end_high * end_terms[1]
    grad_sum = grad_sum + jnp.where(
        lane == BLK - 1, last_low, jnp.where(lane == ROWS - 1, last_high, 0.0)
    )
    grad_log = nn(grad_sum, lower_f, HIGH)
    grad_scaled = gw_v * end_w + intra[...]
    grad_step = grad_log * rate + per_row(grad_scaled * signal_f)
    grad_dt = grad_step * sigmoid(logits)
    ddt_ref[...] = nt(eye, grad_dt, HIGH)
    skip_w = nn(jnp.broadcast_to(skip_ref[...], (HERE, HERE)), spread1, HIGH)[0:1]
    gp[:, :SIG] = (skip_w * d_f + grad_scaled * step_w) * slope[:, :SIG]
    part[...] = jnp.zeros(part.shape, F32)
    part[TAIL, 0:1, :HERE] = nt(ones8, grad_log * step, HIGH)[0:1] * (-jnp.exp(alog_ref[...]))
    part[TAIL + 1, 0:1, :HERE] = nt(ones8, grad_dt, HIGH)[0:1]
    part[TAIL + 2, 0:1, :HERE] = nt(ones8, per_row(d_f * signal_f), HIGH)[0:1]

    def sums(cols, source, at):
        for k in range(KSIZE + 1):
            acc = jnp.zeros((1, STATE), F32)
            for b in range(2):
                g = gp[b * BLK : (b + 1) * BLK, cols]
                if k < KSIZE:
                    start = EDGE - RIM + k
                    g = g * pad[b, start : start + BLK, source]
                acc = acc + jnp.sum(g, axis=0, keepdims=True)
            part[k * (OWN // STATE) + at, 0:1, :] = acc

    for q in range(SIG // STATE):
        cols = slice(q * STATE, (q + 1) * STATE)
        sums(cols, cols, q)

    for k in range(2):

        @pl.when(first + k != f)
        def _():
            remote(
                mg.at[k], mgot.at[k], ms_sem.at[k], mr_sem.at[k], fsdp=first + k
            ).wait_recv()

    gp[:, SIG:] = (mgot[0] + mgot[1]) * slope[:, SIG:]
    up, down = lax.rem(me + 1, n), lax.rem(me + n - 1, n)
    to_down = remote(gp.at[0:EDGE], rims.at[0], hs_sem.at[0], hr_sem.at[0], ctx=down)
    to_up = remote(gp.at[BLK : BLK + EDGE], rims.at[1], hs_sem.at[1], hr_sem.at[1], ctx=up)
    to_down.start()
    to_up.start()
    sums(slice(SIG, OWN), slice(SIG + 2 * STATE, WIDE), SIG // STATE)

    def p_copy(d):
        return remote(part.at[d], parts.at[me], ps_sem.at[d], pr_sem.at[me], ctx=d)

    def t_copy(d):
        return remote(mine_sum, total.at[me], ts_sem.at[d], tr_sem.at[me], ctx=d)

    def send_part(i, _):
        p_copy(other(me, i, n)).start()
        return 0

    lax.fori_loop(1, n, send_part, 0)
    parts[me] = part[me]

    def part_in(i, _):
        s = other(me, i, n)
        remote(part.at[s], parts.at[s], ps_sem.at[s], pr_sem.at[s], ctx=s).wait_recv()
        return 0

    lax.fori_loop(1, n, part_in, 0)
    mine_sum[...] = jnp.sum(parts[...], axis=0)

    def send_total(i, _):
        t_copy(other(me, i, n)).start()
        return 0

    lax.fori_loop(1, n, send_total, 0)
    total[me] = mine_sum[...]

    def done(i, _):
        d = other(me, i, n)
        y_copy(d).wait_send()
        p_copy(d).wait_send()
        t_copy(d).wait_send()
        remote(mine_sum, total.at[d], ts_sem.at[d], tr_sem.at[d], ctx=d).wait_recv()
        return 0

    lax.fori_loop(1, n, done, 0)
    for k in range(2):

        @pl.when(group + k * half != f)
        def _():
            m_copy(k).wait_send()

    to_down.wait()
    to_up.wait()


def main(*operands):
    n = lax.axis_size("ctx")
    half = lax.axis_size("fsdp") // 2
    share = HERE * HDIM // n
    dma = pltpu.SemaphoreType.DMA
    vm = pltpu.VMEM
    return pl.pallas_call(
        functools.partial(main_kernel, n, half),
        out_shape=(
            jax.ShapeDtypeStruct((ROWS, OWN), F32),
            jax.ShapeDtypeStruct((2, EDGE, OWN), F32),
            jax.ShapeDtypeStruct((n, 1, STATE), F32),
            jax.ShapeDtypeStruct((ROWS, HERE), F32),
        ),
        in_specs=[VM] * len(operands),
        out_specs=(VM,) * 4,
        scratch_shapes=[
            vm((2, EDGE + BLK, WIDE), F32),
            vm((ROWS, OWN), F32),
            vm((ROWS, SIG), BF16),
            vm((ROWS, SIG), BF16),
            vm((ROWS, SIG), BF16),
            vm((ROWS, SIG), BF16),
            vm((ROWS, STATE), BF16),
            vm((ROWS, STATE), BF16),
            vm((ROWS, 3 * SIG), F32),
            vm((ROWS, SIG), F32),
            vm((ROWS, SIG), F32),
            vm((ROWS, SIG), F32),
            vm((HERE, ROWS), F32),
            vm((2, SIG, STATE), BF16),
            vm((2, SIG, STATE), F32),
            vm((HERE, 2, STATE), F32),
            vm((n, 2, share, STATE), BF16),
            vm((n, 2, share, STATE), F32),
            vm((n, 2, STATE), F32),
            vm((n, 4, share, STATE), BF16),
            vm((4, SIG, STATE), BF16),
            vm((2, ROWS, STATE), F32),
            vm((2, ROWS, STATE), F32),
            vm((n, 1, STATE), F32),
            vm((n, 1, STATE), F32),
            vm((1, STATE), F32),
        ]
        + [dma((n,))] * 8
        + [dma((2,))] * 4
        + [dma((n,))] * 4,
        compiler_params=pltpu.CompilerParams(
            collective_id=1, has_side_effects=True, vmem_limit_bytes=48 * 1024 * 1024
        ),
        name="main",
    )(*operands)


def last_kernel(
    n, scale, gp, rims, total, ddt, taps_ref, mtaps_ref,
    dsig, dmap, ddt_out, dtaps, dmtaps, dbias, dmbias, dalog, ddtb, dskip, pad
):
    me = lax.axis_index("ctx")
    keep = jnp.where(me == 0, 0.0, 1.0).astype(F32)
    for b in range(2):
        pad[b, :BLK] = gp[b * BLK : (b + 1) * BLK]
    pad[0, BLK:] = jnp.where(me == n - 1, gp[BLK : BLK + EDGE], rims[0])
    pad[1, BLK:] = rims[1] * keep
    for b in range(2):
        rows = slice(b * BLK, (b + 1) * BLK)
        for out, taps, cols in (
            (dsig, taps_ref, slice(0, SIG)),
            (dmap, mtaps_ref, slice(SIG, OWN)),
        ):
            acc = taps[RIM : RIM + 1] * pad[b, 0:BLK, cols]
            for k in range(RIM):
                acc = acc + taps[k : k + 1] * pad[b, RIM - k : RIM - k + BLK, cols]
            out[rows, :] = acc
    ddt_out[...] = ddt[...]
    for k in range(KSIZE + 1):
        for q in range(OWN // STATE):
            row = total[k * (OWN // STATE) + q] * scale
            cols = slice(q * STATE, (q + 1) * STATE)
            if q < SIG // STATE:
                if k < KSIZE:
                    dtaps[k : k + 1, cols] = row
                else:
                    dbias[:, cols] = row
            elif k < KSIZE:
                dmtaps[k : k + 1, :] = row
            else:
                dmbias[...] = row
    for k, out in enumerate((dalog, ddtb, dskip)):
        out[...] = total[TAIL + k][:, :HERE] * scale


def last(gp, rims, total, ddt, sig_taps, map_taps):
    n = lax.axis_size("ctx")
    scale = 1.0 / math.sqrt(float(n * ROWS))
    shapes = (
        (ROWS, SIG), (ROWS, STATE), (ROWS, HERE), (KSIZE, SIG), (KSIZE, STATE),
        (1, SIG), (1, STATE), (1, HERE), (1, HERE), (1, HERE),
    )
    return pl.pallas_call(
        functools.partial(last_kernel, n, scale),
        out_shape=tuple(jax.ShapeDtypeStruct(s, F32) for s in shapes),
        in_specs=[VM] * 6,
        out_specs=(VM,) * len(shapes),
        scratch_shapes=[pltpu.VMEM((2, BLK + EDGE, OWN), F32)],
        name="last",
    )(gp, rims, total, ddt, sig_taps, map_taps)


def shards(
    sig_raw,
    map_raw,
    step_size_logits,
    d_out,
    sig_taps,
    map_taps,
    sig_bias,
    map_bias,
    a_log,
    dt_bias,
    skip_gain,
):
    bias = map_bias[None, :]
    halo, group_taps = entry(sig_raw, map_raw, map_taps, bias)
    found = main(
        sig_raw, map_raw, step_size_logits, d_out, sig_taps, sig_bias[None, :], map_taps, bias,
        a_log[None, :], dt_bias[None, :], skip_gain[None, :], halo, group_taps,
    )
    out = last(*found, sig_taps, map_taps)
    return out[:5] + tuple(a.reshape(-1) for a in out[5:])


def solution(mesh):
    return jax.shard_map(
        shards,
        mesh=mesh,
        in_specs=(
            P("ctx", "fsdp"),
            P("ctx", None),
            P("ctx", "fsdp"),
            P("ctx", "fsdp"),
            P(None, "fsdp"),
            P(None, "fsdp"),
            P("fsdp"),
            P("fsdp"),
            P("fsdp"),
            P("fsdp"),
            P("fsdp"),
        ),
        out_specs=(
            P("ctx", "fsdp"),
            P("ctx", "fsdp"),
            P("ctx", "fsdp"),
            P(None, "fsdp"),
            P(None, "fsdp"),
            P("fsdp"),
            P("fsdp"),
            P("fsdp"),
            P("fsdp"),
            P("fsdp"),
        ),
        check_vma=False,
    )
```

```python
import functools
import math

import jax
import jax.numpy as jnp
from jax import lax
from jax.experimental import pallas as pl
from jax.experimental.pallas import tpu as pltpu
from jax.sharding import PartitionSpec as P

HEADS = 128
HDIM = 64
STATE = 128
GROUPS = 8
HERE = 8
KSIZE = 4
RIM = KSIZE - 1
BLK = 64
ROWS = 2 * BLK
SIG = HERE * HDIM
WIDE = SIG + 3 * STATE
OWN = SIG + STATE
EDGE = 16
RIMS = 8
TAIL = (KSIZE + 1) * OWN // STATE
MESH = pl.DeviceIdType.MESH
VM = pl.BlockSpec(memory_space=pltpu.VMEM)
HIGH = lax.Precision.HIGHEST
F32 = jnp.float32
BF16 = jnp.bfloat16


def signal(sem, **where):
    pl.semaphore_signal(sem, inc=1, device_id=where, device_id_type=MESH)


def remote(src, dst, send_sem, recv_sem, **where):
    return pltpu.make_async_remote_copy(
        src_ref=src,
        dst_ref=dst,
        send_sem=send_sem,
        recv_sem=recv_sem,
        device_id=where,
        device_id_type=MESH,
    )


def other(me, i, n):
    off = jnp.where(lax.rem(i, 2) == 1, (i + 1) // 2, n - i // 2)
    return lax.rem(me + off, n)


def columns(start):
    return pl.ds(pl.multiple_of(start * STATE, STATE), STATE)


def nn(a, b, precision=None):
    return lax.dot_general(
        a, b, (((1,), (0,)), ((), ())), precision=precision, preferred_element_type=F32
    )


def nt(a, b, precision=None):
    return lax.dot_general(
        a, b, (((1,), (1,)), ((), ())), precision=precision, preferred_element_type=F32
    )


def tn(a, b):
    return lax.dot_general(a, b, (((0,), (0,)), ((), ())), preferred_element_type=F32)


def sigmoid(v):
    return 1.0 / (1.0 + jnp.exp(-v))


def log1p_small(e):
    series = e * (
        1.0 + e * (-1.0 / 2 + e * (1.0 / 3 + e * (-1.0 / 4 + e * (1.0 / 5 + e * (-1.0 / 6)))))
    )
    return jnp.where(e < 0.03, series, jnp.log(1.0 + e))


def main_kernel(
    n, half, sig_hbm, map_hbm, dt_hbm, dout_hbm, taps_hbm, bias_hbm, mtaps_hbm, mbias_hbm,
    alog_hbm, dtb_hbm, skip_hbm,
    big, total, ddt_ref,
    sig_in, map_in, dout_ref, dt_in, dt_got, taps_ref, bias_ref, mtaps_ref, mbias_ref,
    alog_ref, dtb_ref, skip_ref, tail_own, tail_got, tap_row, gtaps_ref,
    pad, slope, signal_ref, scaled_ref, weighted_ref, sgrad_ref, imap_ref, omap_ref, wide3, intra,
    oh, gw, drow, xs, gs, es, xr, gr, er, yh, yc, lh, lc, first_local, second_sg, lk,
    mg, mgot, gpad, rims, swap, ddt_mine, ddt_got, part, parts, mine_sum,
    l_sem, n_send, n_recv, b_send, b_recv, tap_send, tap_recv,
    xs_sem, xr_sem, gs_sem, gr_sem, es_sem, er_sem, hs_sem, hr_sem, cs_sem, cr_sem,
    ms_sem, mr_sem, r_sem, w_sem, ps_sem, pr_sem, ts_sem, tr_sem
):
    me = lax.axis_index("ctx")
    f = lax.axis_index("fsdp")
    odd = lax.rem(me, 2)
    mate = me + 1 - 2 * odd
    side_ctx = lax.rem(me + n - 1 + 2 * odd, n)
    slot = f // half
    first = 2 * (f - slot * half)
    group = f // 2
    side = f - 2 * group
    share = SIG // n
    per_head = n // HERE
    kept = pl.multiple_of(odd * BLK, BLK)
    given = pl.multiple_of((1 - odd) * BLK, BLK)
    ending = pl.multiple_of((1 - odd) * BLK + BLK - EDGE, EDGE)
    starts = (group, GROUPS + group, f)
    barrier = pltpu.get_barrier_semaphore()

    def fetch(i, src, dst):
        copy = pltpu.make_async_copy(src, dst, l_sem.at[i])
        copy.start()
        return copy

    def third(k):
        return slice(k * STATE, (k + 1) * STATE)

    local = [
        fetch(0, mtaps_hbm, mtaps_ref),
        fetch(1, mbias_hbm, mbias_ref),
        fetch(2, dt_hbm, dt_in),
        fetch(3, alog_hbm, alog_ref),
        fetch(4, dtb_hbm, dtb_ref),
        fetch(5, skip_hbm, skip_ref),
        fetch(6, taps_hbm, taps_ref),
        fetch(7, bias_hbm, bias_ref),
        fetch(8, sig_hbm.at[pl.ds(kept, BLK)], sig_in.at[0:BLK]),
        fetch(9, dout_hbm.at[pl.ds(kept, BLK)], dout_ref.at[0:BLK]),
        fetch(10, sig_hbm.at[pl.ds(ending, EDGE)], tail_own.at[:, 0:SIG]),
    ]
    for k, start in enumerate(starts):
        local.append(
            fetch(
                11 + k,
                map_hbm.at[pl.ds(kept, BLK), columns(start)],
                map_in.at[0:BLK, third(k)],
            )
        )
        local.append(
            fetch(
                14 + k,
                map_hbm.at[pl.ds(ending, EDGE), columns(start)],
                tail_own.at[:, SIG + k * STATE : SIG + (k + 1) * STATE],
            )
        )

    def greet(i, _):
        signal(barrier, ctx=other(me, i, n))
        return 0

    lax.fori_loop(1, n, greet, 0)
    for k in range(2):

        @pl.when(group + k * half != f)
        def _():
            signal(barrier, fsdp=group + k * half)

        @pl.when(first + k != f)
        def _():
            signal(barrier, fsdp=first + k)

    for copy in local:
        copy.wait()
    tap_row[0:KSIZE] = mtaps_ref[...]
    tap_row[KSIZE : KSIZE + 1] = mbias_ref[...]
    tap_row[KSIZE + 1 :] = jnp.zeros((8 - KSIZE - 1, STATE), F32)
    selves = jnp.where(group == f, 1, 0) + jnp.where(group + half == f, 1, 0)
    pl.semaphore_wait(barrier, n - 1 + 4 - 2 * selves)

    for k in range(2):

        @pl.when(first + k != f)
        def _():
            remote(
                tap_row, gtaps_ref.at[slot], tap_send.at[k], tap_recv.at[slot], fsdp=first + k
            ).start()

        @pl.when(group + k * half == f)
        def _():
            gtaps_ref[k] = tap_row[...]

    def to_mate(i, src, dst):
        copy = remote(src, dst, n_send.at[i], n_recv.at[i], ctx=mate)
        copy.start()
        return copy

    def to_side(i, dst_cols):
        copy = remote(
            tail_own.at[:, dst_cols], tail_got.at[:, dst_cols], b_send.at[i], b_recv.at[i],
            ctx=side_ctx,
        )
        copy.start()
        return copy

    dt_copy = to_mate(0, dt_hbm, dt_got)
    tail_copy = to_side(0, slice(0, WIDE))
    map_copies = [
        to_mate(
            1 + k, map_hbm.at[pl.ds(given, BLK), columns(start)], map_in.at[BLK:ROWS, third(k)]
        )
        for k, start in enumerate(starts)
    ]
    sig_copy = to_mate(4, sig_hbm.at[pl.ds(given, BLK)], sig_in.at[BLK:ROWS])
    dout_copy = to_mate(5, dout_hbm.at[pl.ds(given, BLK)], dout_ref.at[BLK:ROWS])

    lane = lax.broadcasted_iota(jnp.int32, (HERE, ROWS), 1)
    row_id = lax.broadcasted_iota(jnp.int32, (ROWS, ROWS), 0)
    col_id = lax.broadcasted_iota(jnp.int32, (ROWS, ROWS), 1)
    lower = ((row_id >= BLK) == (col_id >= BLK)) & (col_id <= row_id)
    lower_f = jnp.where(lower, 1.0, 0.0).astype(F32)
    eye = jnp.where(row_id == col_id, 1.0, 0.0).astype(F32)
    eye8 = eye[:HERE, :HERE]
    ones8 = jnp.ones((HERE, ROWS), F32)
    head3 = lax.broadcasted_iota(jnp.int32, (3 * HERE, 3 * SIG), 0)
    spread3 = jnp.where(
        lax.broadcasted_iota(jnp.int32, (3 * HERE, 3 * SIG), 1) // HDIM == head3, 1.0, 0.0
    ).astype(F32)
    spread1 = spread3[:HERE, :SIG]

    def in_rows(ref):
        return nt(eye8, jnp.broadcast_to(ref[...], (ROWS, HERE)), HIGH)

    def per_row(y):
        return nt(spread1, y, HIGH)

    def turned(x):
        return pltpu.roll(x, BLK, 1)

    def preact(r, rows, cols, taps, bias):
        acc = bias
        for k in range(KSIZE):
            start = EDGE - RIM + k + r
            acc = acc + taps[k : k + 1] * pad[start : start + rows, cols]
        return acc

    def sig_rows(r, count):
        rows = slice(r, r + count)
        for q in range(SIG // STATE):
            cols = third(q)
            v = preact(r, count, cols, taps_ref[:, cols], bias_ref[:, cols])
            s = sigmoid(v)
            slope[rows, cols] = s * (1.0 + v * (1.0 - s))
            signal_ref[rows, cols] = (v * s).astype(BF16)

    pad[EDGE : EDGE + BLK, :SIG] = sig_in[:BLK, :].astype(F32)
    pad[EDGE : EDGE + BLK, SIG:] = map_in[:BLK, :].astype(F32)
    sig_rows(EDGE, BLK - EDGE)
    dt_copy.wait()
    own, got = dt_in[...], dt_got[...]
    own = jnp.where(odd == 0, own, turned(own))
    got = jnp.where(odd == 0, turned(got), got)
    logits = jnp.where(lane < BLK, own, got) + in_rows(dtb_ref)
    rate = -jnp.exp(in_rows(alog_ref))
    step = jnp.maximum(logits, 0.0) + log1p_small(jnp.exp(-jnp.abs(logits)))
    ds = nt(step * rate, lower_f, HIGH)
    end_low = jnp.exp(ds[:, BLK - 1 : BLK])
    end_high = jnp.exp(ds[:, ROWS - 1 : ROWS])
    end = jnp.where(lane < BLK, ds[:, BLK - 1 : BLK], ds[:, ROWS - 1 : ROWS])
    to_end = jnp.exp(end - ds)
    col4 = nt(eye, jnp.concatenate([step, to_end, jnp.exp(ds), ds], axis=0), HIGH)
    ds_col = col4[:, 3 * HERE :]
    wide3[...] = nn(col4[:, : 3 * HERE], spread3, HIGH)
    end_low8 = jnp.broadcast_to(end_low, (HERE, STATE))
    end_high8 = jnp.broadcast_to(end_high, (HERE, STATE))
    both_ends = end_low8 * end_high8
    for h in range(HERE):
        es[h] = both_ends[h : h + 1]

    for k in range(2):

        @pl.when(group + k * half != f)
        def _():
            remote(
                tap_row, gtaps_ref.at[k], tap_send.at[k], tap_recv.at[k], fsdp=group + k * half
            ).wait_recv()

        @pl.when(first + k != f)
        def _():
            remote(
                tap_row, gtaps_ref.at[slot], tap_send.at[k], tap_recv.at[slot], fsdp=first + k
            ).wait_send()

    tail_copy.wait()
    for copy in map_copies:
        copy.wait()
    keep = jnp.where(me == 0, 0.0, 1.0).astype(F32)
    before = jnp.where(me == n - 1, tail_own[...].astype(F32), tail_got[...].astype(F32))
    pad[:EDGE] = before * keep
    pad[EDGE + BLK :, SIG:] = map_in[BLK:, :].astype(F32)
    for k, out in enumerate((imap_ref, omap_ref)):
        cols = slice(SIG + k * STATE, SIG + (k + 1) * STATE)
        v = preact(0, ROWS, cols, gtaps_ref[k, :KSIZE], gtaps_ref[k, KSIZE : KSIZE + 1])
        out[...] = (v * sigmoid(v)).astype(BF16)
    v = preact(0, ROWS, slice(SIG + 2 * STATE, WIDE), mtaps_ref[...], mbias_ref[...])
    s = sigmoid(v)
    slope[:, SIG:] = s * (1.0 + v * (1.0 - s))
    sig_copy.wait()
    pad[EDGE + BLK :, :SIG] = sig_in[BLK:, :].astype(F32)
    sig_rows(0, EDGE)
    sig_rows(BLK, BLK)
    dout_copy.wait()
    for q in range(SIG // STATE):
        cols = third(q)
        cols2 = slice(SIG + q * STATE, SIG + (q + 1) * STATE)
        cols3 = slice(2 * SIG + q * STATE, 2 * SIG + (q + 1) * STATE)
        scaled_b = (signal_ref[:, cols].astype(F32) * wide3[:, cols]).astype(BF16)
        scaled_ref[:, cols] = scaled_b
        weighted_ref[:, cols] = (scaled_b.astype(F32) * wide3[:, cols2]).astype(BF16)
        sgrad_ref[:, cols] = (dout_ref[:, cols].astype(F32) * wide3[:, cols3]).astype(BF16)
    low, high = slice(0, BLK), slice(BLK, ROWS)
    second_sg[...] = tn(sgrad_ref[high, :], omap_ref[high, :])
    gs[...] = tn(sgrad_ref[low, :], omap_ref[low, :])
    first_local[...] = tn(weighted_ref[low, :], imap_ref[low, :])
    second_local = tn(weighted_ref[high, :], imap_ref[high, :])
    for h in range(HERE):
        at = slice(h * HDIM, (h + 1) * HDIM)
        gs[at, :] = gs[at, :] + end_low8[h : h + 1] * second_sg[at, :]
        xs[at, :] = (end_high8[h : h + 1] * first_local[at, :] + second_local[at, :]).astype(BF16)

    def mine(d):
        return pl.ds(pl.multiple_of(d * share, share), share)

    def x_copy(d):
        return remote(xs.at[mine(d)], xr.at[me], xs_sem.at[d], xr_sem.at[me], ctx=d)

    def g_copy(d):
        return remote(gs.at[mine(d)], gr.at[me], gs_sem.at[d], gr_sem.at[me], ctx=d)

    def e_copy(d):
        return remote(es.at[d // per_head], er.at[me], es_sem.at[d], er_sem.at[me], ctx=d)

    def h_copy(d):
        return remote(yh.at[d], lh.at[mine(me)], hs_sem.at[d], hr_sem.at[me], ctx=d)

    def c_copy(d):
        return remote(yc.at[d], lc.at[mine(me)], cs_sem.at[d], cr_sem.at[me], ctx=d)

    def send(i, _):
        d = other(me, i, n)
        g_copy(d).start()
        x_copy(d).start()
        e_copy(d).start()
        return 0

    lax.fori_loop(1, n, send, 0)
    xr[me] = xs[mine(me)]
    gr[me] = gs[mine(me)]
    er[me] = es[me // per_head]

    score = nt(omap_ref[...], imap_ref[...])
    lane_row = lax.broadcasted_iota(jnp.int32, (ROWS, STATE), 1)
    grad_score = jnp.zeros((ROWS, ROWS), F32)
    for q in range(HERE // 2):
        cols = third(q)
        d_pair = dout_ref[:, cols].astype(F32)
        d_two = jnp.concatenate(
            [jnp.where(lane_row < HDIM, d_pair, 0.0), jnp.where(lane_row < HDIM, 0.0, d_pair)],
            axis=0,
        ).astype(BF16)
        grad_mix2 = nt(d_two, scaled_ref[:, cols])
        mixes = []
        for k in range(2):
            h = 2 * q + k
            grad_mix = grad_mix2[k * ROWS : (k + 1) * ROWS]
            gap = jnp.minimum(ds_col[:, h : h + 1] - ds[h : h + 1, :], 0.0)
            decay = jnp.where(lower, jnp.exp(gap), 0.0)
            mix = score * decay
            mixes.append(mix.astype(BF16))
            grad_score = grad_score + grad_mix * decay
            product = grad_mix * mix
            drow[h : h + 1, :] = nt(ones8, product, HIGH)[0:1] - jnp.sum(
                product, axis=0, keepdims=True
            )
        intra[:, cols] = tn(jnp.concatenate(mixes, axis=0), d_two)
    grad_score = grad_score.astype(BF16)
    mg[0] = tn(grad_score, omap_ref[...])
    mg[1] = nn(grad_score, imap_ref[...])

    def arrived(i, _):
        s = other(me, i, n)
        remote(es.at[s // per_head], er.at[s], es_sem.at[s], er_sem.at[s], ctx=s).wait_recv()
        remote(xs.at[mine(s)], xr.at[s], xs_sem.at[s], xr_sem.at[s], ctx=s).wait_recv()
        remote(gs.at[mine(s)], gr.at[s], gs_sem.at[s], gr_sem.at[s], ctx=s).wait_recv()
        return 0

    lax.fori_loop(1, n, arrived, 0)
    zero = jnp.zeros((share, STATE), F32)

    def holder(i):
        return jnp.where(i < n // 2, 2 * i, 2 * (n - 1 - i) + 1)

    def chain(i, state):
        h, g = state
        up, down = holder(i), holder(n - 1 - i)
        yh[up] = h.astype(BF16)
        yc[down] = g
        h = er[up] * h + xr[up].astype(F32)
        g = er[down] * g + gr[down]
        return h, g

    lax.fori_loop(0, n, chain, (zero, zero))

    def back(i, _):
        d = other(me, i, n)
        c_copy(d).start()
        h_copy(d).start()
        return 0

    lax.fori_loop(1, n, back, 0)
    lh[mine(me)] = yh[me]
    lc[mine(me)] = yc[me]

    def linked(i, _):
        d = other(me, i, n)
        g_copy(d).wait_send()
        x_copy(d).wait_send()
        e_copy(d).wait_send()
        remote(yh.at[d], lh.at[mine(d)], hs_sem.at[d], hr_sem.at[d], ctx=d).wait_recv()
        remote(yc.at[d], lc.at[mine(d)], cs_sem.at[d], cr_sem.at[d], ctx=d).wait_recv()
        return 0

    lax.fori_loop(1, n, linked, 0)
    lk[0] = lh[...]
    lk[3] = lc[...].astype(BF16)
    for h in range(HERE):
        at = slice(h * HDIM, (h + 1) * HDIM)
        lk[1, at, :] = (end_low8[h : h + 1] * lh[at, :].astype(F32) + first_local[at, :]).astype(
            BF16
        )
        lk[2, at, :] = (second_sg[at, :] + end_high8[h : h + 1] * lc[at, :]).astype(BF16)

    for b, rows in enumerate((low, high)):
        mg[0, rows, :] = mg[0, rows, :] + nn(weighted_ref[rows, :], lk[2 + b])
        mg[1, rows, :] = mg[1, rows, :] + nn(sgrad_ref[rows, :], lk[b])

    def m_copy(k):
        return remote(
            mg.at[k], mgot.at[side], ms_sem.at[k], mr_sem.at[side], fsdp=group + k * half
        )

    for k in range(2):

        @pl.when(group + k * half != f)
        def _():
            m_copy(k).start()

        @pl.when(group + k * half == f)
        def _():
            mgot[side] = mg[k]

    end_terms = []
    for b, rows in enumerate((low, high)):
        oh[rows, :] = nt(omap_ref[rows, :], lk[b])
        gw[rows, :] = nt(imap_ref[rows, :], lk[2 + b])
        both = lk[b].astype(F32) * lk[2 + b].astype(F32)
        both = jnp.sum(both.reshape(HERE, HDIM, STATE), axis=1)
        end_terms.append(jnp.sum(both, axis=1, keepdims=True))
    step_w = wide3[:, :SIG]
    end_w = wide3[:, SIG : 2 * SIG]
    exp_w = wide3[:, 2 * SIG :]
    d_f = dout_ref[...].astype(F32)
    signal_f = signal_ref[...].astype(F32)
    gw_v = gw[...]
    back_row = per_row(gw_v * scaled_ref[...].astype(F32)) * to_end
    grad_sum = per_row(d_f * exp_w * oh[...]) - back_row + drow[...]
    back_low = jnp.sum(jnp.where(lane < BLK, back_row, 0.0), axis=1, keepdims=True)
    back_high = jnp.sum(jnp.where(lane < BLK, 0.0, back_row), axis=1, keepdims=True)
    last_low = back_low + end_low * end_terms[0]
    last_high = back_high + end_high * end_terms[1]
    grad_sum = grad_sum + jnp.where(
        lane == BLK - 1, last_low, jnp.where(lane == ROWS - 1, last_high, 0.0)
    )
    grad_log = nn(grad_sum, lower_f, HIGH)
    grad_scaled = gw_v * end_w + intra[...]
    grad_step = grad_log * rate + per_row(grad_scaled * signal_f)
    grad_dt = grad_step * sigmoid(logits)
    ddt_mine[...] = grad_dt
    ddt_copy = remote(ddt_mine, ddt_got, w_sem.at[0], w_sem.at[1], ctx=mate)
    ddt_copy.start()
    skip_w = nn(jnp.broadcast_to(skip_ref[...], (HERE, HERE)), spread1, HIGH)[0:1]
    gpad[:ROWS, :SIG] = (skip_w * d_f + grad_scaled * step_w) * slope[:, :SIG]
    part[TAIL + 3 :] = jnp.zeros((n - TAIL - 3, 1, STATE), F32)

    def small(at, row):
        part[at] = jnp.concatenate([row, jnp.zeros((1, STATE - HERE), F32)], axis=1)

    small(TAIL, nt(ones8, grad_log * step, HIGH)[0:1] * (-jnp.exp(alog_ref[...])))
    small(TAIL + 1, nt(ones8, grad_dt, HIGH)[0:1])
    small(TAIL + 2, nt(ones8, per_row(d_f * signal_f), HIGH)[0:1])

    def sums(cols, source, at):
        g = gpad[:ROWS, cols]
        for k in range(KSIZE):
            start = EDGE - RIM + k
            part[k * (OWN // STATE) + at] = jnp.sum(
                g * pad[start : start + ROWS, source], axis=0, keepdims=True
            )
        part[KSIZE * (OWN // STATE) + at] = jnp.sum(g, axis=0, keepdims=True)

    for q in range(SIG // STATE):
        sums(third(q), third(q), q)

    for k in range(2):

        @pl.when(first + k != f)
        def _():
            remote(
                mg.at[k], mgot.at[k], ms_sem.at[k], mr_sem.at[k], fsdp=first + k
            ).wait_recv()

    gpad[:ROWS, SIG:] = (mgot[0] + mgot[1]) * slope[:, SIG:]
    earlier = jnp.where(
        odd == 0, lax.rem(me + n - 2, n), jnp.where(me == n - 1, n - 2, lax.rem(me + 2, n))
    )
    earlier = jnp.where(me == 0, 1, earlier)
    rim_copy = remote(gpad.at[0:RIMS], rims, r_sem.at[0], r_sem.at[1], ctx=earlier)
    rim_copy.start()
    sums(slice(SIG, OWN), slice(SIG + 2 * STATE, WIDE), SIG // STATE)

    def p_copy(d):
        return remote(part.at[d], parts.at[me], ps_sem.at[d], pr_sem.at[me], ctx=d)

    def t_copy(d):
        return remote(mine_sum, total.at[me], ts_sem.at[d], tr_sem.at[me], ctx=d)

    def send_part(i, _):
        p_copy(other(me, i, n)).start()
        return 0

    lax.fori_loop(1, n, send_part, 0)
    parts[me] = part[me]

    rim_copy.wait()
    gpad[ROWS:] = jnp.where(me == 1, 0.0, rims[...])

    def raw(r):
        out = []
        for taps, cols in ((taps_ref, slice(0, SIG)), (mtaps_ref, slice(SIG, OWN))):
            acc = taps[RIM : RIM + 1] * gpad[r : r + BLK, cols]
            for k in range(RIM):
                acc = acc + taps[k : k + 1] * gpad[r + RIM - k : r + RIM - k + BLK, cols]
            out.append(acc)
        return jnp.concatenate(out, axis=1)

    swap[...] = raw(BLK)
    swap_copy = remote(swap, big.at[pl.ds(kept, BLK)], w_sem.at[2], w_sem.at[3], ctx=mate)
    swap_copy.start()

    def part_in(i, _):
        s = other(me, i, n)
        remote(part.at[s], parts.at[s], ps_sem.at[s], pr_sem.at[s], ctx=s).wait_recv()
        return 0

    lax.fori_loop(1, n, part_in, 0)
    mine_sum[...] = jnp.sum(parts[...], axis=0)

    def send_total(i, _):
        t_copy(other(me, i, n)).start()
        return 0

    lax.fori_loop(1, n, send_total, 0)
    total[me] = mine_sum[...]
    big[pl.ds(kept, BLK)] = raw(0)
    ddt_copy.wait()
    own, got = ddt_mine[...], ddt_got[...]
    ddt_low = jnp.where(odd == 0, own, turned(got))
    ddt_high = jnp.where(odd == 0, got, turned(own))
    ddt_ref[...] = jnp.where(lane < BLK, ddt_low, ddt_high)

    def done(i, _):
        d = other(me, i, n)
        h_copy(d).wait_send()
        c_copy(d).wait_send()
        p_copy(d).wait_send()
        t_copy(d).wait_send()
        remote(mine_sum, total.at[d], ts_sem.at[d], tr_sem.at[d], ctx=d).wait_recv()
        return 0

    lax.fori_loop(1, n, done, 0)
    for k in range(2):

        @pl.when(group + k * half != f)
        def _():
            m_copy(k).wait_send()

    swap_copy.wait()


def main(*operands):
    n = lax.axis_size("ctx")
    half = lax.axis_size("fsdp") // 2
    share = SIG // n
    dma = pltpu.SemaphoreType.DMA
    vm = pltpu.VMEM
    return pl.pallas_call(
        functools.partial(main_kernel, n, half),
        out_shape=(
            jax.ShapeDtypeStruct((ROWS, OWN), F32),
            jax.ShapeDtypeStruct((n, 1, STATE), F32),
            jax.ShapeDtypeStruct((HERE, ROWS), F32),
        ),
        in_specs=[pl.BlockSpec(memory_space=pl.ANY)] * len(operands),
        out_specs=(VM,) * 3,
        scratch_shapes=[
            vm((ROWS, SIG), BF16),
            vm((ROWS, 3 * STATE), BF16),
            vm((ROWS, SIG), BF16),
            vm((HERE, ROWS), F32),
            vm((HERE, ROWS), F32),
            vm((KSIZE, SIG), F32),
            vm((1, SIG), F32),
            vm((KSIZE, STATE), F32),
            vm((1, STATE), F32),
            vm((1, HERE), F32),
            vm((1, HERE), F32),
            vm((1, HERE), F32),
            vm((EDGE, WIDE), BF16),
            vm((EDGE, WIDE), BF16),
            vm((8, STATE), F32),
            vm((2, 8, STATE), F32),
            vm((EDGE + ROWS, WIDE), F32),
            vm((ROWS, OWN), F32),
            vm((ROWS, SIG), BF16),
            vm((ROWS, SIG), BF16),
            vm((ROWS, SIG), BF16),
            vm((ROWS, SIG), BF16),
            vm((ROWS, STATE), BF16),
            vm((ROWS, STATE), BF16),
            vm((ROWS, 3 * SIG), F32),
            vm((ROWS, SIG), F32),
            vm((ROWS, SIG), F32),
            vm((ROWS, SIG), F32),
            vm((HERE, ROWS), F32),
            vm((SIG, STATE), BF16),
            vm((SIG, STATE), F32),
            vm((HERE, 1, STATE), F32),
            vm((n, share, STATE), BF16),
            vm((n, share, STATE), F32),
            vm((n, 1, STATE), F32),
            vm((n, share, STATE), BF16),
            vm((n, share, STATE), F32),
            vm((SIG, STATE), BF16),
            vm((SIG, STATE), F32),
            vm((SIG, STATE), F32),
            vm((SIG, STATE), F32),
            vm((4, SIG, STATE), BF16),
            vm((2, ROWS, STATE), F32),
            vm((2, ROWS, STATE), F32),
            vm((ROWS + RIMS, OWN), F32),
            vm((RIMS, OWN), F32),
            vm((BLK, OWN), F32),
            vm((HERE, ROWS), F32),
            vm((HERE, ROWS), F32),
            vm((n, 1, STATE), F32),
            vm((n, 1, STATE), F32),
            vm((1, STATE), F32),
        ]
        + [dma((17,)), dma((6,)), dma((6,)), dma((1,)), dma((1,)), dma((2,)), dma((2,))]
        + [dma((n,))] * 10
        + [dma((2,)), dma((2,)), dma((2,)), dma((4,))]
        + [dma((n,))] * 4,
        compiler_params=pltpu.CompilerParams(
            collective_id=0, has_side_effects=True, vmem_limit_bytes=56 * 1024 * 1024
        ),
        name="main",
    )(*operands)


def last_kernel(
    scale, big, total, ddt,
    dsig, dmap, ddt_out, dtaps, dmtaps, dbias, dmbias, dalog, ddtb, dskip
):
    dsig[...] = big[:, :SIG]
    dmap[...] = big[:, SIG:]
    ddt_out[...] = ddt[...]
    for k in range(KSIZE + 1):
        for q in range(OWN // STATE):
            row = total[k * (OWN // STATE) + q] * scale
            cols = slice(q * STATE, (q + 1) * STATE)
            if q < SIG // STATE:
                if k < KSIZE:
                    dtaps[k : k + 1, cols] = row
                else:
                    dbias[:, cols] = row
            elif k < KSIZE:
                dmtaps[k : k + 1, :] = row
            else:
                dmbias[...] = row
    for k, out in enumerate((dalog, ddtb, dskip)):
        out[...] = total[TAIL + k][:, :HERE] * scale


def last(*operands):
    scale = 1.0 / math.sqrt(float(lax.axis_size("ctx") * ROWS))
    shapes = (
        (ROWS, SIG), (ROWS, STATE), (HERE, ROWS), (KSIZE, SIG), (KSIZE, STATE),
        (1, SIG), (1, STATE), (1, HERE), (1, HERE), (1, HERE),
    )
    return pl.pallas_call(
        functools.partial(last_kernel, scale),
        out_shape=tuple(jax.ShapeDtypeStruct(s, F32) for s in shapes),
        in_specs=[VM] * 3,
        out_specs=(VM,) * len(shapes),
        compiler_params=pltpu.CompilerParams(vmem_limit_bytes=8 * 1024 * 1024),
        name="last",
    )(*operands)


def shards(
    sig_raw,
    map_raw,
    step_size_logits,
    d_out,
    sig_taps,
    map_taps,
    sig_bias,
    map_bias,
    a_log,
    dt_bias,
    skip_gain,
):
    found = main(
        sig_raw, map_raw, step_size_logits.T, d_out, sig_taps, sig_bias[None, :], map_taps,
        map_bias[None, :], a_log[None, :], dt_bias[None, :], skip_gain[None, :],
    )
    out = last(*found)
    return out[:2] + (out[2].T,) + out[3:5] + tuple(a.reshape(-1) for a in out[5:])


def solution(mesh):
    return jax.shard_map(
        shards,
        mesh=mesh,
        in_specs=(
            P("ctx", "fsdp"),
            P("ctx", None),
            P("ctx", "fsdp"),
            P("ctx", "fsdp"),
            P(None, "fsdp"),
            P(None, "fsdp"),
            P("fsdp"),
            P("fsdp"),
            P("fsdp"),
            P("fsdp"),
            P("fsdp"),
        ),
        out_specs=(
            P("ctx", "fsdp"),
            P("ctx", "fsdp"),
            P("ctx", "fsdp"),
            P(None, "fsdp"),
            P(None, "fsdp"),
            P("fsdp"),
            P("fsdp"),
            P("fsdp"),
            P("fsdp"),
            P("fsdp"),
        ),
        check_vma=False,
    )
```

```python
import functools
import math

import jax
import jax.numpy as jnp
from jax import lax
from jax.experimental import pallas as pl
from jax.experimental.pallas import tpu as pltpu
from jax.sharding import PartitionSpec as P

HEADS = 128
HDIM = 64
STATE = 128
GROUPS = 8
HERE = 8
KSIZE = 4
RIM = KSIZE - 1
BLK = 64
ROWS = 2 * BLK
SIG = HERE * HDIM
WIDE = SIG + 3 * STATE
OWN = SIG + STATE
EDGE = 16
RIMS = 8
TAIL = (KSIZE + 1) * OWN // STATE
MESH = pl.DeviceIdType.MESH
VM = pl.BlockSpec(memory_space=pltpu.VMEM)
HIGH = lax.Precision.HIGHEST
F32 = jnp.float32
BF16 = jnp.bfloat16


def signal(sem, **where):
    pl.semaphore_signal(sem, inc=1, device_id=where, device_id_type=MESH)


def remote(src, dst, send_sem, recv_sem, **where):
    return pltpu.make_async_remote_copy(
        src_ref=src,
        dst_ref=dst,
        send_sem=send_sem,
        recv_sem=recv_sem,
        device_id=where,
        device_id_type=MESH,
    )


def other(me, i, n):
    off = jnp.where(lax.rem(i, 2) == 1, (i + 1) // 2, n - i // 2)
    return lax.rem(me + off, n)


def columns(start):
    return pl.ds(pl.multiple_of(start * STATE, STATE), STATE)


def nn(a, b, precision=None):
    return lax.dot_general(
        a, b, (((1,), (0,)), ((), ())), precision=precision, preferred_element_type=F32
    )


def nt(a, b, precision=None):
    return lax.dot_general(
        a, b, (((1,), (1,)), ((), ())), precision=precision, preferred_element_type=F32
    )


def tn(a, b):
    return lax.dot_general(a, b, (((0,), (0,)), ((), ())), preferred_element_type=F32)


def sigmoid(v):
    return 1.0 / (1.0 + jnp.exp(-v))


def log1p_small(e):
    series = e * (
        1.0 + e * (-1.0 / 2 + e * (1.0 / 3 + e * (-1.0 / 4 + e * (1.0 / 5 + e * (-1.0 / 6)))))
    )
    return jnp.where(e < 0.03, series, jnp.log(1.0 + e))


def main_kernel(
    n, half, sig_hbm, map_hbm, dt_hbm, dout_hbm, taps_hbm, bias_hbm, mtaps_hbm, mbias_hbm,
    alog_hbm, dtb_hbm, skip_hbm,
    big, total_hbm, ddt_hbm,
    sig_in, map_in, dout_ref, dt_in, dt_got, taps_ref, bias_ref, mtaps_ref, mbias_ref,
    alog_ref, dtb_ref, skip_ref, tail_own, tail_got, tap_row, gtaps_ref,
    pad, slope, signal_ref, scaled_ref, weighted_ref, sgrad_ref, imap_ref, omap_ref, wide3, intra,
    oh, gw, drow, xs, gs, es, xr, gr, er, yh, yc, lh, lc, first_local, second_sg, lk,
    mg, mgot, gpad, rims, swap, stay, ddt_mine, ddt_got, ddt_ref, part, near, far, total,
    low_part, low_near,
    l_sem, n_send, n_recv, b_send, b_recv, tap_send, tap_recv,
    xs_sem, xr_sem, gs_sem, gr_sem, es_sem, er_sem, hs_sem, hr_sem, cs_sem, cr_sem,
    ms_sem, mr_sem, r_sem, w_sem, q_send, q_near, q_far
):
    me = lax.axis_index("ctx")
    f = lax.axis_index("fsdp")
    odd = lax.rem(me, 2)
    mate = me + 1 - 2 * odd
    side_ctx = lax.rem(me + n - 1 + 2 * odd, n)
    slot = f // half
    first = 2 * (f - slot * half)
    group = f // 2
    side = f - 2 * group
    share = SIG // n
    per_head = n // HERE
    kept = pl.multiple_of(odd * BLK, BLK)
    given = pl.multiple_of((1 - odd) * BLK, BLK)
    ending = pl.multiple_of((1 - odd) * BLK + BLK - EDGE, EDGE)
    starts = (group, GROUPS + group, f)
    barrier = pltpu.get_barrier_semaphore()

    def fetch(i, src, dst):
        copy = pltpu.make_async_copy(src, dst, l_sem.at[i])
        copy.start()
        return copy

    def third(k):
        return slice(k * STATE, (k + 1) * STATE)

    local = [
        fetch(0, mtaps_hbm, mtaps_ref),
        fetch(1, mbias_hbm, mbias_ref),
        fetch(2, dt_hbm, dt_in),
        fetch(3, alog_hbm, alog_ref),
        fetch(4, dtb_hbm, dtb_ref),
        fetch(5, skip_hbm, skip_ref),
        fetch(6, taps_hbm, taps_ref),
        fetch(7, bias_hbm, bias_ref),
        fetch(8, sig_hbm.at[pl.ds(kept, BLK)], sig_in.at[0:BLK]),
        fetch(9, dout_hbm.at[pl.ds(kept, BLK)], dout_ref.at[0:BLK]),
        fetch(10, sig_hbm.at[pl.ds(ending, EDGE)], tail_own.at[:, 0:SIG]),
    ]
    for k, start in enumerate(starts):
        local.append(
            fetch(
                11 + k,
                map_hbm.at[pl.ds(kept, BLK), columns(start)],
                map_in.at[0:BLK, third(k)],
            )
        )
        local.append(
            fetch(
                14 + k,
                map_hbm.at[pl.ds(ending, EDGE), columns(start)],
                tail_own.at[:, SIG + k * STATE : SIG + (k + 1) * STATE],
            )
        )

    def greet(i, _):
        signal(barrier, ctx=other(me, i, n))
        return 0

    lax.fori_loop(1, n, greet, 0)
    for k in range(2):

        @pl.when(group + k * half != f)
        def _():
            signal(barrier, fsdp=group + k * half)

        @pl.when(first + k != f)
        def _():
            signal(barrier, fsdp=first + k)

    for copy in local:
        copy.wait()
    tap_row[0:KSIZE] = mtaps_ref[...]
    tap_row[KSIZE : KSIZE + 1] = mbias_ref[...]
    tap_row[KSIZE + 1 :] = jnp.zeros((8 - KSIZE - 1, STATE), F32)
    selves = jnp.where(group == f, 1, 0) + jnp.where(group + half == f, 1, 0)
    pl.semaphore_wait(barrier, n - 1 + 4 - 2 * selves)

    for k in range(2):

        @pl.when(first + k != f)
        def _():
            remote(
                tap_row, gtaps_ref.at[slot], tap_send.at[k], tap_recv.at[slot], fsdp=first + k
            ).start()

        @pl.when(group + k * half == f)
        def _():
            gtaps_ref[k] = tap_row[...]

    def to_mate(i, src, dst):
        copy = remote(src, dst, n_send.at[i], n_recv.at[i], ctx=mate)
        copy.start()
        return copy

    def to_side(i, dst_cols):
        copy = remote(
            tail_own.at[:, dst_cols], tail_got.at[:, dst_cols], b_send.at[i], b_recv.at[i],
            ctx=side_ctx,
        )
        copy.start()
        return copy

    dt_copy = to_mate(0, dt_hbm, dt_got)
    tail_copy = to_side(0, slice(0, WIDE))
    map_copies = [
        to_mate(
            1 + k, map_hbm.at[pl.ds(given, BLK), columns(start)], map_in.at[BLK:ROWS, third(k)]
        )
        for k, start in enumerate(starts)
    ]
    sig_copy = to_mate(4, sig_hbm.at[pl.ds(given, BLK)], sig_in.at[BLK:ROWS])
    dout_copy = to_mate(5, dout_hbm.at[pl.ds(given, BLK)], dout_ref.at[BLK:ROWS])

    lane = lax.broadcasted_iota(jnp.int32, (HERE, ROWS), 1)
    row_id = lax.broadcasted_iota(jnp.int32, (ROWS, ROWS), 0)
    col_id = lax.broadcasted_iota(jnp.int32, (ROWS, ROWS), 1)
    lower = ((row_id >= BLK) == (col_id >= BLK)) & (col_id <= row_id)
    lower_f = jnp.where(lower, 1.0, 0.0).astype(F32)
    eye = jnp.where(row_id == col_id, 1.0, 0.0).astype(F32)
    eye8 = eye[:HERE, :HERE]
    ones8 = jnp.ones((HERE, ROWS), F32)
    head3 = lax.broadcasted_iota(jnp.int32, (3 * HERE, 3 * SIG), 0)
    spread3 = jnp.where(
        lax.broadcasted_iota(jnp.int32, (3 * HERE, 3 * SIG), 1) // HDIM == head3, 1.0, 0.0
    ).astype(F32)
    spread1 = spread3[:HERE, :SIG]

    def in_rows(ref):
        return nt(eye8, jnp.broadcast_to(ref[...], (ROWS, HERE)), HIGH)

    def per_row(y):
        return nt(spread1, y, HIGH)

    def turned(x):
        return pltpu.roll(x, BLK, 1)

    def preact(r, rows, cols, taps, bias):
        acc = bias
        for k in range(KSIZE):
            start = EDGE - RIM + k + r
            acc = acc + taps[k : k + 1] * pad[start : start + rows, cols]
        return acc

    def sig_rows(r, count):
        rows = slice(r, r + count)
        for q in range(SIG // STATE):
            cols = third(q)
            v = preact(r, count, cols, taps_ref[:, cols], bias_ref[:, cols])
            s = sigmoid(v)
            slope[rows, cols] = s * (1.0 + v * (1.0 - s))
            signal_ref[rows, cols] = (v * s).astype(BF16)

    pad[EDGE : EDGE + BLK, :SIG] = sig_in[:BLK, :].astype(F32)
    pad[EDGE : EDGE + BLK, SIG:] = map_in[:BLK, :].astype(F32)
    sig_rows(EDGE, BLK - EDGE)
    dt_copy.wait()
    own, got = dt_in[...], dt_got[...]
    own = jnp.where(odd == 0, own, turned(own))
    got = jnp.where(odd == 0, turned(got), got)
    logits = jnp.where(lane < BLK, own, got) + in_rows(dtb_ref)
    rate = -jnp.exp(in_rows(alog_ref))
    step = jnp.maximum(logits, 0.0) + log1p_small(jnp.exp(-jnp.abs(logits)))
    ds = nt(step * rate, lower_f, HIGH)
    end_low = jnp.exp(ds[:, BLK - 1 : BLK])
    end_high = jnp.exp(ds[:, ROWS - 1 : ROWS])
    end = jnp.where(lane < BLK, ds[:, BLK - 1 : BLK], ds[:, ROWS - 1 : ROWS])
    to_end = jnp.exp(end - ds)
    col4 = nt(eye, jnp.concatenate([step, to_end, jnp.exp(ds), ds], axis=0), HIGH)
    ds_col = col4[:, 3 * HERE :]
    wide3[...] = nn(col4[:, : 3 * HERE], spread3, HIGH)
    end_low8 = jnp.broadcast_to(end_low, (HERE, STATE))
    end_high8 = jnp.broadcast_to(end_high, (HERE, STATE))
    both_ends = end_low8 * end_high8
    for h in range(HERE):
        es[h] = both_ends[h : h + 1]

    def e_copy(d):
        return remote(es.at[d // per_head], er.at[me], es_sem.at[d], er_sem.at[me], ctx=d)

    def send_ends(i, _):
        e_copy(other(me, i, n)).start()
        return 0

    lax.fori_loop(1, n, send_ends, 0)
    er[me] = es[me // per_head]

    for k in range(2):

        @pl.when(group + k * half != f)
        def _():
            remote(
                tap_row, gtaps_ref.at[k], tap_send.at[k], tap_recv.at[k], fsdp=group + k * half
            ).wait_recv()

        @pl.when(first + k != f)
        def _():
            remote(
                tap_row, gtaps_ref.at[slot], tap_send.at[k], tap_recv.at[slot], fsdp=first + k
            ).wait_send()

    tail_copy.wait()
    for copy in map_copies:
        copy.wait()
    keep = jnp.where(me == 0, 0.0, 1.0).astype(F32)
    before = jnp.where(me == n - 1, tail_own[...].astype(F32), tail_got[...].astype(F32))
    pad[:EDGE] = before * keep
    pad[EDGE + BLK :, SIG:] = map_in[BLK:, :].astype(F32)
    for k, out in enumerate((imap_ref, omap_ref)):
        cols = slice(SIG + k * STATE, SIG + (k + 1) * STATE)
        v = preact(0, ROWS, cols, gtaps_ref[k, :KSIZE], gtaps_ref[k, KSIZE : KSIZE + 1])
        out[...] = (v * sigmoid(v)).astype(BF16)
    v = preact(0, ROWS, slice(SIG + 2 * STATE, WIDE), mtaps_ref[...], mbias_ref[...])
    s = sigmoid(v)
    slope[:, SIG:] = s * (1.0 + v * (1.0 - s))
    sig_copy.wait()
    pad[EDGE + BLK :, :SIG] = sig_in[BLK:, :].astype(F32)
    sig_rows(0, EDGE)
    sig_rows(BLK, BLK)
    dout_copy.wait()
    for q in range(SIG // STATE):
        cols = third(q)
        cols2 = slice(SIG + q * STATE, SIG + (q + 1) * STATE)
        cols3 = slice(2 * SIG + q * STATE, 2 * SIG + (q + 1) * STATE)
        scaled_b = (signal_ref[:, cols].astype(F32) * wide3[:, cols]).astype(BF16)
        scaled_ref[:, cols] = scaled_b
        weighted_ref[:, cols] = (scaled_b.astype(F32) * wide3[:, cols2]).astype(BF16)
        sgrad_ref[:, cols] = (dout_ref[:, cols].astype(F32) * wide3[:, cols3]).astype(BF16)
    low, high = slice(0, BLK), slice(BLK, ROWS)
    second_sg[...] = tn(sgrad_ref[high, :], omap_ref[high, :])
    gs[...] = tn(sgrad_ref[low, :], omap_ref[low, :])
    for h in range(HERE):
        at = slice(h * HDIM, (h + 1) * HDIM)
        gs[at, :] = gs[at, :] + end_low8[h : h + 1] * second_sg[at, :]

    def mine(d):
        return pl.ds(pl.multiple_of(d * share, share), share)

    def x_copy(d):
        return remote(xs.at[mine(d)], xr.at[me], xs_sem.at[d], xr_sem.at[me], ctx=d)

    def g_copy(d):
        return remote(gs.at[mine(d)], gr.at[me], gs_sem.at[d], gr_sem.at[me], ctx=d)

    def h_copy(d):
        return remote(yh.at[d], lh.at[mine(me)], hs_sem.at[d], hr_sem.at[me], ctx=d)

    def c_copy(d):
        return remote(yc.at[d], lc.at[mine(me)], cs_sem.at[d], cr_sem.at[me], ctx=d)

    def send_g(i, _):
        g_copy(other(me, i, n)).start()
        return 0

    def send_x(i, _):
        x_copy(other(me, i, n)).start()
        return 0

    lax.fori_loop(1, n, send_g, 0)
    first_local[...] = tn(weighted_ref[low, :], imap_ref[low, :])
    second_local = tn(weighted_ref[high, :], imap_ref[high, :])
    for h in range(HERE):
        at = slice(h * HDIM, (h + 1) * HDIM)
        xs[at, :] = (end_high8[h : h + 1] * first_local[at, :] + second_local[at, :]).astype(BF16)
    lax.fori_loop(1, n, send_x, 0)
    xr[me] = xs[mine(me)]
    gr[me] = gs[mine(me)]

    score = nt(omap_ref[...], imap_ref[...])
    lane_row = lax.broadcasted_iota(jnp.int32, (ROWS, STATE), 1)
    grad_score = jnp.zeros((ROWS, ROWS), F32)
    for q in range(HERE // 2):
        cols = third(q)
        d_pair = dout_ref[:, cols].astype(F32)
        d_two = jnp.concatenate(
            [jnp.where(lane_row < HDIM, d_pair, 0.0), jnp.where(lane_row < HDIM, 0.0, d_pair)],
            axis=0,
        ).astype(BF16)
        grad_mix2 = nt(d_two, scaled_ref[:, cols])
        mixes = []
        for k in range(2):
            h = 2 * q + k
            grad_mix = grad_mix2[k * ROWS : (k + 1) * ROWS]
            gap = jnp.minimum(ds_col[:, h : h + 1] - ds[h : h + 1, :], 0.0)
            decay = jnp.where(lower, jnp.exp(gap), 0.0)
            mix = score * decay
            mixes.append(mix.astype(BF16))
            grad_score = grad_score + grad_mix * decay
            product = grad_mix * mix
            drow[h : h + 1, :] = nt(ones8, product, HIGH)[0:1] - jnp.sum(
                product, axis=0, keepdims=True
            )
        intra[:, cols] = tn(jnp.concatenate(mixes, axis=0), d_two)
    grad_score = grad_score.astype(BF16)
    mg[0] = tn(grad_score, omap_ref[...])
    mg[1] = nn(grad_score, imap_ref[...])

    def holder(i):
        return jnp.where(i < n // 2, 2 * i, 2 * (n - 1 - i) + 1)

    zero = jnp.zeros((share, STATE), F32)

    def g_arrived(i, _):
        s = other(me, i, n)
        remote(es.at[s // per_head], er.at[s], es_sem.at[s], er_sem.at[s], ctx=s).wait_recv()
        remote(gs.at[mine(s)], gr.at[s], gs_sem.at[s], gr_sem.at[s], ctx=s).wait_recv()
        return 0

    def to_front(i, g):
        at = holder(n - 1 - i)
        yc[at] = g
        return er[at] * g + gr[at]

    def send_c(i, _):
        c_copy(other(me, i, n)).start()
        return 0

    def x_arrived(i, _):
        s = other(me, i, n)
        remote(xs.at[mine(s)], xr.at[s], xs_sem.at[s], xr_sem.at[s], ctx=s).wait_recv()
        return 0

    def to_back(i, h):
        at = holder(i)
        yh[at] = h.astype(BF16)
        return er[at] * h + xr[at].astype(F32)

    def send_h(i, _):
        h_copy(other(me, i, n)).start()
        return 0

    lax.fori_loop(1, n, g_arrived, 0)
    lax.fori_loop(0, n, to_front, zero)
    lax.fori_loop(1, n, send_c, 0)
    lax.fori_loop(1, n, x_arrived, 0)
    lax.fori_loop(0, n, to_back, zero)
    lax.fori_loop(1, n, send_h, 0)
    lh[mine(me)] = yh[me]
    lc[mine(me)] = yc[me]
    step_w = wide3[:, :SIG]
    end_w = wide3[:, SIG : 2 * SIG]
    exp_w = wide3[:, 2 * SIG :]
    d_f = dout_ref[...].astype(F32)
    signal_f = signal_ref[...].astype(F32)
    skip_w = nn(jnp.broadcast_to(skip_ref[...], (HERE, HERE)), spread1, HIGH)[0:1]
    part[TAIL + 3 :] = jnp.zeros((n - TAIL - 3, STATE), F32)

    def small(at, row):
        part[at : at + 1] = jnp.concatenate([row, jnp.zeros((1, STATE - HERE), F32)], axis=1)

    small(TAIL + 2, nt(ones8, per_row(d_f * signal_f), HIGH)[0:1])

    def m_copy(k):
        return remote(
            mg.at[k], mgot.at[side], ms_sem.at[k], mr_sem.at[side], fsdp=group + k * half
        )

    def to_owner(k):
        @pl.when(group + k * half != f)
        def _():
            m_copy(k).start()

        @pl.when(group + k * half == f)
        def _():
            mgot[side] = mg[k]

    def c_in(i, _):
        d = other(me, i, n)
        g_copy(d).wait_send()
        e_copy(d).wait_send()
        remote(yc.at[d], lc.at[mine(d)], cs_sem.at[d], cr_sem.at[d], ctx=d).wait_recv()
        return 0

    lax.fori_loop(1, n, c_in, 0)
    lk[3] = lc[...].astype(BF16)
    for h in range(HERE):
        at = slice(h * HDIM, (h + 1) * HDIM)
        lk[2, at, :] = (second_sg[at, :] + end_high8[h : h + 1] * lc[at, :]).astype(BF16)
    for b, rows in enumerate((low, high)):
        mg[0, rows, :] = mg[0, rows, :] + nn(weighted_ref[rows, :], lk[2 + b])
    to_owner(0)
    for b, rows in enumerate((low, high)):
        gw[rows, :] = nt(imap_ref[rows, :], lk[2 + b])
    gw_v = gw[...]
    back_row = per_row(gw_v * scaled_ref[...].astype(F32)) * to_end
    back_low = jnp.sum(jnp.where(lane < BLK, back_row, 0.0), axis=1, keepdims=True)
    back_high = jnp.sum(jnp.where(lane < BLK, 0.0, back_row), axis=1, keepdims=True)
    grad_scaled = gw_v * end_w + intra[...]
    own_step = per_row(grad_scaled * signal_f)
    gpad[:ROWS, :SIG] = (skip_w * d_f + grad_scaled * step_w) * slope[:, :SIG]

    def sums(cols, source, at):
        g = gpad[:ROWS, cols]
        for k in range(KSIZE):
            start = EDGE - RIM + k
            row = k * (OWN // STATE) + at
            part[row : row + 1] = jnp.sum(
                g * pad[start : start + ROWS, source], axis=0, keepdims=True
            )
        row = KSIZE * (OWN // STATE) + at
        part[row : row + 1] = jnp.sum(g, axis=0, keepdims=True)

    for q in range(SIG // STATE):
        sums(third(q), third(q), q)

    def h_in(i, _):
        d = other(me, i, n)
        x_copy(d).wait_send()
        remote(yh.at[d], lh.at[mine(d)], hs_sem.at[d], hr_sem.at[d], ctx=d).wait_recv()
        return 0

    lax.fori_loop(1, n, h_in, 0)
    lk[0] = lh[...]
    for h in range(HERE):
        at = slice(h * HDIM, (h + 1) * HDIM)
        lk[1, at, :] = (end_low8[h : h + 1] * lh[at, :].astype(F32) + first_local[at, :]).astype(
            BF16
        )
    for b, rows in enumerate((low, high)):
        mg[1, rows, :] = mg[1, rows, :] + nn(sgrad_ref[rows, :], lk[b])
    to_owner(1)
    end_terms = []
    for b, rows in enumerate((low, high)):
        oh[rows, :] = nt(omap_ref[rows, :], lk[b])
        both = lk[b].astype(F32) * lk[2 + b].astype(F32)
        both = jnp.sum(both.reshape(HERE, HDIM, STATE), axis=1)
        end_terms.append(jnp.sum(both, axis=1, keepdims=True))
    grad_sum = per_row(d_f * exp_w * oh[...]) - back_row + drow[...]
    last_low = back_low + end_low * end_terms[0]
    last_high = back_high + end_high * end_terms[1]
    grad_sum = grad_sum + jnp.where(
        lane == BLK - 1, last_low, jnp.where(lane == ROWS - 1, last_high, 0.0)
    )
    grad_log = nn(grad_sum, lower_f, HIGH)
    grad_step = grad_log * rate + own_step
    grad_dt = grad_step * sigmoid(logits)
    ddt_mine[...] = grad_dt
    ddt_copy = remote(ddt_mine, ddt_got, w_sem.at[0], w_sem.at[1], ctx=mate)
    ddt_copy.start()
    small(TAIL, nt(ones8, grad_log * step, HIGH)[0:1] * (-jnp.exp(alog_ref[...])))
    small(TAIL + 1, nt(ones8, grad_dt, HIGH)[0:1])

    for k in range(2):

        @pl.when(first + k != f)
        def _():
            remote(
                mg.at[k], mgot.at[k], ms_sem.at[k], mr_sem.at[k], fsdp=first + k
            ).wait_recv()

    gpad[:ROWS, SIG:] = (mgot[0] + mgot[1]) * slope[:, SIG:]
    earlier = jnp.where(
        odd == 0, lax.rem(me + n - 2, n), jnp.where(me == n - 1, n - 2, lax.rem(me + 2, n))
    )
    earlier = jnp.where(me == 0, 1, earlier)
    rim_copy = remote(gpad.at[0:RIMS], rims, r_sem.at[0], r_sem.at[1], ctx=earlier)
    rim_copy.start()
    sums(slice(SIG, OWN), slice(SIG + 2 * STATE, WIDE), SIG // STATE)

    heads_at, rest_at = slice(TAIL, TAIL + 3), slice(TAIL + 3, TAIL + 6)

    def narrow(ref):
        value = ref[heads_at]
        ref[rest_at] = value - value.astype(BF16).astype(F32)
        return ref[...].astype(BF16)

    planes = n // 2
    y = me // planes
    z = me - y * planes
    z_high = z // 4
    z_low = z - 4 * z_high
    here = 4 * y + z_low

    def near_at(k):
        s = lax.rem(here + k, 8)
        y_of = s // 4
        return y_of * planes + z_high * 4 + s - 4 * y_of, s

    def far_at(k):
        s = lax.rem(z_high + k, 4)
        return y * planes + 4 * s + z_low, s

    low_part[...] = narrow(part)
    sent = []
    for k in range(1, 8):
        d, _ = near_at(k)
        copy = remote(low_part, near.at[here], q_send.at[k], q_near.at[here], ctx=d)
        copy.start()
        sent.append(copy)
    near[here] = low_part[...]

    rim_copy.wait()
    gpad[ROWS:] = jnp.where(me == 1, 0.0, rims[...])

    def raw(r, out):
        for taps, cols in ((taps_ref, slice(0, SIG)), (mtaps_ref, slice(SIG, OWN))):
            acc = taps[RIM : RIM + 1] * gpad[r : r + BLK, cols]
            for k in range(RIM):
                acc = acc + taps[k : k + 1] * gpad[r + RIM - k : r + RIM - k + BLK, cols]
            out[:, cols] = acc

    raw(BLK, swap)
    swap_copy = remote(swap, big.at[pl.ds(kept, BLK)], w_sem.at[2], w_sem.at[3], ctx=mate)
    swap_copy.start()
    for k in range(1, 8):
        d, s = near_at(k)
        remote(low_part, near.at[s], q_send.at[k], q_near.at[s], ctx=d).wait_recv()
    part[...] = jnp.sum(near[...].astype(F32), axis=0)
    part[heads_at] = part[heads_at] + part[rest_at]
    low_near[...] = narrow(part)
    for k in range(1, 4):
        d, _ = far_at(k)
        copy = remote(low_near, far.at[z_high], q_send.at[7 + k], q_far.at[z_high], ctx=d)
        copy.start()
        sent.append(copy)
    far[z_high] = low_near[...]
    raw(0, stay)
    stay_copy = fetch(0, stay, big.at[pl.ds(kept, BLK)])
    ddt_copy.wait()
    own, got = ddt_mine[...], ddt_got[...]
    ddt_low = jnp.where(odd == 0, own, turned(got))
    ddt_high = jnp.where(odd == 0, got, turned(own))
    ddt_ref[...] = jnp.where(lane < BLK, ddt_low, ddt_high)
    ddt_out = fetch(1, ddt_ref, ddt_hbm)
    for k in range(1, 4):
        d, s = far_at(k)
        remote(low_near, far.at[s], q_send.at[7 + k], q_far.at[s], ctx=d).wait_recv()
    total[...] = jnp.sum(far[...].astype(F32), axis=0)
    total[heads_at] = total[heads_at] + total[rest_at]
    total_out = fetch(2, total, total_hbm)
    for copy in sent:
        copy.wait_send()

    def done(i, _):
        d = other(me, i, n)
        h_copy(d).wait_send()
        c_copy(d).wait_send()
        return 0

    lax.fori_loop(1, n, done, 0)
    for k in range(2):

        @pl.when(group + k * half != f)
        def _():
            m_copy(k).wait_send()

    stay_copy.wait()
    ddt_out.wait()
    total_out.wait()
    swap_copy.wait()


def main(*operands):
    n = lax.axis_size("ctx")
    half = lax.axis_size("fsdp") // 2
    share = SIG // n
    dma = pltpu.SemaphoreType.DMA
    vm = pltpu.VMEM
    return pl.pallas_call(
        functools.partial(main_kernel, n, half),
        out_shape=(
            jax.ShapeDtypeStruct((ROWS, OWN), F32),
            jax.ShapeDtypeStruct((n, STATE), F32),
            jax.ShapeDtypeStruct((HERE, ROWS), F32),
        ),
        in_specs=[pl.BlockSpec(memory_space=pl.ANY)] * len(operands),
        out_specs=(pl.BlockSpec(memory_space=pl.ANY),) * 3,
        scratch_shapes=[
            vm((ROWS, SIG), BF16),
            vm((ROWS, 3 * STATE), BF16),
            vm((ROWS, SIG), BF16),
            vm((HERE, ROWS), F32),
            vm((HERE, ROWS), F32),
            vm((KSIZE, SIG), F32),
            vm((1, SIG), F32),
            vm((KSIZE, STATE), F32),
            vm((1, STATE), F32),
            vm((1, HERE), F32),
            vm((1, HERE), F32),
            vm((1, HERE), F32),
            vm((EDGE, WIDE), BF16),
            vm((EDGE, WIDE), BF16),
            vm((8, STATE), F32),
            vm((2, 8, STATE), F32),
            vm((EDGE + ROWS, WIDE), F32),
            vm((ROWS, OWN), F32),
            vm((ROWS, SIG), BF16),
            vm((ROWS, SIG), BF16),
            vm((ROWS, SIG), BF16),
            vm((ROWS, SIG), BF16),
            vm((ROWS, STATE), BF16),
            vm((ROWS, STATE), BF16),
            vm((ROWS, 3 * SIG), F32),
            vm((ROWS, SIG), F32),
            vm((ROWS, SIG), F32),
            vm((ROWS, SIG), F32),
            vm((HERE, ROWS), F32),
            vm((SIG, STATE), BF16),
            vm((SIG, STATE), F32),
            vm((HERE, 1, STATE), F32),
            vm((n, share, STATE), BF16),
            vm((n, share, STATE), F32),
            vm((n, 1, STATE), F32),
            vm((n, share, STATE), BF16),
            vm((n, share, STATE), F32),
            vm((SIG, STATE), BF16),
            vm((SIG, STATE), F32),
            vm((SIG, STATE), F32),
            vm((SIG, STATE), F32),
            vm((4, SIG, STATE), BF16),
            vm((2, ROWS, STATE), F32),
            vm((2, ROWS, STATE), F32),
            vm((ROWS + RIMS, OWN), F32),
            vm((RIMS, OWN), F32),
            vm((BLK, OWN), F32),
            vm((BLK, OWN), F32),
            vm((HERE, ROWS), F32),
            vm((HERE, ROWS), F32),
            vm((HERE, ROWS), F32),
            vm((n, STATE), F32),
            vm((8, n, STATE), BF16),
            vm((4, n, STATE), BF16),
            vm((n, STATE), F32),
            vm((n, STATE), BF16),
            vm((n, STATE), BF16),
        ]
        + [dma((17,)), dma((6,)), dma((6,)), dma((1,)), dma((1,)), dma((2,)), dma((2,))]
        + [dma((n,))] * 10
        + [dma((2,)), dma((2,)), dma((2,)), dma((4,)), dma((11,)), dma((8,)), dma((4,))],
        compiler_params=pltpu.CompilerParams(
            collective_id=0, has_side_effects=True, vmem_limit_bytes=56 * 1024 * 1024
        ),
        name="main",
    )(*operands)


def last_kernel(
    scale, big, total, ddt,
    dsig, dmap, ddt_out, dtaps, dmtaps, dbias, dmbias, dalog, ddtb, dskip
):
    dsig[...] = big[:, :SIG]
    dmap[...] = big[:, SIG:]
    ddt_out[...] = ddt[...]
    for k in range(KSIZE + 1):
        for q in range(OWN // STATE):
            at = k * (OWN // STATE) + q
            row = total[at : at + 1] * scale
            cols = slice(q * STATE, (q + 1) * STATE)
            if q < SIG // STATE:
                if k < KSIZE:
                    dtaps[k : k + 1, cols] = row
                else:
                    dbias[:, cols] = row
            elif k < KSIZE:
                dmtaps[k : k + 1, :] = row
            else:
                dmbias[...] = row
    for k, out in enumerate((dalog, ddtb, dskip)):
        out[...] = total[TAIL + k : TAIL + k + 1, :HERE] * scale


def last(*operands):
    scale = 1.0 / math.sqrt(float(lax.axis_size("ctx") * ROWS))
    shapes = (
        (ROWS, SIG), (ROWS, STATE), (HERE, ROWS), (KSIZE, SIG), (KSIZE, STATE),
        (1, SIG), (1, STATE), (1, HERE), (1, HERE), (1, HERE),
    )
    return pl.pallas_call(
        functools.partial(last_kernel, scale),
        out_shape=tuple(jax.ShapeDtypeStruct(s, F32) for s in shapes),
        in_specs=[VM] * 3,
        out_specs=(VM,) * len(shapes),
        compiler_params=pltpu.CompilerParams(vmem_limit_bytes=8 * 1024 * 1024),
        name="last",
    )(*operands)


def shards(
    sig_raw,
    map_raw,
    step_size_logits,
    d_out,
    sig_taps,
    map_taps,
    sig_bias,
    map_bias,
    a_log,
    dt_bias,
    skip_gain,
):
    found = main(
        sig_raw, map_raw, step_size_logits.T, d_out, sig_taps, sig_bias[None, :], map_taps,
        map_bias[None, :], a_log[None, :], dt_bias[None, :], skip_gain[None, :],
    )
    out = last(*found)
    return out[:2] + (out[2].T,) + out[3:5] + tuple(a.reshape(-1) for a in out[5:])


def solution(mesh):
    return jax.shard_map(
        shards,
        mesh=mesh,
        in_specs=(
            P("ctx", "fsdp"),
            P("ctx", None),
            P("ctx", "fsdp"),
            P("ctx", "fsdp"),
            P(None, "fsdp"),
            P(None, "fsdp"),
            P("fsdp"),
            P("fsdp"),
            P("fsdp"),
            P("fsdp"),
            P("fsdp"),
        ),
        out_specs=(
            P("ctx", "fsdp"),
            P("ctx", "fsdp"),
            P("ctx", "fsdp"),
            P(None, "fsdp"),
            P(None, "fsdp"),
            P("fsdp"),
            P("fsdp"),
            P("fsdp"),
            P("fsdp"),
            P("fsdp"),
        ),
        check_vma=False,
    )
```

```python
import functools
import math

import jax
import jax.numpy as jnp
from jax import lax
from jax.experimental import pallas as pl
from jax.experimental.pallas import tpu as pltpu
from jax.sharding import PartitionSpec as P

HEADS = 128
HDIM = 64
STATE = 128
GROUPS = 8
HERE = 8
KSIZE = 4
RIM = KSIZE - 1
BLK = 64
ROWS = 2 * BLK
SIG = HERE * HDIM
WIDE = SIG + 3 * STATE
OWN = SIG + STATE
EDGE = 16
RIMS = 8
QUADS = SIG // STATE
SUMS = 24
FINE = 10
MESH = pl.DeviceIdType.MESH
VM = pl.BlockSpec(memory_space=pltpu.VMEM)
HBM = pl.BlockSpec(memory_space=pltpu.HBM)
HIGH = lax.Precision.HIGHEST
F32 = jnp.float32
BF16 = jnp.bfloat16


def signal(sem, **where):
    pl.semaphore_signal(sem, inc=1, device_id=where, device_id_type=MESH)


def remote(src, dst, send_sem, recv_sem, **where):
    return pltpu.make_async_remote_copy(
        src_ref=src,
        dst_ref=dst,
        send_sem=send_sem,
        recv_sem=recv_sem,
        device_id=where,
        device_id_type=MESH,
    )


def other(me, i, n):
    off = jnp.where(lax.rem(i, 2) == 1, (i + 1) // 2, n - i // 2)
    return lax.rem(me + off, n)


def columns(start):
    return pl.ds(pl.multiple_of(start * STATE, STATE), STATE)


def nn(a, b, precision=None):
    return lax.dot_general(
        a, b, (((1,), (0,)), ((), ())), precision=precision, preferred_element_type=F32
    )


def nt(a, b, precision=None):
    return lax.dot_general(
        a, b, (((1,), (1,)), ((), ())), precision=precision, preferred_element_type=F32
    )


def tn(a, b):
    return lax.dot_general(a, b, (((0,), (0,)), ((), ())), preferred_element_type=F32)


def sigmoid(v):
    return 1.0 / (1.0 + jnp.exp(-v))


def log1p_small(e):
    series = e * (
        1.0 + e * (-1.0 / 2 + e * (1.0 / 3 + e * (-1.0 / 4 + e * (1.0 / 5 + e * (-1.0 / 6)))))
    )
    return jnp.where(e < 0.03, series, jnp.log(1.0 + e))


def pack(v):
    n, rows, _ = v.shape
    high = v.astype(BF16)
    value = high.astype(F32)
    tiny = jnp.abs(value) < 1e-30
    ratio = jnp.where(tiny, 0.0, (v - value) / jnp.where(tiny, 1.0, value))
    steps = jnp.clip(jnp.round(ratio * (256.0 * FINE)), -FINE, FINE)
    both = steps[:, : rows // 2] * (2.0 * FINE + 1.0) + steps[:, rows // 2 :]
    return high, both.astype(BF16)


def unpack(high, both):
    value = high.astype(F32)
    both = both.astype(F32)
    first = jnp.floor((both + (FINE + 0.5)) * (1.0 / (2.0 * FINE + 1.0)))
    second = both - first * (2.0 * FINE + 1.0)
    steps = jnp.concatenate([first, second], axis=-2)
    return value + value * steps * (1.0 / (256.0 * FINE))


def main_kernel(
    n, half, sig_hbm, map_hbm, dt_hbm, dout_hbm, taps_hbm, bias_hbm, mtaps_hbm, mbias_hbm,
    alog_hbm, dtb_hbm, skip_hbm,
    dsig_hbm, dmap_hbm, sums_hbm, small_hbm, ddt_hbm,
    sig_in, map_in, dout_ref, dt_in, dt_got, taps_ref, bias_ref, mtaps_ref, mbias_ref,
    alog_ref, dtb_ref, skip_ref, tail_own, tail_got, tap_row, gtaps_ref,
    pad, slope, signal_ref, scaled_ref, weighted_ref, sgrad_ref, imap_ref, omap_ref, wide3, intra,
    oh, gw, drow, xs, gs, es, xr, gr, er, yh, yc, lh, lc, first_local, second_sg, lk,
    mg, mgot, gpad, rims, swap, stay, ddt_mine, ddt_got, ddt_ref,
    part, low_part, near, low_near, far, total, part_b, near_b, sum_b, far_b, total_b,
    l_sem, n_send, n_recv, b_send, b_recv, tap_send, tap_recv,
    xs_sem, xr_sem, gs_sem, gr_sem, es_sem, er_sem, hs_sem, hr_sem, cs_sem, cr_sem,
    ms_sem, mr_sem, r_sem, w_sem, q_send, q_near, q_far, q_near_b, q_far_b
):
    me = lax.axis_index("ctx")
    f = lax.axis_index("fsdp")
    odd = lax.rem(me, 2)
    mate = me + 1 - 2 * odd
    side_ctx = lax.rem(me + n - 1 + 2 * odd, n)
    slot = f // half
    first = 2 * (f - slot * half)
    group = f // 2
    side = f - 2 * group
    share = SIG // n
    per_head = n // HERE
    kept = pl.multiple_of(odd * BLK, BLK)
    given = pl.multiple_of((1 - odd) * BLK, BLK)
    ending = pl.multiple_of((1 - odd) * BLK + BLK - EDGE, EDGE)
    starts = (group, GROUPS + group, f)
    barrier = pltpu.get_barrier_semaphore()

    def fetch(i, src, dst):
        copy = pltpu.make_async_copy(src, dst, l_sem.at[i])
        copy.start()
        return copy

    def third(k):
        return slice(k * STATE, (k + 1) * STATE)

    local = [
        fetch(0, mtaps_hbm, mtaps_ref),
        fetch(1, mbias_hbm, mbias_ref),
        fetch(2, dt_hbm, dt_in),
        fetch(3, alog_hbm, alog_ref),
        fetch(4, dtb_hbm, dtb_ref),
        fetch(5, skip_hbm, skip_ref),
        fetch(6, taps_hbm, taps_ref),
        fetch(7, bias_hbm, bias_ref),
        fetch(8, sig_hbm.at[pl.ds(kept, BLK)], sig_in.at[0:BLK]),
        fetch(9, dout_hbm.at[pl.ds(kept, BLK)], dout_ref.at[0:BLK]),
        fetch(10, sig_hbm.at[pl.ds(ending, EDGE)], tail_own.at[:, 0:SIG]),
    ]
    for k, start in enumerate(starts):
        local.append(
            fetch(
                11 + k,
                map_hbm.at[pl.ds(kept, BLK), columns(start)],
                map_in.at[0:BLK, third(k)],
            )
        )
        local.append(
            fetch(
                14 + k,
                map_hbm.at[pl.ds(ending, EDGE), columns(start)],
                tail_own.at[:, SIG + k * STATE : SIG + (k + 1) * STATE],
            )
        )

    def greet(i, _):
        signal(barrier, ctx=other(me, i, n))
        return 0

    lax.fori_loop(1, n, greet, 0)
    for k in range(2):

        @pl.when(group + k * half != f)
        def _():
            signal(barrier, fsdp=group + k * half)

        @pl.when(first + k != f)
        def _():
            signal(barrier, fsdp=first + k)

    for copy in local:
        copy.wait()
    tap_row[0:KSIZE] = mtaps_ref[...]
    tap_row[KSIZE : KSIZE + 1] = mbias_ref[...]
    tap_row[KSIZE + 1 :] = jnp.zeros((8 - KSIZE - 1, STATE), F32)
    selves = jnp.where(group == f, 1, 0) + jnp.where(group + half == f, 1, 0)
    pl.semaphore_wait(barrier, n - 1 + 4 - 2 * selves)

    for k in range(2):

        @pl.when(first + k != f)
        def _():
            remote(
                tap_row, gtaps_ref.at[slot], tap_send.at[k], tap_recv.at[slot], fsdp=first + k
            ).start()

        @pl.when(group + k * half == f)
        def _():
            gtaps_ref[k] = tap_row[...]

    def to_mate(i, src, dst):
        copy = remote(src, dst, n_send.at[i], n_recv.at[i], ctx=mate)
        copy.start()
        return copy

    def to_side(i, dst_cols):
        copy = remote(
            tail_own.at[:, dst_cols], tail_got.at[:, dst_cols], b_send.at[i], b_recv.at[i],
            ctx=side_ctx,
        )
        copy.start()
        return copy

    dt_copy = to_mate(0, dt_hbm, dt_got)
    tail_copy = to_side(0, slice(0, WIDE))
    map_copies = [
        to_mate(
            1 + k, map_hbm.at[pl.ds(given, BLK), columns(start)], map_in.at[BLK:ROWS, third(k)]
        )
        for k, start in enumerate(starts)
    ]
    dout_copy = to_mate(5, dout_hbm.at[pl.ds(given, BLK)], dout_ref.at[BLK:ROWS])
    sig_copy = to_mate(4, sig_hbm.at[pl.ds(given, BLK)], sig_in.at[BLK:ROWS])

    lane = lax.broadcasted_iota(jnp.int32, (HERE, ROWS), 1)
    row_id = lax.broadcasted_iota(jnp.int32, (ROWS, ROWS), 0)
    col_id = lax.broadcasted_iota(jnp.int32, (ROWS, ROWS), 1)
    lower = ((row_id >= BLK) == (col_id >= BLK)) & (col_id <= row_id)
    lower_f = jnp.where(lower, 1.0, 0.0).astype(F32)
    eye = jnp.where(row_id == col_id, 1.0, 0.0).astype(F32)
    eye8 = eye[:HERE, :HERE]
    ones8 = jnp.ones((HERE, ROWS), F32)
    head3 = lax.broadcasted_iota(jnp.int32, (3 * HERE, 3 * SIG), 0)
    spread3 = jnp.where(
        lax.broadcasted_iota(jnp.int32, (3 * HERE, 3 * SIG), 1) // HDIM == head3, 1.0, 0.0
    ).astype(F32)
    spread1 = spread3[:HERE, :SIG]

    def in_rows(ref):
        return nt(eye8, jnp.broadcast_to(ref[...], (ROWS, HERE)), HIGH)

    def per_row(y):
        return nt(spread1, y, HIGH)

    def turned(x):
        return pltpu.roll(x, BLK, 1)

    def preact(r, rows, cols, taps, bias):
        acc = bias
        for k in range(KSIZE):
            start = EDGE - RIM + k + r
            acc = acc + taps[k : k + 1] * pad[start : start + rows, cols]
        return acc

    def sig_rows(r, count):
        rows = slice(r, r + count)
        for q in range(SIG // STATE):
            cols = third(q)
            v = preact(r, count, cols, taps_ref[:, cols], bias_ref[:, cols])
            s = sigmoid(v)
            slope[rows, cols] = s * (1.0 + v * (1.0 - s))
            signal_ref[rows, cols] = (v * s).astype(BF16)

    pad[EDGE : EDGE + BLK, :SIG] = sig_in[:BLK, :].astype(F32)
    pad[EDGE : EDGE + BLK, SIG:] = map_in[:BLK, :].astype(F32)
    dt_copy.wait()
    own, got = dt_in[...], dt_got[...]
    own = jnp.where(odd == 0, own, turned(own))
    got = jnp.where(odd == 0, turned(got), got)
    logits = jnp.where(lane < BLK, own, got) + in_rows(dtb_ref)
    rate = -jnp.exp(in_rows(alog_ref))
    step = jnp.maximum(logits, 0.0) + log1p_small(jnp.exp(-jnp.abs(logits)))
    ds = nt(step * rate, lower_f, HIGH)
    end_low = jnp.exp(ds[:, BLK - 1 : BLK])
    end_high = jnp.exp(ds[:, ROWS - 1 : ROWS])
    end = jnp.where(lane < BLK, ds[:, BLK - 1 : BLK], ds[:, ROWS - 1 : ROWS])
    to_end = jnp.exp(end - ds)
    col4 = nt(eye, jnp.concatenate([step, to_end, jnp.exp(ds), ds], axis=0), HIGH)
    ds_col = col4[:, 3 * HERE :]
    wide3[...] = nn(col4[:, : 3 * HERE], spread3, HIGH)
    end_low8 = jnp.broadcast_to(end_low, (HERE, STATE))
    end_high8 = jnp.broadcast_to(end_high, (HERE, STATE))
    both_ends = end_low8 * end_high8
    for h in range(HERE):
        es[h] = both_ends[h : h + 1]

    def e_copy(d):
        return remote(es.at[d // per_head], er.at[me], es_sem.at[d], er_sem.at[me], ctx=d)

    def send_ends(i, _):
        e_copy(other(me, i, n)).start()
        return 0

    lax.fori_loop(1, n, send_ends, 0)
    er[me] = es[me // per_head]

    for k in range(2):

        @pl.when(group + k * half != f)
        def _():
            remote(
                tap_row, gtaps_ref.at[k], tap_send.at[k], tap_recv.at[k], fsdp=group + k * half
            ).wait_recv()

        @pl.when(first + k != f)
        def _():
            remote(
                tap_row, gtaps_ref.at[slot], tap_send.at[k], tap_recv.at[slot], fsdp=first + k
            ).wait_send()

    tail_copy.wait()
    for copy in map_copies:
        copy.wait()
    keep = jnp.where(me == 0, 0.0, 1.0).astype(F32)
    before = jnp.where(me == n - 1, tail_own[...].astype(F32), tail_got[...].astype(F32))
    pad[:EDGE] = before * keep
    pad[EDGE + BLK :, SIG:] = map_in[BLK:, :].astype(F32)
    def map_rows(k, out):
        cols = slice(SIG + k * STATE, SIG + (k + 1) * STATE)
        v = preact(0, ROWS, cols, gtaps_ref[k, :KSIZE], gtaps_ref[k, KSIZE : KSIZE + 1])
        out[...] = (v * sigmoid(v)).astype(BF16)

    def mine(d):
        return pl.ds(pl.multiple_of(d * share, share), share)

    def x_copy(d):
        return remote(xs.at[mine(d)], xr.at[me], xs_sem.at[d], xr_sem.at[me], ctx=d)

    def g_copy(d):
        return remote(gs.at[d], gr.at[me], gs_sem.at[d], gr_sem.at[me], ctx=d)

    def h_copy(d):
        return remote(yh.at[d], lh.at[mine(me)], hs_sem.at[d], hr_sem.at[me], ctx=d)

    def c_copy(d):
        return remote(yc.at[d], lc.at[me], cs_sem.at[d], cr_sem.at[me], ctx=d)

    def send_g(i, _):
        g_copy(other(me, i, n)).start()
        return 0

    def send_x(i, _):
        x_copy(other(me, i, n)).start()
        return 0

    map_rows(1, omap_ref)
    dout_copy.wait()
    low, high = slice(0, BLK), slice(BLK, ROWS)
    for q in range(QUADS):
        cols3 = slice(2 * SIG + q * STATE, 2 * SIG + (q + 1) * STATE)
        sgrad_ref[:, third(q)] = (dout_ref[:, third(q)].astype(F32) * wide3[:, cols3]).astype(BF16)
    second_sg[...] = tn(sgrad_ref[high, :], omap_ref[high, :])
    first_sg = tn(sgrad_ref[low, :], omap_ref[low, :])
    for h in range(HERE):
        at = slice(h * HDIM, (h + 1) * HDIM)
        link = first_sg[at, :] + end_low8[h : h + 1] * second_sg[at, :]
        top, rest = pack(link.reshape(per_head, share, STATE))
        gs[h * per_head : (h + 1) * per_head, :share, :] = top
        gs[h * per_head : (h + 1) * per_head, share:, :] = rest
    lax.fori_loop(1, n, send_g, 0)
    gr[me] = gs[me]

    map_rows(0, imap_ref)
    v = preact(0, ROWS, slice(SIG + 2 * STATE, WIDE), mtaps_ref[...], mbias_ref[...])
    s = sigmoid(v)
    slope[:, SIG:] = s * (1.0 + v * (1.0 - s))
    sig_copy.wait()
    pad[EDGE + BLK :, :SIG] = sig_in[BLK:, :].astype(F32)
    sig_rows(0, ROWS)
    for q in range(QUADS):
        cols = third(q)
        cols2 = slice(SIG + q * STATE, SIG + (q + 1) * STATE)
        scaled_b = (signal_ref[:, cols].astype(F32) * wide3[:, cols]).astype(BF16)
        scaled_ref[:, cols] = scaled_b
        weighted_ref[:, cols] = (scaled_b.astype(F32) * wide3[:, cols2]).astype(BF16)
    first_local[...] = tn(weighted_ref[low, :], imap_ref[low, :])
    second_local = tn(weighted_ref[high, :], imap_ref[high, :])
    for h in range(HERE):
        at = slice(h * HDIM, (h + 1) * HDIM)
        xs[at, :] = (end_high8[h : h + 1] * first_local[at, :] + second_local[at, :]).astype(BF16)
    lax.fori_loop(1, n, send_x, 0)
    xr[me] = xs[mine(me)]

    score = nt(omap_ref[...], imap_ref[...])
    lane_row = lax.broadcasted_iota(jnp.int32, (ROWS, STATE), 1)
    grad_score = jnp.zeros((ROWS, ROWS), F32)
    for q in range(HERE // 2):
        cols = third(q)
        d_pair = dout_ref[:, cols].astype(F32)
        d_two = jnp.concatenate(
            [jnp.where(lane_row < HDIM, d_pair, 0.0), jnp.where(lane_row < HDIM, 0.0, d_pair)],
            axis=0,
        ).astype(BF16)
        grad_mix2 = nt(d_two, scaled_ref[:, cols])
        mixes = []
        for k in range(2):
            h = 2 * q + k
            grad_mix = grad_mix2[k * ROWS : (k + 1) * ROWS]
            gap = jnp.minimum(ds_col[:, h : h + 1] - ds[h : h + 1, :], 0.0)
            decay = jnp.where(lower, jnp.exp(gap), 0.0)
            mix = score * decay
            mixes.append(mix.astype(BF16))
            grad_score = grad_score + grad_mix * decay
            product = grad_mix * mix
            drow[h : h + 1, :] = nt(ones8, product, HIGH)[0:1] - jnp.sum(
                product, axis=0, keepdims=True
            )
        intra[:, cols] = tn(jnp.concatenate(mixes, axis=0), d_two)
    grad_score = grad_score.astype(BF16)
    mg[0] = tn(grad_score, omap_ref[...])
    mg[1] = nn(grad_score, imap_ref[...])

    def holder(i):
        return jnp.where(i < n // 2, 2 * i, 2 * (n - 1 - i) + 1)

    zero = jnp.zeros((share, STATE), F32)

    def g_arrived(i, _):
        s = other(me, i, n)
        remote(es.at[s // per_head], er.at[s], es_sem.at[s], er_sem.at[s], ctx=s).wait_recv()
        remote(gs.at[s], gr.at[s], gs_sem.at[s], gr_sem.at[s], ctx=s).wait_recv()
        return 0

    def to_front(i, g):
        at = holder(n - 1 - i)
        top, rest = pack(g[None])
        yc[at, :share, :] = top[0]
        yc[at, share:, :] = rest[0]
        got = gr[at]
        return er[at] * g + unpack(got[:share], got[share:])

    def send_c(i, _):
        c_copy(other(me, i, n)).start()
        return 0

    def x_arrived(i, _):
        s = other(me, i, n)
        remote(xs.at[mine(s)], xr.at[s], xs_sem.at[s], xr_sem.at[s], ctx=s).wait_recv()
        return 0

    def to_back(i, h):
        at = holder(i)
        yh[at] = h.astype(BF16)
        return er[at] * h + xr[at].astype(F32)

    def send_h(i, _):
        h_copy(other(me, i, n)).start()
        return 0

    lax.fori_loop(1, n, g_arrived, 0)
    lax.fori_loop(0, n, to_front, zero)
    lax.fori_loop(1, n, send_c, 0)
    lax.fori_loop(1, n, x_arrived, 0)
    lax.fori_loop(0, n, to_back, zero)
    lax.fori_loop(1, n, send_h, 0)
    lh[mine(me)] = yh[me]
    lc[me] = yc[me]
    step_w = wide3[:, :SIG]
    end_w = wide3[:, SIG : 2 * SIG]
    exp_w = wide3[:, 2 * SIG :]
    d_f = dout_ref[...].astype(F32)
    signal_f = signal_ref[...].astype(F32)
    skip_w = nn(jnp.broadcast_to(skip_ref[...], (HERE, HERE)), spread1, HIGH)[0:1]
    part[(KSIZE + 1) * QUADS :] = jnp.zeros((SUMS - (KSIZE + 1) * QUADS, STATE), F32)

    def small(at, row):
        at = KSIZE + 1 + at
        part_b[at : at + 1] = jnp.concatenate([row, jnp.zeros((1, STATE - HERE), F32)], axis=1)

    small(2, nt(ones8, per_row(d_f * signal_f), HIGH)[0:1])

    def m_copy(k):
        return remote(
            mg.at[k], mgot.at[side], ms_sem.at[k], mr_sem.at[side], fsdp=group + k * half
        )

    def to_owner(k):
        @pl.when(group + k * half != f)
        def _():
            m_copy(k).start()

        @pl.when(group + k * half == f)
        def _():
            mgot[side] = mg[k]

    def c_in(i, _):
        d = other(me, i, n)
        g_copy(d).wait_send()
        e_copy(d).wait_send()
        remote(yc.at[d], lc.at[d], cs_sem.at[d], cr_sem.at[d], ctx=d).wait_recv()
        return 0

    lax.fori_loop(1, n, c_in, 0)
    for h in range(HERE):
        at = slice(h * HDIM, (h + 1) * HDIM)
        got = lc[h * per_head : (h + 1) * per_head]
        state = unpack(got[:, :share], got[:, share:]).reshape(HDIM, STATE)
        lk[3, at, :] = state.astype(BF16)
        lk[2, at, :] = (second_sg[at, :] + end_high8[h : h + 1] * state).astype(BF16)
    for b, rows in enumerate((low, high)):
        mg[0, rows, :] = mg[0, rows, :] + nn(weighted_ref[rows, :], lk[2 + b])
    to_owner(0)
    for b, rows in enumerate((low, high)):
        gw[rows, :] = nt(imap_ref[rows, :], lk[2 + b])
    gw_v = gw[...]
    back_row = per_row(gw_v * scaled_ref[...].astype(F32)) * to_end
    back_low = jnp.sum(jnp.where(lane < BLK, back_row, 0.0), axis=1, keepdims=True)
    back_high = jnp.sum(jnp.where(lane < BLK, 0.0, back_row), axis=1, keepdims=True)
    grad_scaled = gw_v * end_w + intra[...]
    own_step = per_row(grad_scaled * signal_f)
    gpad[:ROWS, :SIG] = (skip_w * d_f + grad_scaled * step_w) * slope[:, :SIG]

    def sums(cols, source, into, every, at):
        g = gpad[:ROWS, cols]
        for k in range(KSIZE):
            start = EDGE - RIM + k
            row = k * every + at
            into[row : row + 1] = jnp.sum(
                g * pad[start : start + ROWS, source], axis=0, keepdims=True
            )
        row = KSIZE * every + at
        into[row : row + 1] = jnp.sum(g, axis=0, keepdims=True)

    earlier = jnp.where(
        odd == 0, lax.rem(me + n - 2, n), jnp.where(me == n - 1, n - 2, lax.rem(me + 2, n))
    )
    earlier = jnp.where(me == 0, 1, earlier)

    def rim(i, cols):
        copy = remote(
            gpad.at[0:RIMS, cols], rims.at[:, cols], r_sem.at[2 * i], r_sem.at[2 * i + 1],
            ctx=earlier,
        )
        copy.start()
        return copy

    sig_cols, map_cols = slice(0, SIG), slice(SIG, OWN)
    sig_rim = rim(0, sig_cols)
    for q in range(QUADS):
        sums(third(q), third(q), part, QUADS, q)

    planes = n // 2
    y = me // planes
    z = me - y * planes
    z_high = z // 4
    z_low = z - 4 * z_high
    here = 4 * y + z_low
    sent = []

    def to_near(src, dst, at, recv_sem):
        for k in range(1, 8):
            s = lax.rem(here + k, 8)
            d = s // 4 * planes + z_high * 4 + s - s // 4 * 4
            copy = remote(src, dst.at[here], q_send.at[at + k], recv_sem.at[here], ctx=d)
            copy.start()
            sent.append(copy)
        dst[here] = src[...]

    def near_in(src, dst, recv_sem):
        for k in range(1, 8):
            s = lax.rem(here + k, 8)
            remote(src, dst.at[s], q_send.at[k], recv_sem.at[s], ctx=mate).wait_recv()

    def to_far(src, dst, at, recv_sem):
        for k in range(1, 4):
            s = lax.rem(z_high + k, 4)
            d = y * planes + 4 * s + z_low
            copy = remote(src, dst.at[z_high], q_send.at[at + k], recv_sem.at[z_high], ctx=d)
            copy.start()
            sent.append(copy)
        dst[z_high] = src[...]

    def far_in(src, dst, recv_sem):
        for k in range(1, 4):
            s = lax.rem(z_high + k, 4)
            remote(src, dst.at[s], q_send.at[k], recv_sem.at[s], ctx=mate).wait_recv()

    low_part[...] = part[...].astype(BF16)
    to_near(low_part, near, 0, q_near)

    def raw(r, out, taps, cols):
        acc = taps[RIM : RIM + 1] * gpad[r : r + BLK, cols]
        for k in range(RIM):
            acc = acc + taps[k : k + 1] * gpad[r + RIM - k : r + RIM - k + BLK, cols]
        out[:, cols] = acc

    def transposed(i, rim_copy, taps, cols, out):
        rim_copy.wait()
        gpad[ROWS:, cols] = jnp.where(me == 1, 0.0, rims[:, cols])
        raw(BLK, swap, taps, cols)
        away = remote(
            swap.at[:, cols], out.at[pl.ds(kept, BLK)], w_sem.at[2 * i], w_sem.at[2 * i + 1],
            ctx=mate,
        )
        away.start()
        raw(0, stay, taps, cols)
        return away, fetch(i, stay.at[:, cols], out.at[pl.ds(kept, BLK)])

    def h_in(i, _):
        d = other(me, i, n)
        x_copy(d).wait_send()
        remote(yh.at[d], lh.at[mine(d)], hs_sem.at[d], hr_sem.at[d], ctx=d).wait_recv()
        return 0

    lax.fori_loop(1, n, h_in, 0)
    lk[0] = lh[...]
    for h in range(HERE):
        at = slice(h * HDIM, (h + 1) * HDIM)
        lk[1, at, :] = (end_low8[h : h + 1] * lh[at, :].astype(F32) + first_local[at, :]).astype(
            BF16
        )
    for b, rows in enumerate((low, high)):
        mg[1, rows, :] = mg[1, rows, :] + nn(sgrad_ref[rows, :], lk[b])
    to_owner(1)
    end_terms = []
    for b, rows in enumerate((low, high)):
        oh[rows, :] = nt(omap_ref[rows, :], lk[b])
        both = lk[b].astype(F32) * lk[2 + b].astype(F32)
        both = jnp.sum(both.reshape(HERE, HDIM, STATE), axis=1)
        end_terms.append(jnp.sum(both, axis=1, keepdims=True))
    grad_sum = per_row(d_f * exp_w * oh[...]) - back_row + drow[...]
    last_low = back_low + end_low * end_terms[0]
    last_high = back_high + end_high * end_terms[1]
    grad_sum = grad_sum + jnp.where(
        lane == BLK - 1, last_low, jnp.where(lane == ROWS - 1, last_high, 0.0)
    )
    grad_log = nn(grad_sum, lower_f, HIGH)
    grad_step = grad_log * rate + own_step
    grad_dt = grad_step * sigmoid(logits)
    ddt_mine[...] = grad_dt
    ddt_copy = remote(ddt_mine, ddt_got, w_sem.at[0], w_sem.at[1], ctx=mate)
    ddt_copy.start()
    small(0, nt(ones8, grad_log * step, HIGH)[0:1] * (-jnp.exp(alog_ref[...])))
    small(1, nt(ones8, grad_dt, HIGH)[0:1])
    near_in(low_part, near, q_near)
    low_near[...] = jnp.sum(near[...].astype(F32), axis=0).astype(BF16)
    to_far(low_near, far, 7, q_far)

    for k in range(2):

        @pl.when(first + k != f)
        def _():
            remote(
                mg.at[k], mgot.at[k], ms_sem.at[k], mr_sem.at[k], fsdp=first + k
            ).wait_recv()

    gpad[:ROWS, SIG:] = (mgot[0] + mgot[1]) * slope[:, SIG:]
    map_rim = rim(1, map_cols)
    sums(map_cols, slice(SIG + 2 * STATE, WIDE), part_b, 1, 0)
    to_near(part_b, near_b, 10, q_near_b)
    sig_out = transposed(1, sig_rim, taps_ref, sig_cols, dsig_hbm)
    map_out = transposed(2, map_rim, mtaps_ref, map_cols, dmap_hbm)
    near_in(part_b, near_b, q_near_b)
    sum_b[...] = jnp.sum(near_b[...], axis=0)
    to_far(sum_b, far_b, 17, q_far_b)
    ddt_copy.wait()
    own, got = ddt_mine[...], ddt_got[...]
    ddt_low = jnp.where(odd == 0, own, turned(got))
    ddt_high = jnp.where(odd == 0, got, turned(own))
    ddt_ref[...] = jnp.where(lane < BLK, ddt_low, ddt_high)
    ddt_out = fetch(3, ddt_ref, ddt_hbm)
    far_in(low_near, far, q_far)
    total[...] = jnp.sum(far[...].astype(F32), axis=0)
    sums_out = fetch(4, total, sums_hbm)

    def done(i, _):
        d = other(me, i, n)
        h_copy(d).wait_send()
        c_copy(d).wait_send()
        return 0

    lax.fori_loop(1, n, done, 0)
    for k in range(2):

        @pl.when(group + k * half != f)
        def _():
            m_copy(k).wait_send()

    far_in(sum_b, far_b, q_far_b)
    total_b[...] = jnp.sum(far_b[...], axis=0)
    small_out = fetch(5, total_b, small_hbm)
    for copy in sent:
        copy.wait_send()
    for copy in sig_out + map_out + (ddt_out, sums_out, small_out):
        copy.wait()


def main(*operands):
    n = lax.axis_size("ctx")
    half = lax.axis_size("fsdp") // 2
    share = SIG // n
    dma = pltpu.SemaphoreType.DMA
    vm = pltpu.VMEM
    return pl.pallas_call(
        functools.partial(main_kernel, n, half),
        out_shape=(
            jax.ShapeDtypeStruct((ROWS, SIG), F32),
            jax.ShapeDtypeStruct((ROWS, STATE), F32),
            jax.ShapeDtypeStruct((SUMS, STATE), F32),
            jax.ShapeDtypeStruct((8, STATE), F32),
            jax.ShapeDtypeStruct((HERE, ROWS), F32),
        ),
        in_specs=[pl.BlockSpec(memory_space=pl.ANY)] * len(operands),
        out_specs=(HBM,) * 5,
        scratch_shapes=[
            vm((ROWS, SIG), BF16),
            vm((ROWS, 3 * STATE), BF16),
            vm((ROWS, SIG), BF16),
            vm((HERE, ROWS), F32),
            vm((HERE, ROWS), F32),
            vm((KSIZE, SIG), F32),
            vm((1, SIG), F32),
            vm((KSIZE, STATE), F32),
            vm((1, STATE), F32),
            vm((1, HERE), F32),
            vm((1, HERE), F32),
            vm((1, HERE), F32),
            vm((EDGE, WIDE), BF16),
            vm((EDGE, WIDE), BF16),
            vm((8, STATE), F32),
            vm((2, 8, STATE), F32),
            vm((EDGE + ROWS, WIDE), F32),
            vm((ROWS, OWN), F32),
            vm((ROWS, SIG), BF16),
            vm((ROWS, SIG), BF16),
            vm((ROWS, SIG), BF16),
            vm((ROWS, SIG), BF16),
            vm((ROWS, STATE), BF16),
            vm((ROWS, STATE), BF16),
            vm((ROWS, 3 * SIG), F32),
            vm((ROWS, SIG), F32),
            vm((ROWS, SIG), F32),
            vm((ROWS, SIG), F32),
            vm((HERE, ROWS), F32),
            vm((SIG, STATE), BF16),
            vm((n, 3 * share // 2, STATE), BF16),
            vm((HERE, 1, STATE), F32),
            vm((n, share, STATE), BF16),
            vm((n, 3 * share // 2, STATE), BF16),
            vm((n, 1, STATE), F32),
            vm((n, share, STATE), BF16),
            vm((n, 3 * share // 2, STATE), BF16),
            vm((SIG, STATE), BF16),
            vm((n, 3 * share // 2, STATE), BF16),
            vm((SIG, STATE), F32),
            vm((SIG, STATE), F32),
            vm((4, SIG, STATE), BF16),
            vm((2, ROWS, STATE), F32),
            vm((2, ROWS, STATE), F32),
            vm((ROWS + RIMS, OWN), F32),
            vm((RIMS, OWN), F32),
            vm((BLK, OWN), F32),
            vm((BLK, OWN), F32),
            vm((HERE, ROWS), F32),
            vm((HERE, ROWS), F32),
            vm((HERE, ROWS), F32),
            vm((SUMS, STATE), F32),
            vm((SUMS, STATE), BF16),
            vm((8, SUMS, STATE), BF16),
            vm((SUMS, STATE), BF16),
            vm((4, SUMS, STATE), BF16),
            vm((SUMS, STATE), F32),
            vm((8, STATE), F32),
            vm((8, 8, STATE), F32),
            vm((8, STATE), F32),
            vm((4, 8, STATE), F32),
            vm((8, STATE), F32),
        ]
        + [dma((17,)), dma((6,)), dma((6,)), dma((1,)), dma((1,)), dma((2,)), dma((2,))]
        + [dma((n,))] * 10
        + [dma((2,)), dma((2,)), dma((4,)), dma((6,)), dma((21,)), dma((8,)), dma((4,)), dma((8,)), dma((4,))],
        compiler_params=pltpu.CompilerParams(
            collective_id=0, has_side_effects=True, vmem_limit_bytes=56 * 1024 * 1024
        ),
        name="main",
    )(*operands)


def last_kernel(
    scale, dsig_in, dmap_in, sums_in, small_in, ddt_in,
    dsig, dmap, ddt, dtaps, dmtaps, dbias, dmbias, dalog, ddtb, dskip
):
    dsig[...] = dsig_in[...]
    dmap[...] = dmap_in[...]
    ddt[...] = ddt_in[...]
    for k in range(KSIZE + 1):
        for q in range(QUADS):
            at = k * QUADS + q
            cols = slice(q * STATE, (q + 1) * STATE)
            row = sums_in[at : at + 1] * scale
            if k < KSIZE:
                dtaps[k : k + 1, cols] = row
            else:
                dbias[:, cols] = row
    dmtaps[...] = small_in[:KSIZE] * scale
    dmbias[...] = small_in[KSIZE : KSIZE + 1] * scale
    for k, out in enumerate((dalog, ddtb, dskip)):
        at = KSIZE + 1 + k
        out[...] = small_in[at : at + 1, :HERE] * scale


def last(*operands):
    scale = 1.0 / math.sqrt(float(lax.axis_size("ctx") * ROWS))
    shapes = (
        (ROWS, SIG), (ROWS, STATE), (HERE, ROWS), (KSIZE, SIG), (KSIZE, STATE),
        (1, SIG), (1, STATE), (1, HERE), (1, HERE), (1, HERE),
    )
    return pl.pallas_call(
        functools.partial(last_kernel, scale),
        out_shape=tuple(jax.ShapeDtypeStruct(s, F32) for s in shapes),
        in_specs=[VM] * 5,
        out_specs=(VM,) * len(shapes),
        compiler_params=pltpu.CompilerParams(vmem_limit_bytes=8 * 1024 * 1024),
        name="last",
    )(*operands)


def shards(
    sig_raw,
    map_raw,
    step_size_logits,
    d_out,
    sig_taps,
    map_taps,
    sig_bias,
    map_bias,
    a_log,
    dt_bias,
    skip_gain,
):
    found = main(
        sig_raw, map_raw, step_size_logits.T, d_out, sig_taps, sig_bias[None, :], map_taps,
        map_bias[None, :], a_log[None, :], dt_bias[None, :], skip_gain[None, :],
    )
    out = last(*found)
    return out[:2] + (out[2].T,) + out[3:5] + tuple(a.reshape(-1) for a in out[5:])


def solution(mesh):
    return jax.shard_map(
        shards,
        mesh=mesh,
        in_specs=(
            P("ctx", "fsdp"),
            P("ctx", None),
            P("ctx", "fsdp"),
            P("ctx", "fsdp"),
            P(None, "fsdp"),
            P(None, "fsdp"),
            P("fsdp"),
            P("fsdp"),
            P("fsdp"),
            P("fsdp"),
            P("fsdp"),
        ),
        out_specs=(
            P("ctx", "fsdp"),
            P("ctx", "fsdp"),
            P("ctx", "fsdp"),
            P(None, "fsdp"),
            P(None, "fsdp"),
            P("fsdp"),
            P("fsdp"),
            P("fsdp"),
            P("fsdp"),
            P("fsdp"),
        ),
        check_vma=False,
    )
```

```python
import functools
import math

import jax
import jax.numpy as jnp
from jax import lax
from jax.experimental import pallas as pl
from jax.experimental.pallas import tpu as pltpu
from jax.sharding import PartitionSpec as P

HEADS = 128
HDIM = 64
STATE = 128
GROUPS = 8
HERE = 8
KSIZE = 4
RIM = KSIZE - 1
BLK = 64
ROWS = 2 * BLK
SIG = HERE * HDIM
WIDE = SIG + 3 * STATE
OWN = SIG + STATE
EDGE = 16
RIMS = 8
QUADS = SIG // STATE
SUMS = 24
FINE = 10
MESH = pl.DeviceIdType.MESH
VM = pl.BlockSpec(memory_space=pltpu.VMEM)
HBM = pl.BlockSpec(memory_space=pltpu.HBM)
HIGH = lax.Precision.HIGHEST
F32 = jnp.float32
BF16 = jnp.bfloat16


def signal(sem, **where):
    pl.semaphore_signal(sem, inc=1, device_id=where, device_id_type=MESH)


def remote(src, dst, send_sem, recv_sem, **where):
    return pltpu.make_async_remote_copy(
        src_ref=src,
        dst_ref=dst,
        send_sem=send_sem,
        recv_sem=recv_sem,
        device_id=where,
        device_id_type=MESH,
    )


def other(me, i, n):
    off = jnp.where(lax.rem(i, 2) == 1, (i + 1) // 2, n - i // 2)
    return lax.rem(me + off, n)


def columns(start):
    return pl.ds(pl.multiple_of(start * STATE, STATE), STATE)


def nn(a, b, precision=None):
    return lax.dot_general(
        a, b, (((1,), (0,)), ((), ())), precision=precision, preferred_element_type=F32
    )


def nt(a, b, precision=None):
    return lax.dot_general(
        a, b, (((1,), (1,)), ((), ())), precision=precision, preferred_element_type=F32
    )


def tn(a, b):
    return lax.dot_general(a, b, (((0,), (0,)), ((), ())), preferred_element_type=F32)


def sigmoid(v):
    return 1.0 / (1.0 + jnp.exp(-v))


def log1p_small(e):
    series = e * (
        1.0 + e * (-1.0 / 2 + e * (1.0 / 3 + e * (-1.0 / 4 + e * (1.0 / 5 + e * (-1.0 / 6)))))
    )
    return jnp.where(e < 0.03, series, jnp.log(1.0 + e))


def pack(v):
    n, rows, _ = v.shape
    high = v.astype(BF16)
    value = high.astype(F32)
    tiny = jnp.abs(value) < 1e-30
    ratio = jnp.where(tiny, 0.0, (v - value) / jnp.where(tiny, 1.0, value))
    steps = jnp.clip(jnp.round(ratio * (256.0 * FINE)), -FINE, FINE)
    both = steps[:, : rows // 2] * (2.0 * FINE + 1.0) + steps[:, rows // 2 :]
    return high, both.astype(BF16)


def unpack(high, both):
    value = high.astype(F32)
    both = both.astype(F32)
    first = jnp.floor((both + (FINE + 0.5)) * (1.0 / (2.0 * FINE + 1.0)))
    second = both - first * (2.0 * FINE + 1.0)
    steps = jnp.concatenate([first, second], axis=-2)
    return value + value * steps * (1.0 / (256.0 * FINE))


def main_kernel(
    n, half, sig_hbm, map_hbm, dt_hbm, dout_hbm, taps_hbm, bias_hbm, mtaps_hbm, mbias_hbm,
    alog_hbm, dtb_hbm, skip_hbm,
    dsig_hbm, dmap_hbm, sums_hbm, small_hbm, ddt_hbm,
    sig_in, map_in, dout_ref, dt_in, dt_got, taps_ref, bias_ref, mtaps_ref, mbias_ref,
    alog_ref, dtb_ref, skip_ref, tail_own, tail_got, tap_row, gtaps_ref,
    pad, slope, signal_ref, scaled_ref, weighted_ref, sgrad_ref, imap_ref, omap_ref, wide3, intra,
    oh, gw, drow, m_out, xs, gs, es, xr, gr, er, yh, yc, lh, lc, first_local, second_sg, lk,
    mg, mgot, gpad, rims, swap, stay, ddt_mine, ddt_got, ddt_ref,
    part, low_part, near, low_near, far, total, part_b, near_b, sum_b, far_b, total_b,
    l_sem, n_send, n_recv, b_send, b_recv, tap_send, tap_recv,
    xs_sem, xr_sem, gs_sem, gr_sem, es_sem, er_sem, hs_sem, hr_sem, cs_sem, cr_sem,
    ms_sem, mr_sem, r_sem, w_sem, q_send, q_near, q_far, q_near_b, q_far_b
):
    me = lax.axis_index("ctx")
    f = lax.axis_index("fsdp")
    odd = lax.rem(me, 2)
    mate = me + 1 - 2 * odd
    side_ctx = lax.rem(me + n - 1 + 2 * odd, n)
    slot = f // half
    first = 2 * (f - slot * half)
    group = f // 2
    side = f - 2 * group
    share = SIG // n
    per_head = n // HERE
    kept = pl.multiple_of(odd * BLK, BLK)
    given = pl.multiple_of((1 - odd) * BLK, BLK)
    ending = pl.multiple_of((1 - odd) * BLK + BLK - EDGE, EDGE)
    starts = (group, GROUPS + group, f)
    barrier = pltpu.get_barrier_semaphore()

    def greet(i, _):
        signal(barrier, ctx=other(me, i, n))
        return 0

    lax.fori_loop(1, n, greet, 0)
    for k in range(2):

        @pl.when(group + k * half != f)
        def _():
            signal(barrier, fsdp=group + k * half)

        @pl.when(first + k != f)
        def _():
            signal(barrier, fsdp=first + k)

    def fetch(i, src, dst):
        copy = pltpu.make_async_copy(src, dst, l_sem.at[i])
        copy.start()
        return copy

    def third(k):
        return slice(k * STATE, (k + 1) * STATE)

    local = [
        fetch(0, mtaps_hbm, mtaps_ref),
        fetch(1, mbias_hbm, mbias_ref),
        fetch(2, dt_hbm, dt_in),
        fetch(3, alog_hbm, alog_ref),
        fetch(4, dtb_hbm, dtb_ref),
        fetch(5, skip_hbm, skip_ref),
        fetch(6, taps_hbm, taps_ref),
        fetch(7, bias_hbm, bias_ref),
        fetch(8, sig_hbm.at[pl.ds(kept, BLK)], sig_in.at[0:BLK]),
        fetch(9, dout_hbm.at[pl.ds(kept, BLK)], dout_ref.at[0:BLK]),
        fetch(10, sig_hbm.at[pl.ds(ending, EDGE)], tail_own.at[:, 0:SIG]),
    ]
    for k, start in enumerate(starts):
        local.append(
            fetch(
                11 + k,
                map_hbm.at[pl.ds(kept, BLK), columns(start)],
                map_in.at[0:BLK, third(k)],
            )
        )
        local.append(
            fetch(
                14 + k,
                map_hbm.at[pl.ds(ending, EDGE), columns(start)],
                tail_own.at[:, SIG + k * STATE : SIG + (k + 1) * STATE],
            )
        )

    for copy in local:
        copy.wait()
    tap_row[0:KSIZE] = mtaps_ref[...]
    tap_row[KSIZE : KSIZE + 1] = mbias_ref[...]
    tap_row[KSIZE + 1 :] = jnp.zeros((8 - KSIZE - 1, STATE), F32)
    selves = jnp.where(group == f, 1, 0) + jnp.where(group + half == f, 1, 0)
    pl.semaphore_wait(barrier, n - 1 + 4 - 2 * selves)

    for k in range(2):

        @pl.when(first + k != f)
        def _():
            remote(
                tap_row, gtaps_ref.at[slot], tap_send.at[k], tap_recv.at[slot], fsdp=first + k
            ).start()

        @pl.when(group + k * half == f)
        def _():
            gtaps_ref[k] = tap_row[...]

    def to_mate(i, src, dst):
        copy = remote(src, dst, n_send.at[i], n_recv.at[i], ctx=mate)
        copy.start()
        return copy

    def to_side(i, dst_cols):
        copy = remote(
            tail_own.at[:, dst_cols], tail_got.at[:, dst_cols], b_send.at[i], b_recv.at[i],
            ctx=side_ctx,
        )
        copy.start()
        return copy

    def map_copy(k):
        return to_mate(
            1 + k, map_hbm.at[pl.ds(given, BLK), columns(starts[k])], map_in.at[BLK:ROWS, third(k)]
        )

    dt_copy = to_mate(0, dt_hbm, dt_got)
    out_cols = slice(SIG + STATE, SIG + 2 * STATE)
    out_tail = to_side(0, out_cols)
    out_copy = map_copy(1)
    dout_copy = to_mate(5, dout_hbm.at[pl.ds(given, BLK)], dout_ref.at[BLK:ROWS])
    tails = [to_side(1, slice(0, SIG + STATE)), to_side(2, slice(SIG + 2 * STATE, WIDE))]
    map_copies = [map_copy(0), map_copy(2)]
    sig_copy = to_mate(4, sig_hbm.at[pl.ds(given, BLK)], sig_in.at[BLK:ROWS])

    lane = lax.broadcasted_iota(jnp.int32, (HERE, ROWS), 1)
    row_id = lax.broadcasted_iota(jnp.int32, (ROWS, ROWS), 0)
    col_id = lax.broadcasted_iota(jnp.int32, (ROWS, ROWS), 1)
    lower = ((row_id >= BLK) == (col_id >= BLK)) & (col_id <= row_id)
    lower_f = jnp.where(lower, 1.0, 0.0).astype(F32)
    eye = jnp.where(row_id == col_id, 1.0, 0.0).astype(F32)
    eye8 = eye[:HERE, :HERE]
    ones8 = jnp.ones((HERE, ROWS), F32)
    head3 = lax.broadcasted_iota(jnp.int32, (3 * HERE, 3 * SIG), 0)
    spread3 = jnp.where(
        lax.broadcasted_iota(jnp.int32, (3 * HERE, 3 * SIG), 1) // HDIM == head3, 1.0, 0.0
    ).astype(F32)
    spread1 = spread3[:HERE, :SIG]

    def in_rows(ref):
        return nt(eye8, jnp.broadcast_to(ref[...], (ROWS, HERE)), HIGH)

    def per_row(y):
        return nt(spread1, y, HIGH)

    def turned(x):
        return pltpu.roll(x, BLK, 1)

    def preact(r, rows, cols, taps, bias):
        acc = bias
        for k in range(KSIZE):
            start = EDGE - RIM + k + r
            acc = acc + taps[k : k + 1] * pad[start : start + rows, cols]
        return acc

    def sig_rows(r, count):
        rows = slice(r, r + count)
        for q in range(SIG // STATE):
            cols = third(q)
            v = preact(r, count, cols, taps_ref[:, cols], bias_ref[:, cols])
            s = sigmoid(v)
            slope[rows, cols] = s * (1.0 + v * (1.0 - s))
            signal_ref[rows, cols] = (v * s).astype(BF16)

    pad[EDGE : EDGE + BLK, :SIG] = sig_in[:BLK, :].astype(F32)
    pad[EDGE : EDGE + BLK, SIG:] = map_in[:BLK, :].astype(F32)
    keep = jnp.where(me == 0, 0.0, 1.0).astype(F32)

    def before(cols):
        mine_then = tail_own[:, cols].astype(F32)
        pad[:EDGE, cols] = keep * jnp.where(me == n - 1, mine_then, tail_got[:, cols].astype(F32))

    dt_copy.wait()
    own, got = dt_in[...], dt_got[...]
    own = jnp.where(odd == 0, own, turned(own))
    got = jnp.where(odd == 0, turned(got), got)
    logits = jnp.where(lane < BLK, own, got) + in_rows(dtb_ref)
    rate = -jnp.exp(in_rows(alog_ref))
    step = jnp.maximum(logits, 0.0) + log1p_small(jnp.exp(-jnp.abs(logits)))
    ds = nt(step * rate, lower_f, HIGH)
    end_low = jnp.exp(ds[:, BLK - 1 : BLK])
    end_high = jnp.exp(ds[:, ROWS - 1 : ROWS])
    end = jnp.where(lane < BLK, ds[:, BLK - 1 : BLK], ds[:, ROWS - 1 : ROWS])
    to_end = jnp.exp(end - ds)
    col4 = nt(eye, jnp.concatenate([step, to_end, jnp.exp(ds), ds], axis=0), HIGH)
    ds_col = col4[:, 3 * HERE :]
    wide3[...] = nn(col4[:, : 3 * HERE], spread3, HIGH)
    end_low8 = jnp.broadcast_to(end_low, (HERE, STATE))
    end_high8 = jnp.broadcast_to(end_high, (HERE, STATE))
    both_ends = end_low8 * end_high8
    for h in range(HERE):
        es[h] = both_ends[h : h + 1]

    def e_copy(d):
        return remote(es.at[d // per_head], er.at[me], es_sem.at[d], er_sem.at[me], ctx=d)

    def send_ends(i, _):
        e_copy(other(me, i, n)).start()
        return 0

    lax.fori_loop(1, n, send_ends, 0)
    er[me] = es[me // per_head]

    for k in range(2):

        @pl.when(group + k * half != f)
        def _():
            remote(
                tap_row, gtaps_ref.at[k], tap_send.at[k], tap_recv.at[k], fsdp=group + k * half
            ).wait_recv()

        @pl.when(first + k != f)
        def _():
            remote(
                tap_row, gtaps_ref.at[slot], tap_send.at[k], tap_recv.at[slot], fsdp=first + k
            ).wait_send()

    out_tail.wait()
    out_copy.wait()
    before(out_cols)
    pad[EDGE + BLK :, out_cols] = map_in[BLK:, third(1)].astype(F32)
    def map_rows(k, out):
        cols = slice(SIG + k * STATE, SIG + (k + 1) * STATE)
        v = preact(0, ROWS, cols, gtaps_ref[k, :KSIZE], gtaps_ref[k, KSIZE : KSIZE + 1])
        out[...] = (v * sigmoid(v)).astype(BF16)

    def mine(d):
        return pl.ds(pl.multiple_of(d * share, share), share)

    def x_copy(d):
        return remote(xs.at[mine(d)], xr.at[me], xs_sem.at[d], xr_sem.at[me], ctx=d)

    def g_copy(d):
        return remote(gs.at[d], gr.at[me], gs_sem.at[d], gr_sem.at[me], ctx=d)

    def h_copy(d):
        return remote(yh.at[d], lh.at[mine(me)], hs_sem.at[d], hr_sem.at[me], ctx=d)

    def c_copy(d):
        return remote(yc.at[d], lc.at[me], cs_sem.at[d], cr_sem.at[me], ctx=d)

    def send_g(i, _):
        g_copy(other(me, i, n)).start()
        return 0

    def send_x(i, _):
        x_copy(other(me, i, n)).start()
        return 0

    map_rows(1, omap_ref)
    dout_copy.wait()
    low, high = slice(0, BLK), slice(BLK, ROWS)
    for q in range(QUADS):
        cols3 = slice(2 * SIG + q * STATE, 2 * SIG + (q + 1) * STATE)
        sgrad_ref[:, third(q)] = (dout_ref[:, third(q)].astype(F32) * wide3[:, cols3]).astype(BF16)
    second_sg[...] = tn(sgrad_ref[high, :], omap_ref[high, :])
    first_sg = tn(sgrad_ref[low, :], omap_ref[low, :])
    for h in range(HERE):
        at = slice(h * HDIM, (h + 1) * HDIM)
        link = first_sg[at, :] + end_low8[h : h + 1] * second_sg[at, :]
        top, rest = pack(link.reshape(per_head, share, STATE))
        gs[h * per_head : (h + 1) * per_head, :share, :] = top
        gs[h * per_head : (h + 1) * per_head, share:, :] = rest
    lax.fori_loop(1, n, send_g, 0)
    gr[me] = gs[me]

    for copy in tails + map_copies:
        copy.wait()
    for cols in (slice(0, SIG + STATE), slice(SIG + 2 * STATE, WIDE)):
        before(cols)
    pad[EDGE + BLK :, SIG : SIG + STATE] = map_in[BLK:, third(0)].astype(F32)
    pad[EDGE + BLK :, SIG + 2 * STATE :] = map_in[BLK:, third(2)].astype(F32)
    map_rows(0, imap_ref)
    v = preact(0, ROWS, slice(SIG + 2 * STATE, WIDE), mtaps_ref[...], mbias_ref[...])
    s = sigmoid(v)
    slope[:, SIG:] = s * (1.0 + v * (1.0 - s))
    sig_copy.wait()
    pad[EDGE + BLK :, :SIG] = sig_in[BLK:, :].astype(F32)
    sig_rows(0, ROWS)
    for q in range(QUADS):
        cols = third(q)
        cols2 = slice(SIG + q * STATE, SIG + (q + 1) * STATE)
        scaled_b = (signal_ref[:, cols].astype(F32) * wide3[:, cols]).astype(BF16)
        scaled_ref[:, cols] = scaled_b
        weighted_ref[:, cols] = (scaled_b.astype(F32) * wide3[:, cols2]).astype(BF16)
    first_local[...] = tn(weighted_ref[low, :], imap_ref[low, :])
    second_local = tn(weighted_ref[high, :], imap_ref[high, :])
    for h in range(HERE):
        at = slice(h * HDIM, (h + 1) * HDIM)
        xs[at, :] = (end_high8[h : h + 1] * first_local[at, :] + second_local[at, :]).astype(BF16)
    lax.fori_loop(1, n, send_x, 0)
    xr[me] = xs[mine(me)]

    score = nt(omap_ref[...], imap_ref[...])
    lane_row = lax.broadcasted_iota(jnp.int32, (ROWS, STATE), 1)
    grad_score = jnp.zeros((ROWS, ROWS), F32)
    for q in range(HERE // 2):
        cols = third(q)
        d_pair = dout_ref[:, cols].astype(F32)
        d_two = jnp.concatenate(
            [jnp.where(lane_row < HDIM, d_pair, 0.0), jnp.where(lane_row < HDIM, 0.0, d_pair)],
            axis=0,
        ).astype(BF16)
        grad_mix2 = nt(d_two, scaled_ref[:, cols])
        mixes = []
        for k in range(2):
            h = 2 * q + k
            grad_mix = grad_mix2[k * ROWS : (k + 1) * ROWS]
            gap = jnp.minimum(ds_col[:, h : h + 1] - ds[h : h + 1, :], 0.0)
            decay = jnp.where(lower, jnp.exp(gap), 0.0)
            mix = score * decay
            mixes.append(mix.astype(BF16))
            grad_score = grad_score + grad_mix * decay
            product = grad_mix * mix
            drow[h : h + 1, :] = nt(ones8, product, HIGH)[0:1] - jnp.sum(
                product, axis=0, keepdims=True
            )
        intra[:, cols] = tn(jnp.concatenate(mixes, axis=0), d_two)
    grad_score = grad_score.astype(BF16)
    mg[0] = tn(grad_score, omap_ref[...])
    mg[1] = nn(grad_score, imap_ref[...])

    def holder(i):
        return jnp.where(i < n // 2, 2 * i, 2 * (n - 1 - i) + 1)

    zero = jnp.zeros((share, STATE), F32)

    def g_arrived(i, _):
        s = other(me, i, n)
        remote(es.at[s // per_head], er.at[s], es_sem.at[s], er_sem.at[s], ctx=s).wait_recv()
        remote(gs.at[s], gr.at[s], gs_sem.at[s], gr_sem.at[s], ctx=s).wait_recv()
        return 0

    def to_front(i, g):
        at = holder(n - 1 - i)
        top, rest = pack(g[None])
        yc[at, :share, :] = top[0]
        yc[at, share:, :] = rest[0]
        got = gr[at]
        return er[at] * g + unpack(got[:share], got[share:])

    def send_c(i, _):
        c_copy(other(me, i, n)).start()
        return 0

    def x_arrived(i, _):
        s = other(me, i, n)
        remote(xs.at[mine(s)], xr.at[s], xs_sem.at[s], xr_sem.at[s], ctx=s).wait_recv()
        return 0

    def to_back(i, h):
        at = holder(i)
        yh[at] = h.astype(BF16)
        return er[at] * h + xr[at].astype(F32)

    def send_h(i, _):
        h_copy(other(me, i, n)).start()
        return 0

    lax.fori_loop(1, n, g_arrived, 0)
    lax.fori_loop(0, n, to_front, zero, unroll=4)
    lax.fori_loop(1, n, send_c, 0)
    lax.fori_loop(1, n, x_arrived, 0)
    lax.fori_loop(0, n, to_back, zero, unroll=4)
    lax.fori_loop(1, n, send_h, 0)
    lh[mine(me)] = yh[me]
    lc[me] = yc[me]
    step_w = wide3[:, :SIG]
    end_w = wide3[:, SIG : 2 * SIG]
    exp_w = wide3[:, 2 * SIG :]
    d_f = dout_ref[...].astype(F32)
    signal_f = signal_ref[...].astype(F32)
    skip_w = nn(jnp.broadcast_to(skip_ref[...], (HERE, HERE)), spread1, HIGH)[0:1]
    part[(KSIZE + 1) * QUADS :] = jnp.zeros((SUMS - (KSIZE + 1) * QUADS, STATE), F32)

    def small(at, row):
        at = KSIZE + 1 + at
        part_b[at : at + 1] = jnp.concatenate([row, jnp.zeros((1, STATE - HERE), F32)], axis=1)

    small(2, nt(ones8, per_row(d_f * signal_f), HIGH)[0:1])

    def m_copy(k):
        return remote(
            m_out.at[k], mgot.at[side], ms_sem.at[k], mr_sem.at[side], fsdp=group + k * half
        )

    def to_owner(k):
        m_out[k] = mg[k].astype(BF16)

        @pl.when(group + k * half != f)
        def _():
            m_copy(k).start()

        @pl.when(group + k * half == f)
        def _():
            mgot[side] = m_out[k]

    def c_in(i, _):
        d = other(me, i, n)
        g_copy(d).wait_send()
        e_copy(d).wait_send()
        remote(yc.at[d], lc.at[d], cs_sem.at[d], cr_sem.at[d], ctx=d).wait_recv()
        return 0

    lax.fori_loop(1, n, c_in, 0)
    for h in range(HERE):
        at = slice(h * HDIM, (h + 1) * HDIM)
        got = lc[h * per_head : (h + 1) * per_head]
        state = unpack(got[:, :share], got[:, share:]).reshape(HDIM, STATE)
        lk[3, at, :] = state.astype(BF16)
        lk[2, at, :] = (second_sg[at, :] + end_high8[h : h + 1] * state).astype(BF16)
    for b, rows in enumerate((low, high)):
        mg[0, rows, :] = mg[0, rows, :] + nn(weighted_ref[rows, :], lk[2 + b])
    to_owner(0)
    for b, rows in enumerate((low, high)):
        gw[rows, :] = nt(imap_ref[rows, :], lk[2 + b])
    gw_v = gw[...]
    back_row = per_row(gw_v * scaled_ref[...].astype(F32)) * to_end
    back_low = jnp.sum(jnp.where(lane < BLK, back_row, 0.0), axis=1, keepdims=True)
    back_high = jnp.sum(jnp.where(lane < BLK, 0.0, back_row), axis=1, keepdims=True)
    grad_scaled = gw_v * end_w + intra[...]
    own_step = per_row(grad_scaled * signal_f)
    gpad[:ROWS, :SIG] = (skip_w * d_f + grad_scaled * step_w) * slope[:, :SIG]

    def sums(cols, source, into, every, at):
        g = gpad[:ROWS, cols]
        for k in range(KSIZE):
            start = EDGE - RIM + k
            row = k * every + at
            into[row : row + 1] = jnp.sum(
                g * pad[start : start + ROWS, source], axis=0, keepdims=True
            )
        row = KSIZE * every + at
        into[row : row + 1] = jnp.sum(g, axis=0, keepdims=True)

    earlier = jnp.where(
        odd == 0, lax.rem(me + n - 2, n), jnp.where(me == n - 1, n - 2, lax.rem(me + 2, n))
    )
    earlier = jnp.where(me == 0, 1, earlier)

    def rim(i, cols):
        copy = remote(
            gpad.at[0:RIMS, cols], rims.at[:, cols], r_sem.at[2 * i], r_sem.at[2 * i + 1],
            ctx=earlier,
        )
        copy.start()
        return copy

    sig_cols, map_cols = slice(0, SIG), slice(SIG, OWN)
    sig_rim = rim(0, sig_cols)
    for q in range(QUADS):
        sums(third(q), third(q), part, QUADS, q)

    planes = n // 2
    y = me // planes
    z = me - y * planes
    z_high = z // 4
    z_low = z - 4 * z_high
    here = 4 * y + z_low
    sent = []

    def to_near(src, dst, at, recv_sem):
        for k in range(1, 8):
            s = lax.rem(here + k, 8)
            d = s // 4 * planes + z_high * 4 + s - s // 4 * 4
            copy = remote(src, dst.at[here], q_send.at[at + k], recv_sem.at[here], ctx=d)
            copy.start()
            sent.append(copy)
        dst[here] = src[...]

    def near_in(src, dst, recv_sem):
        for k in range(1, 8):
            s = lax.rem(here + k, 8)
            remote(src, dst.at[s], q_send.at[k], recv_sem.at[s], ctx=mate).wait_recv()

    def to_far(src, dst, at, recv_sem):
        for k in range(1, 4):
            s = lax.rem(z_high + k, 4)
            d = y * planes + 4 * s + z_low
            copy = remote(src, dst.at[z_high], q_send.at[at + k], recv_sem.at[z_high], ctx=d)
            copy.start()
            sent.append(copy)
        dst[z_high] = src[...]

    def far_in(src, dst, recv_sem):
        for k in range(1, 4):
            s = lax.rem(z_high + k, 4)
            remote(src, dst.at[s], q_send.at[k], recv_sem.at[s], ctx=mate).wait_recv()

    low_part[...] = part[...].astype(BF16)
    to_near(low_part, near, 0, q_near)

    def raw(r, out, taps, cols):
        acc = taps[RIM : RIM + 1] * gpad[r : r + BLK, cols]
        for k in range(RIM):
            acc = acc + taps[k : k + 1] * gpad[r + RIM - k : r + RIM - k + BLK, cols]
        out[:, cols] = acc

    def transposed(i, rim_copy, taps, cols, out):
        rim_copy.wait()
        gpad[ROWS:, cols] = jnp.where(me == 1, 0.0, rims[:, cols])
        raw(BLK, swap, taps, cols)
        away = remote(
            swap.at[:, cols], out.at[pl.ds(kept, BLK)], w_sem.at[2 * i], w_sem.at[2 * i + 1],
            ctx=mate,
        )
        away.start()
        raw(0, stay, taps, cols)
        return away, fetch(i, stay.at[:, cols], out.at[pl.ds(kept, BLK)])

    def h_in(i, _):
        d = other(me, i, n)
        x_copy(d).wait_send()
        remote(yh.at[d], lh.at[mine(d)], hs_sem.at[d], hr_sem.at[d], ctx=d).wait_recv()
        return 0

    lax.fori_loop(1, n, h_in, 0)
    lk[0] = lh[...]
    for h in range(HERE):
        at = slice(h * HDIM, (h + 1) * HDIM)
        lk[1, at, :] = (end_low8[h : h + 1] * lh[at, :].astype(F32) + first_local[at, :]).astype(
            BF16
        )
    for b, rows in enumerate((low, high)):
        mg[1, rows, :] = mg[1, rows, :] + nn(sgrad_ref[rows, :], lk[b])
    to_owner(1)
    end_terms = []
    for b, rows in enumerate((low, high)):
        oh[rows, :] = nt(omap_ref[rows, :], lk[b])
        both = lk[b].astype(F32) * lk[2 + b].astype(F32)
        both = jnp.sum(both.reshape(HERE, HDIM, STATE), axis=1)
        end_terms.append(jnp.sum(both, axis=1, keepdims=True))
    grad_sum = per_row(d_f * exp_w * oh[...]) - back_row + drow[...]
    last_low = back_low + end_low * end_terms[0]
    last_high = back_high + end_high * end_terms[1]
    grad_sum = grad_sum + jnp.where(
        lane == BLK - 1, last_low, jnp.where(lane == ROWS - 1, last_high, 0.0)
    )
    grad_log = nn(grad_sum, lower_f, HIGH)
    grad_step = grad_log * rate + own_step
    grad_dt = grad_step * sigmoid(logits)
    ddt_mine[...] = grad_dt
    ddt_copy = remote(ddt_mine, ddt_got, w_sem.at[0], w_sem.at[1], ctx=mate)
    ddt_copy.start()
    small(0, nt(ones8, grad_log * step, HIGH)[0:1] * (-jnp.exp(alog_ref[...])))
    small(1, nt(ones8, grad_dt, HIGH)[0:1])
    near_in(low_part, near, q_near)
    low_near[...] = jnp.sum(near[...].astype(F32), axis=0).astype(BF16)
    to_far(low_near, far, 7, q_far)

    for k in range(2):

        @pl.when(first + k != f)
        def _():
            remote(
                m_out.at[k], mgot.at[k], ms_sem.at[k], mr_sem.at[k], fsdp=first + k
            ).wait_recv()

    gpad[:ROWS, SIG:] = (mgot[0].astype(F32) + mgot[1].astype(F32)) * slope[:, SIG:]
    map_rim = rim(1, map_cols)
    sums(map_cols, slice(SIG + 2 * STATE, WIDE), part_b, 1, 0)
    to_near(part_b, near_b, 10, q_near_b)
    sig_out = transposed(1, sig_rim, taps_ref, sig_cols, dsig_hbm)
    map_out = transposed(2, map_rim, mtaps_ref, map_cols, dmap_hbm)
    near_in(part_b, near_b, q_near_b)
    sum_b[...] = jnp.sum(near_b[...], axis=0)
    to_far(sum_b, far_b, 17, q_far_b)
    ddt_copy.wait()
    own, got = ddt_mine[...], ddt_got[...]
    ddt_low = jnp.where(odd == 0, own, turned(got))
    ddt_high = jnp.where(odd == 0, got, turned(own))
    ddt_ref[...] = jnp.where(lane < BLK, ddt_low, ddt_high)
    ddt_out = fetch(3, ddt_ref, ddt_hbm)
    far_in(low_near, far, q_far)
    total[...] = jnp.sum(far[...].astype(F32), axis=0)
    sums_out = fetch(4, total, sums_hbm)

    def done(i, _):
        d = other(me, i, n)
        h_copy(d).wait_send()
        c_copy(d).wait_send()
        return 0

    lax.fori_loop(1, n, done, 0)
    for k in range(2):

        @pl.when(group + k * half != f)
        def _():
            m_copy(k).wait_send()

    far_in(sum_b, far_b, q_far_b)
    total_b[...] = jnp.sum(far_b[...], axis=0)
    small_out = fetch(5, total_b, small_hbm)
    for copy in sent:
        copy.wait_send()
    for copy in sig_out + map_out + (ddt_out, sums_out, small_out):
        copy.wait()


def main(*operands):
    n = lax.axis_size("ctx")
    half = lax.axis_size("fsdp") // 2
    share = SIG // n
    dma = pltpu.SemaphoreType.DMA
    vm = pltpu.VMEM
    return pl.pallas_call(
        functools.partial(main_kernel, n, half),
        out_shape=(
            jax.ShapeDtypeStruct((ROWS, SIG), F32),
            jax.ShapeDtypeStruct((ROWS, STATE), F32),
            jax.ShapeDtypeStruct((SUMS, STATE), F32),
            jax.ShapeDtypeStruct((8, STATE), F32),
            jax.ShapeDtypeStruct((HERE, ROWS), F32),
        ),
        in_specs=[pl.BlockSpec(memory_space=pl.ANY)] * len(operands),
        out_specs=(HBM,) * 5,
        scratch_shapes=[
            vm((ROWS, SIG), BF16),
            vm((ROWS, 3 * STATE), BF16),
            vm((ROWS, SIG), BF16),
            vm((HERE, ROWS), F32),
            vm((HERE, ROWS), F32),
            vm((KSIZE, SIG), F32),
            vm((1, SIG), F32),
            vm((KSIZE, STATE), F32),
            vm((1, STATE), F32),
            vm((1, HERE), F32),
            vm((1, HERE), F32),
            vm((1, HERE), F32),
            vm((EDGE, WIDE), BF16),
            vm((EDGE, WIDE), BF16),
            vm((8, STATE), F32),
            vm((2, 8, STATE), F32),
            vm((EDGE + ROWS, WIDE), F32),
            vm((ROWS, OWN), F32),
            vm((ROWS, SIG), BF16),
            vm((ROWS, SIG), BF16),
            vm((ROWS, SIG), BF16),
            vm((ROWS, SIG), BF16),
            vm((ROWS, STATE), BF16),
            vm((ROWS, STATE), BF16),
            vm((ROWS, 3 * SIG), F32),
            vm((ROWS, SIG), F32),
            vm((ROWS, SIG), F32),
            vm((ROWS, SIG), F32),
            vm((HERE, ROWS), F32),
            vm((2, ROWS, STATE), BF16),
            vm((SIG, STATE), BF16),
            vm((n, 3 * share // 2, STATE), BF16),
            vm((HERE, 1, STATE), F32),
            vm((n, share, STATE), BF16),
            vm((n, 3 * share // 2, STATE), BF16),
            vm((n, 1, STATE), F32),
            vm((n, share, STATE), BF16),
            vm((n, 3 * share // 2, STATE), BF16),
            vm((SIG, STATE), BF16),
            vm((n, 3 * share // 2, STATE), BF16),
            vm((SIG, STATE), F32),
            vm((SIG, STATE), F32),
            vm((4, SIG, STATE), BF16),
            vm((2, ROWS, STATE), F32),
            vm((2, ROWS, STATE), BF16),
            vm((ROWS + RIMS, OWN), F32),
            vm((RIMS, OWN), F32),
            vm((BLK, OWN), F32),
            vm((BLK, OWN), F32),
            vm((HERE, ROWS), F32),
            vm((HERE, ROWS), F32),
            vm((HERE, ROWS), F32),
            vm((SUMS, STATE), F32),
            vm((SUMS, STATE), BF16),
            vm((8, SUMS, STATE), BF16),
            vm((SUMS, STATE), BF16),
            vm((4, SUMS, STATE), BF16),
            vm((SUMS, STATE), F32),
            vm((8, STATE), F32),
            vm((8, 8, STATE), F32),
            vm((8, STATE), F32),
            vm((4, 8, STATE), F32),
            vm((8, STATE), F32),
        ]
        + [dma((17,)), dma((6,)), dma((6,)), dma((3,)), dma((3,)), dma((2,)), dma((2,))]
        + [dma((n,))] * 10
        + [dma((2,)), dma((2,)), dma((4,)), dma((6,)), dma((21,)), dma((8,)), dma((4,)), dma((8,)), dma((4,))],
        compiler_params=pltpu.CompilerParams(
            collective_id=0, has_side_effects=True, vmem_limit_bytes=56 * 1024 * 1024
        ),
        name="main",
    )(*operands)


def last_kernel(
    scale, dsig_in, dmap_in, sums_hbm, small_hbm, ddt_in,
    dsig, dmap, ddt, dtaps, dmtaps, dbias, dmbias, dalog, ddtb, dskip,
    sums_in, small_in, sem
):
    copies = []
    for src, dst in (
        (sums_hbm, sums_in), (small_hbm, small_in), (dsig_in, dsig), (dmap_in, dmap), (ddt_in, ddt)
    ):
        copies.append(pltpu.make_async_copy(src, dst, sem.at[len(copies)]))
        copies[-1].start()
    copies[0].wait()
    copies[1].wait()
    for k in range(KSIZE + 1):
        for q in range(QUADS):
            at = k * QUADS + q
            cols = slice(q * STATE, (q + 1) * STATE)
            row = sums_in[at : at + 1] * scale
            if k < KSIZE:
                dtaps[k : k + 1, cols] = row
            else:
                dbias[:, cols] = row
    dmtaps[...] = small_in[:KSIZE] * scale
    dmbias[...] = small_in[KSIZE : KSIZE + 1] * scale
    for k, out in enumerate((dalog, ddtb, dskip)):
        at = KSIZE + 1 + k
        out[...] = small_in[at : at + 1, :HERE] * scale
    for copy in copies[2:]:
        copy.wait()


def last(*operands):
    scale = 1.0 / math.sqrt(float(lax.axis_size("ctx") * ROWS))
    shapes = (
        (ROWS, SIG), (ROWS, STATE), (HERE, ROWS), (KSIZE, SIG), (KSIZE, STATE),
        (1, SIG), (1, STATE), (1, HERE), (1, HERE), (1, HERE),
    )
    return pl.pallas_call(
        functools.partial(last_kernel, scale),
        out_shape=tuple(jax.ShapeDtypeStruct(s, F32) for s in shapes),
        in_specs=[HBM] * 5,
        out_specs=(HBM,) * 3 + (VM,) * (len(shapes) - 3),
        scratch_shapes=[
            pltpu.VMEM((SUMS, STATE), F32),
            pltpu.VMEM((8, STATE), F32),
            pltpu.SemaphoreType.DMA((5,)),
        ],
        compiler_params=pltpu.CompilerParams(vmem_limit_bytes=60 * 1024 * 1024),
        name="last",
    )(*operands)


def shards(
    sig_raw,
    map_raw,
    step_size_logits,
    d_out,
    sig_taps,
    map_taps,
    sig_bias,
    map_bias,
    a_log,
    dt_bias,
    skip_gain,
):
    found = main(
        sig_raw, map_raw, step_size_logits.T, d_out, sig_taps, sig_bias[None, :], map_taps,
        map_bias[None, :], a_log[None, :], dt_bias[None, :], skip_gain[None, :],
    )
    out = last(*found)
    return out[:2] + (out[2].T,) + out[3:5] + tuple(a.reshape(-1) for a in out[5:])


def solution(mesh):
    return jax.shard_map(
        shards,
        mesh=mesh,
        in_specs=(
            P("ctx", "fsdp"),
            P("ctx", None),
            P("ctx", "fsdp"),
            P("ctx", "fsdp"),
            P(None, "fsdp"),
            P(None, "fsdp"),
            P("fsdp"),
            P("fsdp"),
            P("fsdp"),
            P("fsdp"),
            P("fsdp"),
        ),
        out_specs=(
            P("ctx", "fsdp"),
            P("ctx", "fsdp"),
            P("ctx", "fsdp"),
            P(None, "fsdp"),
            P(None, "fsdp"),
            P("fsdp"),
            P("fsdp"),
            P("fsdp"),
            P("fsdp"),
            P("fsdp"),
        ),
        check_vma=False,
    )
```

```python
import functools
import math

import jax
import jax.numpy as jnp
from jax import lax
from jax.experimental import pallas as pl
from jax.experimental.pallas import tpu as pltpu
from jax.sharding import PartitionSpec as P

HEADS = 128
HDIM = 64
STATE = 128
GROUPS = 8
HERE = 8
KSIZE = 4
RIM = KSIZE - 1
BLK = 64
ROWS = 2 * BLK
SIG = HERE * HDIM
WIDE = SIG + 3 * STATE
OWN = SIG + STATE
EDGE = 16
RIMS = 8
QUADS = SIG // STATE
SUMS = 24
FINE = 10
MESH = pl.DeviceIdType.MESH
VM = pl.BlockSpec(memory_space=pltpu.VMEM)
HBM = pl.BlockSpec(memory_space=pltpu.HBM)
HIGH = lax.Precision.HIGHEST
F32 = jnp.float32
BF16 = jnp.bfloat16


def signal(sem, **where):
    pl.semaphore_signal(sem, inc=1, device_id=where, device_id_type=MESH)


def remote(src, dst, send_sem, recv_sem, **where):
    return pltpu.make_async_remote_copy(
        src_ref=src,
        dst_ref=dst,
        send_sem=send_sem,
        recv_sem=recv_sem,
        device_id=where,
        device_id_type=MESH,
    )


def other(me, i, n):
    off = jnp.where(lax.rem(i, 2) == 1, (i + 1) // 2, n - i // 2)
    return lax.rem(me + off, n)


def columns(start):
    return pl.ds(pl.multiple_of(start * STATE, STATE), STATE)


def nn(a, b, precision=None):
    return lax.dot_general(
        a, b, (((1,), (0,)), ((), ())), precision=precision, preferred_element_type=F32
    )


def nt(a, b, precision=None):
    return lax.dot_general(
        a, b, (((1,), (1,)), ((), ())), precision=precision, preferred_element_type=F32
    )


def tn(a, b):
    return lax.dot_general(a, b, (((0,), (0,)), ((), ())), preferred_element_type=F32)


def sigmoid(v):
    return 1.0 / (1.0 + jnp.exp(-v))


def log1p_small(e):
    series = e * (
        1.0 + e * (-1.0 / 2 + e * (1.0 / 3 + e * (-1.0 / 4 + e * (1.0 / 5 + e * (-1.0 / 6)))))
    )
    return jnp.where(e < 0.03, series, jnp.log(1.0 + e))


def pack(v):
    n, rows, _ = v.shape
    high = v.astype(BF16)
    value = high.astype(F32)
    tiny = jnp.abs(value) < 1e-30
    ratio = jnp.where(tiny, 0.0, (v - value) / jnp.where(tiny, 1.0, value))
    steps = jnp.clip(jnp.round(ratio * (256.0 * FINE)), -FINE, FINE)
    both = steps[:, : rows // 2] * (2.0 * FINE + 1.0) + steps[:, rows // 2 :]
    return high, both.astype(BF16)


def unpack(high, both):
    value = high.astype(F32)
    both = both.astype(F32)
    first = jnp.floor((both + (FINE + 0.5)) * (1.0 / (2.0 * FINE + 1.0)))
    second = both - first * (2.0 * FINE + 1.0)
    steps = jnp.concatenate([first, second], axis=-2)
    return value + value * steps * (1.0 / (256.0 * FINE))


def main_kernel(
    n, half, sig_hbm, map_hbm, dt_hbm, dout_hbm, taps_hbm, bias_hbm, mtaps_hbm, mbias_hbm,
    alog_hbm, dtb_hbm, skip_hbm,
    dsig_hbm, dmap_hbm, sums_hbm, small_hbm, ddt_hbm,
    sig_in, map_in, dout_ref, dt_in, dt_got, taps_ref, bias_ref, mtaps_ref, mbias_ref,
    alog_ref, dtb_ref, skip_ref, tail_own, tail_got, tap_row, gtaps_ref,
    pad, slope, signal_ref, scaled_ref, weighted_ref, sgrad_ref, imap_ref, omap_ref, wide3, intra,
    oh, gw, drow, m_out, xs, gs, es, xr, gr, er, yh, yc, lh, lc, first_local, first_sg, second_sg, lk,
    mg, mgot, gpad, rims, swap, stay, ddt_mine, ddt_got, ddt_ref,
    part, low_part, near, low_near, far, total, part_b, near_b, sum_b, far_b, total_b,
    l_sem, n_send, n_recv, b_send, b_recv, tap_send, tap_recv,
    xs_sem, xr_sem, gs_sem, gr_sem, es_sem, er_sem, hs_sem, hr_sem, cs_sem, cr_sem,
    ms_sem, mr_sem, r_sem, w_sem, q_send, q_near, q_far, q_near_b, q_far_b
):
    me = lax.axis_index("ctx")
    f = lax.axis_index("fsdp")
    odd = lax.rem(me, 2)
    mate = me + 1 - 2 * odd
    side_ctx = lax.rem(me + n - 1 + 2 * odd, n)
    slot = f // half
    first = 2 * (f - slot * half)
    group = f // 2
    side = f - 2 * group
    share = SIG // n
    per_head = n // HERE
    kept = pl.multiple_of(odd * BLK, BLK)
    given = pl.multiple_of((1 - odd) * BLK, BLK)
    ending = pl.multiple_of((1 - odd) * BLK + BLK - EDGE, EDGE)
    starts = (group, GROUPS + group, f)
    barrier = pltpu.get_barrier_semaphore()

    def greet(i, _):
        signal(barrier, ctx=other(me, i, n))
        return 0

    lax.fori_loop(1, n, greet, 0)
    for k in range(2):

        @pl.when(group + k * half != f)
        def _():
            signal(barrier, fsdp=group + k * half)

        @pl.when(first + k != f)
        def _():
            signal(barrier, fsdp=first + k)

    def fetch(i, src, dst):
        copy = pltpu.make_async_copy(src, dst, l_sem.at[i])
        copy.start()
        return copy

    def third(k):
        return slice(k * STATE, (k + 1) * STATE)

    local = [
        fetch(0, mtaps_hbm, mtaps_ref),
        fetch(1, mbias_hbm, mbias_ref),
        fetch(2, dt_hbm, dt_in),
        fetch(3, alog_hbm, alog_ref),
        fetch(4, dtb_hbm, dtb_ref),
        fetch(5, skip_hbm, skip_ref),
        fetch(6, taps_hbm, taps_ref),
        fetch(7, bias_hbm, bias_ref),
        fetch(8, sig_hbm.at[pl.ds(kept, BLK)], sig_in.at[0:BLK]),
        fetch(9, dout_hbm.at[pl.ds(kept, BLK)], dout_ref.at[0:BLK]),
        fetch(10, sig_hbm.at[pl.ds(ending, EDGE)], tail_own.at[:, 0:SIG]),
    ]
    for k, start in enumerate(starts):
        local.append(
            fetch(
                11 + k,
                map_hbm.at[pl.ds(kept, BLK), columns(start)],
                map_in.at[0:BLK, third(k)],
            )
        )
        local.append(
            fetch(
                14 + k,
                map_hbm.at[pl.ds(ending, EDGE), columns(start)],
                tail_own.at[:, SIG + k * STATE : SIG + (k + 1) * STATE],
            )
        )

    for copy in local:
        copy.wait()
    tap_row[0:KSIZE] = mtaps_ref[...]
    tap_row[KSIZE : KSIZE + 1] = mbias_ref[...]
    tap_row[KSIZE + 1 :] = jnp.zeros((8 - KSIZE - 1, STATE), F32)
    selves = jnp.where(group == f, 1, 0) + jnp.where(group + half == f, 1, 0)
    pl.semaphore_wait(barrier, n - 1 + 4 - 2 * selves)

    for k in range(2):

        @pl.when(first + k != f)
        def _():
            remote(
                tap_row, gtaps_ref.at[slot], tap_send.at[k], tap_recv.at[slot], fsdp=first + k
            ).start()

        @pl.when(group + k * half == f)
        def _():
            gtaps_ref[k] = tap_row[...]

    def to_mate(i, src, dst):
        copy = remote(src, dst, n_send.at[i], n_recv.at[i], ctx=mate)
        copy.start()
        return copy

    def to_side(i, dst_cols):
        copy = remote(
            tail_own.at[:, dst_cols], tail_got.at[:, dst_cols], b_send.at[i], b_recv.at[i],
            ctx=side_ctx,
        )
        copy.start()
        return copy

    def map_copy(k):
        return to_mate(
            1 + k, map_hbm.at[pl.ds(given, BLK), columns(starts[k])], map_in.at[BLK:ROWS, third(k)]
        )

    dt_copy = to_mate(0, dt_hbm, dt_got)
    out_cols = slice(SIG + STATE, SIG + 2 * STATE)
    out_tail = to_side(0, out_cols)
    out_copy = map_copy(1)
    dout_copy = to_mate(5, dout_hbm.at[pl.ds(given, BLK)], dout_ref.at[BLK:ROWS])
    tails = [to_side(1, slice(0, SIG + STATE)), to_side(2, slice(SIG + 2 * STATE, WIDE))]
    map_copies = [map_copy(0), map_copy(2)]
    sig_copy = to_mate(4, sig_hbm.at[pl.ds(given, BLK)], sig_in.at[BLK:ROWS])

    lane = lax.broadcasted_iota(jnp.int32, (HERE, ROWS), 1)
    row_id = lax.broadcasted_iota(jnp.int32, (ROWS, ROWS), 0)
    col_id = lax.broadcasted_iota(jnp.int32, (ROWS, ROWS), 1)
    lower = ((row_id >= BLK) == (col_id >= BLK)) & (col_id <= row_id)
    lower_f = jnp.where(lower, 1.0, 0.0).astype(F32)
    eye = jnp.where(row_id == col_id, 1.0, 0.0).astype(F32)
    eye8 = eye[:HERE, :HERE]
    ones8 = jnp.ones((HERE, ROWS), F32)
    head3 = lax.broadcasted_iota(jnp.int32, (3 * HERE, 3 * SIG), 0)
    spread3 = jnp.where(
        lax.broadcasted_iota(jnp.int32, (3 * HERE, 3 * SIG), 1) // HDIM == head3, 1.0, 0.0
    ).astype(F32)
    spread1 = spread3[:HERE, :SIG]

    def in_rows(ref):
        return nt(eye8, jnp.broadcast_to(ref[...], (ROWS, HERE)), HIGH)

    def per_row(y):
        return nt(spread1, y, HIGH)

    def turned(x):
        return pltpu.roll(x, BLK, 1)

    def preact(r, rows, cols, taps, bias):
        acc = bias
        for k in range(KSIZE):
            start = EDGE - RIM + k + r
            acc = acc + taps[k : k + 1] * pad[start : start + rows, cols]
        return acc

    def sig_rows(r, count):
        rows = slice(r, r + count)
        for q in range(SIG // STATE):
            cols = third(q)
            v = preact(r, count, cols, taps_ref[:, cols], bias_ref[:, cols])
            s = sigmoid(v)
            slope[rows, cols] = s * (1.0 + v * (1.0 - s))
            signal_ref[rows, cols] = (v * s).astype(BF16)

    pad[EDGE : EDGE + BLK, :SIG] = sig_in[:BLK, :].astype(F32)
    pad[EDGE : EDGE + BLK, SIG:] = map_in[:BLK, :].astype(F32)
    keep = jnp.where(me == 0, 0.0, 1.0).astype(F32)

    def before(cols):
        mine_then = tail_own[:, cols].astype(F32)
        pad[:EDGE, cols] = keep * jnp.where(me == n - 1, mine_then, tail_got[:, cols].astype(F32))

    dt_copy.wait()
    own, got = dt_in[...], dt_got[...]
    own = jnp.where(odd == 0, own, turned(own))
    got = jnp.where(odd == 0, turned(got), got)
    logits = jnp.where(lane < BLK, own, got) + in_rows(dtb_ref)
    rate = -jnp.exp(in_rows(alog_ref))
    step = jnp.maximum(logits, 0.0) + log1p_small(jnp.exp(-jnp.abs(logits)))
    ds = nt(step * rate, lower_f, HIGH)
    end_low = jnp.exp(ds[:, BLK - 1 : BLK])
    end_high = jnp.exp(ds[:, ROWS - 1 : ROWS])
    end = jnp.where(lane < BLK, ds[:, BLK - 1 : BLK], ds[:, ROWS - 1 : ROWS])
    to_end = jnp.exp(end - ds)
    col4 = nt(eye, jnp.concatenate([step, to_end, jnp.exp(ds), ds], axis=0), HIGH)
    ds_col = col4[:, 3 * HERE :]
    wide3[...] = nn(col4[:, : 3 * HERE], spread3, HIGH)
    end_low8 = jnp.broadcast_to(end_low, (HERE, STATE))
    end_high8 = jnp.broadcast_to(end_high, (HERE, STATE))
    both_ends = end_low8 * end_high8
    for h in range(HERE):
        es[h] = both_ends[h : h + 1]

    def e_copy(d):
        return remote(es.at[d // per_head], er.at[me], es_sem.at[d], er_sem.at[me], ctx=d)

    def send_ends(i, _):
        e_copy(other(me, i, n)).start()
        return 0

    lax.fori_loop(1, n, send_ends, 0)
    er[me] = es[me // per_head]

    for k in range(2):

        @pl.when(group + k * half != f)
        def _():
            remote(
                tap_row, gtaps_ref.at[k], tap_send.at[k], tap_recv.at[k], fsdp=group + k * half
            ).wait_recv()

        @pl.when(first + k != f)
        def _():
            remote(
                tap_row, gtaps_ref.at[slot], tap_send.at[k], tap_recv.at[slot], fsdp=first + k
            ).wait_send()

    out_tail.wait()
    before(out_cols)
    def map_rows(k, out, r, count):
        cols = slice(SIG + k * STATE, SIG + (k + 1) * STATE)
        v = preact(r, count, cols, gtaps_ref[k, :KSIZE], gtaps_ref[k, KSIZE : KSIZE + 1])
        out[r : r + count, :] = (v * sigmoid(v)).astype(BF16)

    def sgrad_rows(rows):
        for q in range(QUADS):
            cols3 = slice(2 * SIG + q * STATE, 2 * SIG + (q + 1) * STATE)
            grad = dout_ref[rows, third(q)].astype(F32) * wide3[rows, cols3]
            sgrad_ref[rows, third(q)] = grad.astype(BF16)
        return tn(sgrad_ref[rows, :], omap_ref[rows, :])

    def mine(d):
        return pl.ds(pl.multiple_of(d * share, share), share)

    def x_copy(d):
        return remote(xs.at[mine(d)], xr.at[me], xs_sem.at[d], xr_sem.at[me], ctx=d)

    def g_copy(d):
        return remote(gs.at[d], gr.at[me], gs_sem.at[d], gr_sem.at[me], ctx=d)

    def h_copy(d):
        return remote(yh.at[d], lh.at[mine(me)], hs_sem.at[d], hr_sem.at[me], ctx=d)

    def c_copy(d):
        return remote(yc.at[d], lc.at[me], cs_sem.at[d], cr_sem.at[me], ctx=d)

    def send_g(i, _):
        g_copy(other(me, i, n)).start()
        return 0

    def send_x(i, _):
        x_copy(other(me, i, n)).start()
        return 0

    low, high = slice(0, BLK), slice(BLK, ROWS)
    map_rows(1, omap_ref, 0, BLK)
    first_sg[...] = sgrad_rows(low)
    out_copy.wait()
    pad[EDGE + BLK :, out_cols] = map_in[BLK:, third(1)].astype(F32)
    map_rows(1, omap_ref, BLK, BLK)
    dout_copy.wait()
    second_sg[...] = sgrad_rows(high)
    for h in range(HERE):
        at = slice(h * HDIM, (h + 1) * HDIM)
        link = first_sg[at, :] + end_low8[h : h + 1] * second_sg[at, :]
        top, rest = pack(link.reshape(per_head, share, STATE))
        gs[h * per_head : (h + 1) * per_head, :share, :] = top
        gs[h * per_head : (h + 1) * per_head, share:, :] = rest
    lax.fori_loop(1, n, send_g, 0)
    gr[me] = gs[me]

    for copy in tails + map_copies:
        copy.wait()
    for cols in (slice(0, SIG + STATE), slice(SIG + 2 * STATE, WIDE)):
        before(cols)
    pad[EDGE + BLK :, SIG : SIG + STATE] = map_in[BLK:, third(0)].astype(F32)
    pad[EDGE + BLK :, SIG + 2 * STATE :] = map_in[BLK:, third(2)].astype(F32)
    map_rows(0, imap_ref, 0, ROWS)
    v = preact(0, ROWS, slice(SIG + 2 * STATE, WIDE), mtaps_ref[...], mbias_ref[...])
    s = sigmoid(v)
    slope[:, SIG:] = s * (1.0 + v * (1.0 - s))
    sig_copy.wait()
    pad[EDGE + BLK :, :SIG] = sig_in[BLK:, :].astype(F32)
    sig_rows(0, ROWS)
    for q in range(QUADS):
        cols = third(q)
        cols2 = slice(SIG + q * STATE, SIG + (q + 1) * STATE)
        scaled_b = (signal_ref[:, cols].astype(F32) * wide3[:, cols]).astype(BF16)
        scaled_ref[:, cols] = scaled_b
        weighted_ref[:, cols] = (scaled_b.astype(F32) * wide3[:, cols2]).astype(BF16)
    first_local[...] = tn(weighted_ref[low, :], imap_ref[low, :])
    second_local = tn(weighted_ref[high, :], imap_ref[high, :])
    for h in range(HERE):
        at = slice(h * HDIM, (h + 1) * HDIM)
        xs[at, :] = (end_high8[h : h + 1] * first_local[at, :] + second_local[at, :]).astype(BF16)
    lax.fori_loop(1, n, send_x, 0)
    xr[me] = xs[mine(me)]

    score = nt(omap_ref[...], imap_ref[...])
    lane_row = lax.broadcasted_iota(jnp.int32, (ROWS, STATE), 1)
    grad_score = jnp.zeros((ROWS, ROWS), F32)
    for q in range(HERE // 2):
        cols = third(q)
        d_pair = dout_ref[:, cols].astype(F32)
        d_two = jnp.concatenate(
            [jnp.where(lane_row < HDIM, d_pair, 0.0), jnp.where(lane_row < HDIM, 0.0, d_pair)],
            axis=0,
        ).astype(BF16)
        grad_mix2 = nt(d_two, scaled_ref[:, cols])
        mixes = []
        for k in range(2):
            h = 2 * q + k
            grad_mix = grad_mix2[k * ROWS : (k + 1) * ROWS]
            gap = jnp.minimum(ds_col[:, h : h + 1] - ds[h : h + 1, :], 0.0)
            decay = jnp.where(lower, jnp.exp(gap), 0.0)
            mix = score * decay
            mixes.append(mix.astype(BF16))
            grad_score = grad_score + grad_mix * decay
            product = grad_mix * mix
            drow[h : h + 1, :] = nt(ones8, product, HIGH)[0:1] - jnp.sum(
                product, axis=0, keepdims=True
            )
        intra[:, cols] = tn(jnp.concatenate(mixes, axis=0), d_two)
    grad_score = grad_score.astype(BF16)
    mg[0] = tn(grad_score, omap_ref[...])
    mg[1] = nn(grad_score, imap_ref[...])

    def holder(i):
        return jnp.where(i < n // 2, 2 * i, 2 * (n - 1 - i) + 1)

    zero = jnp.zeros((share, STATE), F32)

    def g_arrived(i, _):
        s = other(me, i, n)
        remote(es.at[s // per_head], er.at[s], es_sem.at[s], er_sem.at[s], ctx=s).wait_recv()
        remote(gs.at[s], gr.at[s], gs_sem.at[s], gr_sem.at[s], ctx=s).wait_recv()
        return 0

    def to_front(i, g):
        at = holder(n - 1 - i)
        top, rest = pack(g[None])
        yc[at, :share, :] = top[0]
        yc[at, share:, :] = rest[0]
        got = gr[at]
        return er[at] * g + unpack(got[:share], got[share:])

    def send_c(i, _):
        c_copy(other(me, i, n)).start()
        return 0

    def x_arrived(i, _):
        s = other(me, i, n)
        remote(xs.at[mine(s)], xr.at[s], xs_sem.at[s], xr_sem.at[s], ctx=s).wait_recv()
        return 0

    def to_back(i, h):
        at = holder(i)
        yh[at] = h.astype(BF16)
        return er[at] * h + xr[at].astype(F32)

    def send_h(i, _):
        h_copy(other(me, i, n)).start()
        return 0

    lax.fori_loop(1, n, g_arrived, 0)
    lax.fori_loop(0, n, to_front, zero, unroll=4)
    lax.fori_loop(1, n, send_c, 0)
    lax.fori_loop(1, n, x_arrived, 0)
    lax.fori_loop(0, n, to_back, zero, unroll=4)
    lax.fori_loop(1, n, send_h, 0)
    lh[mine(me)] = yh[me]
    lc[me] = yc[me]
    step_w = wide3[:, :SIG]
    end_w = wide3[:, SIG : 2 * SIG]
    exp_w = wide3[:, 2 * SIG :]
    d_f = dout_ref[...].astype(F32)
    signal_f = signal_ref[...].astype(F32)
    skip_w = nn(jnp.broadcast_to(skip_ref[...], (HERE, HERE)), spread1, HIGH)[0:1]
    part[(KSIZE + 1) * QUADS :] = jnp.zeros((SUMS - (KSIZE + 1) * QUADS, STATE), F32)

    def small(at, row):
        at = KSIZE + 1 + at
        part_b[at : at + 1] = jnp.concatenate([row, jnp.zeros((1, STATE - HERE), F32)], axis=1)

    small(2, nt(ones8, per_row(d_f * signal_f), HIGH)[0:1])

    def m_copy(k):
        return remote(
            m_out.at[k], mgot.at[side], ms_sem.at[k], mr_sem.at[side], fsdp=group + k * half
        )

    def to_owner(k):
        m_out[k] = mg[k].astype(BF16)

        @pl.when(group + k * half != f)
        def _():
            m_copy(k).start()

        @pl.when(group + k * half == f)
        def _():
            mgot[side] = m_out[k]

    def c_in(i, _):
        d = other(me, i, n)
        g_copy(d).wait_send()
        e_copy(d).wait_send()
        remote(yc.at[d], lc.at[d], cs_sem.at[d], cr_sem.at[d], ctx=d).wait_recv()
        return 0

    lax.fori_loop(1, n, c_in, 0)
    for h in range(HERE):
        at = slice(h * HDIM, (h + 1) * HDIM)
        got = lc[h * per_head : (h + 1) * per_head]
        state = unpack(got[:, :share], got[:, share:]).reshape(HDIM, STATE)
        lk[3, at, :] = state.astype(BF16)
        lk[2, at, :] = (second_sg[at, :] + end_high8[h : h + 1] * state).astype(BF16)
    for b, rows in enumerate((low, high)):
        mg[0, rows, :] = mg[0, rows, :] + nn(weighted_ref[rows, :], lk[2 + b])
    to_owner(0)
    for b, rows in enumerate((low, high)):
        gw[rows, :] = nt(imap_ref[rows, :], lk[2 + b])
    gw_v = gw[...]
    back_row = per_row(gw_v * scaled_ref[...].astype(F32)) * to_end
    back_low = jnp.sum(jnp.where(lane < BLK, back_row, 0.0), axis=1, keepdims=True)
    back_high = jnp.sum(jnp.where(lane < BLK, 0.0, back_row), axis=1, keepdims=True)
    grad_scaled = gw_v * end_w + intra[...]
    own_step = per_row(grad_scaled * signal_f)
    gpad[:ROWS, :SIG] = (skip_w * d_f + grad_scaled * step_w) * slope[:, :SIG]

    def sums(cols, source, into, every, at):
        g = gpad[:ROWS, cols]
        for k in range(KSIZE):
            start = EDGE - RIM + k
            row = k * every + at
            into[row : row + 1] = jnp.sum(
                g * pad[start : start + ROWS, source], axis=0, keepdims=True
            )
        row = KSIZE * every + at
        into[row : row + 1] = jnp.sum(g, axis=0, keepdims=True)

    earlier = jnp.where(
        odd == 0, lax.rem(me + n - 2, n), jnp.where(me == n - 1, n - 2, lax.rem(me + 2, n))
    )
    earlier = jnp.where(me == 0, 1, earlier)

    def rim(i, cols):
        copy = remote(
            gpad.at[0:RIMS, cols], rims.at[:, cols], r_sem.at[2 * i], r_sem.at[2 * i + 1],
            ctx=earlier,
        )
        copy.start()
        return copy

    sig_cols, map_cols = slice(0, SIG), slice(SIG, OWN)
    sig_rim = rim(0, sig_cols)
    for q in range(QUADS):
        sums(third(q), third(q), part, QUADS, q)

    planes = n // 2
    y = me // planes
    z = me - y * planes
    z_high = z // 4
    z_low = z - 4 * z_high
    here = 4 * y + z_low
    sent = []

    def to_near(src, dst, at, recv_sem):
        for k in range(1, 8):
            s = lax.rem(here + k, 8)
            d = s // 4 * planes + z_high * 4 + s - s // 4 * 4
            copy = remote(src, dst.at[here], q_send.at[at + k], recv_sem.at[here], ctx=d)
            copy.start()
            sent.append(copy)
        dst[here] = src[...]

    def near_in(src, dst, recv_sem):
        for k in range(1, 8):
            s = lax.rem(here + k, 8)
            remote(src, dst.at[s], q_send.at[k], recv_sem.at[s], ctx=mate).wait_recv()

    def to_far(src, dst, at, recv_sem):
        for k in range(1, 4):
            s = lax.rem(z_high + k, 4)
            d = y * planes + 4 * s + z_low
            copy = remote(src, dst.at[z_high], q_send.at[at + k], recv_sem.at[z_high], ctx=d)
            copy.start()
            sent.append(copy)
        dst[z_high] = src[...]

    def far_in(src, dst, recv_sem):
        for k in range(1, 4):
            s = lax.rem(z_high + k, 4)
            remote(src, dst.at[s], q_send.at[k], recv_sem.at[s], ctx=mate).wait_recv()

    low_part[...] = part[...].astype(BF16)
    to_near(low_part, near, 0, q_near)

    def raw(r, out, taps, cols):
        acc = taps[RIM : RIM + 1] * gpad[r : r + BLK, cols]
        for k in range(RIM):
            acc = acc + taps[k : k + 1] * gpad[r + RIM - k : r + RIM - k + BLK, cols]
        out[:, cols] = acc

    def transposed(i, rim_copy, taps, cols, out):
        rim_copy.wait()
        gpad[ROWS:, cols] = jnp.where(me == 1, 0.0, rims[:, cols])
        raw(BLK, swap, taps, cols)
        away = remote(
            swap.at[:, cols], out.at[pl.ds(kept, BLK)], w_sem.at[2 * i], w_sem.at[2 * i + 1],
            ctx=mate,
        )
        away.start()
        raw(0, stay, taps, cols)
        return away, fetch(i, stay.at[:, cols], out.at[pl.ds(kept, BLK)])

    def h_in(i, _):
        d = other(me, i, n)
        x_copy(d).wait_send()
        remote(yh.at[d], lh.at[mine(d)], hs_sem.at[d], hr_sem.at[d], ctx=d).wait_recv()
        return 0

    lax.fori_loop(1, n, h_in, 0)
    lk[0] = lh[...]
    for h in range(HERE):
        at = slice(h * HDIM, (h + 1) * HDIM)
        lk[1, at, :] = (end_low8[h : h + 1] * lh[at, :].astype(F32) + first_local[at, :]).astype(
            BF16
        )
    for b, rows in enumerate((low, high)):
        mg[1, rows, :] = mg[1, rows, :] + nn(sgrad_ref[rows, :], lk[b])
    to_owner(1)
    end_terms = []
    for b, rows in enumerate((low, high)):
        oh[rows, :] = nt(omap_ref[rows, :], lk[b])
        both = lk[b].astype(F32) * lk[2 + b].astype(F32)
        both = jnp.sum(both.reshape(HERE, HDIM, STATE), axis=1)
        end_terms.append(jnp.sum(both, axis=1, keepdims=True))
    grad_sum = per_row(d_f * exp_w * oh[...]) - back_row + drow[...]
    last_low = back_low + end_low * end_terms[0]
    last_high = back_high + end_high * end_terms[1]
    grad_sum = grad_sum + jnp.where(
        lane == BLK - 1, last_low, jnp.where(lane == ROWS - 1, last_high, 0.0)
    )
    grad_log = nn(grad_sum, lower_f, HIGH)
    grad_step = grad_log * rate + own_step
    grad_dt = grad_step * sigmoid(logits)
    ddt_mine[...] = grad_dt
    ddt_copy = remote(ddt_mine, ddt_got, w_sem.at[0], w_sem.at[1], ctx=mate)
    ddt_copy.start()
    small(0, nt(ones8, grad_log * step, HIGH)[0:1] * (-jnp.exp(alog_ref[...])))
    small(1, nt(ones8, grad_dt, HIGH)[0:1])
    near_in(low_part, near, q_near)
    low_near[...] = jnp.sum(near[...].astype(F32), axis=0).astype(BF16)
    to_far(low_near, far, 7, q_far)

    for k in range(2):

        @pl.when(first + k != f)
        def _():
            remote(
                m_out.at[k], mgot.at[k], ms_sem.at[k], mr_sem.at[k], fsdp=first + k
            ).wait_recv()

    gpad[:ROWS, SIG:] = (mgot[0].astype(F32) + mgot[1].astype(F32)) * slope[:, SIG:]
    map_rim = rim(1, map_cols)
    sums(map_cols, slice(SIG + 2 * STATE, WIDE), part_b, 1, 0)
    to_near(part_b, near_b, 10, q_near_b)
    sig_out = transposed(1, sig_rim, taps_ref, sig_cols, dsig_hbm)
    map_out = transposed(2, map_rim, mtaps_ref, map_cols, dmap_hbm)
    near_in(part_b, near_b, q_near_b)
    sum_b[...] = jnp.sum(near_b[...], axis=0)
    to_far(sum_b, far_b, 17, q_far_b)
    ddt_copy.wait()
    own, got = ddt_mine[...], ddt_got[...]
    ddt_low = jnp.where(odd == 0, own, turned(got))
    ddt_high = jnp.where(odd == 0, got, turned(own))
    ddt_ref[...] = jnp.where(lane < BLK, ddt_low, ddt_high)
    ddt_out = fetch(3, ddt_ref, ddt_hbm)
    far_in(low_near, far, q_far)
    total[...] = jnp.sum(far[...].astype(F32), axis=0)
    sums_out = fetch(4, total, sums_hbm)

    def done(i, _):
        d = other(me, i, n)
        h_copy(d).wait_send()
        c_copy(d).wait_send()
        return 0

    lax.fori_loop(1, n, done, 0)
    for k in range(2):

        @pl.when(group + k * half != f)
        def _():
            m_copy(k).wait_send()

    far_in(sum_b, far_b, q_far_b)
    total_b[...] = jnp.sum(far_b[...], axis=0)
    small_out = fetch(5, total_b, small_hbm)
    for copy in sent:
        copy.wait_send()
    for copy in sig_out + map_out + (ddt_out, sums_out, small_out):
        copy.wait()


def main(*operands):
    n = lax.axis_size("ctx")
    half = lax.axis_size("fsdp") // 2
    share = SIG // n
    dma = pltpu.SemaphoreType.DMA
    vm = pltpu.VMEM
    return pl.pallas_call(
        functools.partial(main_kernel, n, half),
        out_shape=(
            jax.ShapeDtypeStruct((ROWS, SIG), F32),
            jax.ShapeDtypeStruct((ROWS, STATE), F32),
            jax.ShapeDtypeStruct((SUMS, STATE), F32),
            jax.ShapeDtypeStruct((8, STATE), F32),
            jax.ShapeDtypeStruct((HERE, ROWS), F32),
        ),
        in_specs=[pl.BlockSpec(memory_space=pl.ANY)] * len(operands),
        out_specs=(HBM,) * 5,
        scratch_shapes=[
            vm((ROWS, SIG), BF16),
            vm((ROWS, 3 * STATE), BF16),
            vm((ROWS, SIG), BF16),
            vm((HERE, ROWS), F32),
            vm((HERE, ROWS), F32),
            vm((KSIZE, SIG), F32),
            vm((1, SIG), F32),
            vm((KSIZE, STATE), F32),
            vm((1, STATE), F32),
            vm((1, HERE), F32),
            vm((1, HERE), F32),
            vm((1, HERE), F32),
            vm((EDGE, WIDE), BF16),
            vm((EDGE, WIDE), BF16),
            vm((8, STATE), F32),
            vm((2, 8, STATE), F32),
            vm((EDGE + ROWS, WIDE), F32),
            vm((ROWS, OWN), F32),
            vm((ROWS, SIG), BF16),
            vm((ROWS, SIG), BF16),
            vm((ROWS, SIG), BF16),
            vm((ROWS, SIG), BF16),
            vm((ROWS, STATE), BF16),
            vm((ROWS, STATE), BF16),
            vm((ROWS, 3 * SIG), F32),
            vm((ROWS, SIG), F32),
            vm((ROWS, SIG), F32),
            vm((ROWS, SIG), F32),
            vm((HERE, ROWS), F32),
            vm((2, ROWS, STATE), BF16),
            vm((SIG, STATE), BF16),
            vm((n, 3 * share // 2, STATE), BF16),
            vm((HERE, 1, STATE), F32),
            vm((n, share, STATE), BF16),
            vm((n, 3 * share // 2, STATE), BF16),
            vm((n, 1, STATE), F32),
            vm((n, share, STATE), BF16),
            vm((n, 3 * share // 2, STATE), BF16),
            vm((SIG, STATE), BF16),
            vm((n, 3 * share // 2, STATE), BF16),
            vm((SIG, STATE), F32),
            vm((SIG, STATE), F32),
            vm((SIG, STATE), F32),
            vm((4, SIG, STATE), BF16),
            vm((2, ROWS, STATE), F32),
            vm((2, ROWS, STATE), BF16),
            vm((ROWS + RIMS, OWN), F32),
            vm((RIMS, OWN), F32),
            vm((BLK, OWN), F32),
            vm((BLK, OWN), F32),
            vm((HERE, ROWS), F32),
            vm((HERE, ROWS), F32),
            vm((HERE, ROWS), F32),
            vm((SUMS, STATE), F32),
            vm((SUMS, STATE), BF16),
            vm((8, SUMS, STATE), BF16),
            vm((SUMS, STATE), BF16),
            vm((4, SUMS, STATE), BF16),
            vm((SUMS, STATE), F32),
            vm((8, STATE), F32),
            vm((8, 8, STATE), F32),
            vm((8, STATE), F32),
            vm((4, 8, STATE), F32),
            vm((8, STATE), F32),
        ]
        + [dma((17,)), dma((6,)), dma((6,)), dma((3,)), dma((3,)), dma((2,)), dma((2,))]
        + [dma((n,))] * 10
        + [dma((2,)), dma((2,)), dma((4,)), dma((6,)), dma((21,)), dma((8,)), dma((4,)), dma((8,)), dma((4,))],
        compiler_params=pltpu.CompilerParams(
            collective_id=0, has_side_effects=True, vmem_limit_bytes=56 * 1024 * 1024
        ),
        name="main",
    )(*operands)


def last_kernel(
    scale, dsig_in, dmap_in, sums_in, small_in, ddt_in,
    dsig, dmap, ddt, dtaps, dmtaps, dbias, dmbias, dalog, ddtb, dskip
):
    dsig[...] = dsig_in[...]
    dmap[...] = dmap_in[...]
    ddt[...] = ddt_in[...]
    for k in range(KSIZE + 1):
        for q in range(QUADS):
            at = k * QUADS + q
            cols = slice(q * STATE, (q + 1) * STATE)
            row = sums_in[at : at + 1] * scale
            if k < KSIZE:
                dtaps[k : k + 1, cols] = row
            else:
                dbias[:, cols] = row
    dmtaps[...] = small_in[:KSIZE] * scale
    dmbias[...] = small_in[KSIZE : KSIZE + 1] * scale
    for k, out in enumerate((dalog, ddtb, dskip)):
        at = KSIZE + 1 + k
        out[...] = small_in[at : at + 1, :HERE] * scale


def last(*operands):
    scale = 1.0 / math.sqrt(float(lax.axis_size("ctx") * ROWS))
    shapes = (
        (ROWS, SIG), (ROWS, STATE), (HERE, ROWS), (KSIZE, SIG), (KSIZE, STATE),
        (1, SIG), (1, STATE), (1, HERE), (1, HERE), (1, HERE),
    )
    return pl.pallas_call(
        functools.partial(last_kernel, scale),
        out_shape=tuple(jax.ShapeDtypeStruct(s, F32) for s in shapes),
        in_specs=[VM] * 5,
        out_specs=(VM,) * len(shapes),
        compiler_params=pltpu.CompilerParams(vmem_limit_bytes=60 * 1024 * 1024),
        name="last",
    )(*operands)


def shards(
    sig_raw,
    map_raw,
    step_size_logits,
    d_out,
    sig_taps,
    map_taps,
    sig_bias,
    map_bias,
    a_log,
    dt_bias,
    skip_gain,
):
    found = main(
        sig_raw, map_raw, step_size_logits.T, d_out, sig_taps, sig_bias[None, :], map_taps,
        map_bias[None, :], a_log[None, :], dt_bias[None, :], skip_gain[None, :],
    )
    out = last(*found)
    return out[:2] + (out[2].T,) + out[3:5] + tuple(a.reshape(-1) for a in out[5:])


def solution(mesh):
    return jax.shard_map(
        shards,
        mesh=mesh,
        in_specs=(
            P("ctx", "fsdp"),
            P("ctx", None),
            P("ctx", "fsdp"),
            P("ctx", "fsdp"),
            P(None, "fsdp"),
            P(None, "fsdp"),
            P("fsdp"),
            P("fsdp"),
            P("fsdp"),
            P("fsdp"),
            P("fsdp"),
        ),
        out_specs=(
            P("ctx", "fsdp"),
            P("ctx", "fsdp"),
            P("ctx", "fsdp"),
            P(None, "fsdp"),
            P(None, "fsdp"),
            P("fsdp"),
            P("fsdp"),
            P("fsdp"),
            P("fsdp"),
            P("fsdp"),
        ),
        check_vma=False,
    )
```

```python
import functools
import math

import jax
import jax.numpy as jnp
from jax import lax
from jax.experimental import pallas as pl
from jax.experimental.pallas import tpu as pltpu
from jax.sharding import PartitionSpec as P

HEADS = 128
HDIM = 64
STATE = 128
GROUPS = 8
HERE = 8
KSIZE = 4
RIM = KSIZE - 1
BLK = 64
ROWS = 2 * BLK
SIG = HERE * HDIM
WIDE = SIG + 3 * STATE
OWN = SIG + STATE
EDGE = 16
RIMS = 8
QUADS = SIG // STATE
SUMS = 24
FINE = 10
MESH = pl.DeviceIdType.MESH
VM = pl.BlockSpec(memory_space=pltpu.VMEM)
HBM = pl.BlockSpec(memory_space=pltpu.HBM)
HIGH = lax.Precision.HIGHEST
F32 = jnp.float32
BF16 = jnp.bfloat16


def signal(sem, **where):
    pl.semaphore_signal(sem, inc=1, device_id=where, device_id_type=MESH)


def remote(src, dst, send_sem, recv_sem, **where):
    return pltpu.make_async_remote_copy(
        src_ref=src,
        dst_ref=dst,
        send_sem=send_sem,
        recv_sem=recv_sem,
        device_id=where,
        device_id_type=MESH,
    )


def other(me, i, n):
    off = jnp.where(lax.rem(i, 2) == 1, (i + 1) // 2, n - i // 2)
    return lax.rem(me + off, n)


def columns(start):
    return pl.ds(pl.multiple_of(start * STATE, STATE), STATE)


def nn(a, b, precision=None):
    return lax.dot_general(
        a, b, (((1,), (0,)), ((), ())), precision=precision, preferred_element_type=F32
    )


def nt(a, b, precision=None):
    return lax.dot_general(
        a, b, (((1,), (1,)), ((), ())), precision=precision, preferred_element_type=F32
    )


def tn(a, b):
    return lax.dot_general(a, b, (((0,), (0,)), ((), ())), preferred_element_type=F32)


def sigmoid(v):
    return 1.0 / (1.0 + jnp.exp(-v))


def log1p_small(e):
    series = e * (
        1.0 + e * (-1.0 / 2 + e * (1.0 / 3 + e * (-1.0 / 4 + e * (1.0 / 5 + e * (-1.0 / 6)))))
    )
    return jnp.where(e < 0.03, series, jnp.log(1.0 + e))


def pack(v):
    n, rows, _ = v.shape
    high = v.astype(BF16)
    value = high.astype(F32)
    tiny = jnp.abs(value) < 1e-30
    ratio = jnp.where(tiny, 0.0, (v - value) / jnp.where(tiny, 1.0, value))
    steps = jnp.clip(jnp.round(ratio * (256.0 * FINE)), -FINE, FINE)
    both = steps[:, : rows // 2] * (2.0 * FINE + 1.0) + steps[:, rows // 2 :]
    return high, both.astype(BF16)


def unpack(high, both):
    value = high.astype(F32)
    both = both.astype(F32)
    first = jnp.floor((both + (FINE + 0.5)) * (1.0 / (2.0 * FINE + 1.0)))
    second = both - first * (2.0 * FINE + 1.0)
    steps = jnp.concatenate([first, second], axis=-2)
    return value + value * steps * (1.0 / (256.0 * FINE))


def main_kernel(
    n, half, sig_hbm, map_hbm, dt_hbm, dout_hbm, taps_hbm, bias_hbm, mtaps_hbm, mbias_hbm,
    alog_hbm, dtb_hbm, skip_hbm,
    dsig_hbm, dmap_hbm, sums_hbm, small_hbm, ddt_hbm,
    sig_in, map_in, dout_ref, dt_in, dt_got, taps_ref, bias_ref, mtaps_ref, mbias_ref,
    alog_ref, dtb_ref, skip_ref, tail_own, tail_got, tap_row, gtaps_ref,
    pad, slope, signal_ref, scaled_ref, weighted_ref, sgrad_ref, imap_ref, omap_ref, wide3, intra,
    oh, gw, drow, m_out, xs, gs, es, xr, gr, er, yh, yc, lh, lc, first_local, first_sg, second_sg, lk,
    mg, mgot, gpad, rims, swap, stay, ddt_mine, ddt_got, ddt_ref,
    part, low_part, near, low_near, far, total, part_b, near_b, sum_b, far_b, total_b,
    l_sem, n_send, n_recv, b_send, b_recv, tap_send, tap_recv,
    xs_sem, xr_sem, gs_sem, gr_sem, es_sem, er_sem, hs_sem, hr_sem, cs_sem, cr_sem,
    ms_sem, mr_sem, r_sem, w_sem, q_send, q_near, q_far, q_near_b, q_far_b
):
    me = lax.axis_index("ctx")
    f = lax.axis_index("fsdp")
    odd = lax.rem(me, 2)
    mate = me + 1 - 2 * odd
    side_ctx = lax.rem(me + n - 1 + 2 * odd, n)
    slot = f // half
    first = 2 * (f - slot * half)
    group = f // 2
    side = f - 2 * group
    share = SIG // n
    per_head = n // HERE
    kept = pl.multiple_of(odd * BLK, BLK)
    given = pl.multiple_of((1 - odd) * BLK, BLK)
    ending = pl.multiple_of((1 - odd) * BLK + BLK - EDGE, EDGE)
    starts = (group, GROUPS + group, f)
    barrier = pltpu.get_barrier_semaphore()

    for i in range(1, n):
        signal(barrier, ctx=lax.rem(me + (i + 1) // 2 if i % 2 else me + n - i // 2, n))
    for k in range(2):

        @pl.when(group + k * half != f)
        def _():
            signal(barrier, fsdp=group + k * half)

        @pl.when(first + k != f)
        def _():
            signal(barrier, fsdp=first + k)

    def fetch(i, src, dst):
        copy = pltpu.make_async_copy(src, dst, l_sem.at[i])
        copy.start()
        return copy

    def third(k):
        return slice(k * STATE, (k + 1) * STATE)

    local = [
        fetch(0, mtaps_hbm, mtaps_ref),
        fetch(1, mbias_hbm, mbias_ref),
        fetch(2, dt_hbm, dt_in),
        fetch(3, alog_hbm, alog_ref),
        fetch(4, dtb_hbm, dtb_ref),
        fetch(5, skip_hbm, skip_ref),
        fetch(6, taps_hbm, taps_ref),
        fetch(7, bias_hbm, bias_ref),
        fetch(8, sig_hbm.at[pl.ds(kept, BLK)], sig_in.at[0:BLK]),
        fetch(9, dout_hbm.at[pl.ds(kept, BLK)], dout_ref.at[0:BLK]),
        fetch(10, sig_hbm.at[pl.ds(ending, EDGE)], tail_own.at[:, 0:SIG]),
    ]
    for k, start in enumerate(starts):
        local.append(
            fetch(
                11 + k,
                map_hbm.at[pl.ds(kept, BLK), columns(start)],
                map_in.at[0:BLK, third(k)],
            )
        )
        local.append(
            fetch(
                14 + k,
                map_hbm.at[pl.ds(ending, EDGE), columns(start)],
                tail_own.at[:, SIG + k * STATE : SIG + (k + 1) * STATE],
            )
        )

    tap_row[KSIZE + 1 :] = jnp.zeros((8 - KSIZE - 1, STATE), F32)
    selves = jnp.where(group == f, 1, 0) + jnp.where(group + half == f, 1, 0)
    pl.semaphore_wait(barrier, n - 1 + 4 - 2 * selves)

    def to_mate(i, src, dst):
        copy = remote(src, dst, n_send.at[i], n_recv.at[i], ctx=mate)
        copy.start()
        return copy

    def map_copy(k):
        return to_mate(
            1 + k, map_hbm.at[pl.ds(given, BLK), columns(starts[k])], map_in.at[BLK:ROWS, third(k)]
        )

    dt_copy = to_mate(0, dt_hbm, dt_got)
    out_copy = map_copy(1)
    dout_copy = to_mate(5, dout_hbm.at[pl.ds(given, BLK)], dout_ref.at[BLK:ROWS])
    for copy in local:
        copy.wait()
    tap_row[0:KSIZE] = mtaps_ref[...]
    tap_row[KSIZE : KSIZE + 1] = mbias_ref[...]
    for k in range(2):

        @pl.when(first + k != f)
        def _():
            remote(
                tap_row, gtaps_ref.at[slot], tap_send.at[k], tap_recv.at[slot], fsdp=first + k
            ).start()

        @pl.when(group + k * half == f)
        def _():
            gtaps_ref[k] = tap_row[...]

    def to_side(i, dst_cols):
        copy = remote(
            tail_own.at[:, dst_cols], tail_got.at[:, dst_cols], b_send.at[i], b_recv.at[i],
            ctx=side_ctx,
        )
        copy.start()
        return copy

    out_cols = slice(SIG + STATE, SIG + 2 * STATE)
    out_tail = to_side(0, out_cols)
    tails = [to_side(1, slice(0, SIG + STATE)), to_side(2, slice(SIG + 2 * STATE, WIDE))]
    map_copies = [map_copy(0), map_copy(2)]
    sig_copy = to_mate(4, sig_hbm.at[pl.ds(given, BLK)], sig_in.at[BLK:ROWS])

    lane = lax.broadcasted_iota(jnp.int32, (HERE, ROWS), 1)
    row_id = lax.broadcasted_iota(jnp.int32, (ROWS, ROWS), 0)
    col_id = lax.broadcasted_iota(jnp.int32, (ROWS, ROWS), 1)
    lower = ((row_id >= BLK) == (col_id >= BLK)) & (col_id <= row_id)
    lower_f = jnp.where(lower, 1.0, 0.0).astype(F32)
    eye = jnp.where(row_id == col_id, 1.0, 0.0).astype(F32)
    eye8 = eye[:HERE, :HERE]
    ones8 = jnp.ones((HERE, ROWS), F32)
    head3 = lax.broadcasted_iota(jnp.int32, (3 * HERE, 3 * SIG), 0)
    spread3 = jnp.where(
        lax.broadcasted_iota(jnp.int32, (3 * HERE, 3 * SIG), 1) // HDIM == head3, 1.0, 0.0
    ).astype(F32)
    spread1 = spread3[:HERE, :SIG]

    def in_rows(ref):
        return nt(eye8, jnp.broadcast_to(ref[...], (ROWS, HERE)), HIGH)

    def per_row(y):
        return nt(spread1, y, HIGH)

    def turned(x):
        return pltpu.roll(x, BLK, 1)

    def preact(r, rows, cols, taps, bias):
        acc = bias
        for k in range(KSIZE):
            start = EDGE - RIM + k + r
            acc = acc + taps[k : k + 1] * pad[start : start + rows, cols]
        return acc

    def sig_rows(r, count):
        rows = slice(r, r + count)
        for q in range(SIG // STATE):
            cols = third(q)
            v = preact(r, count, cols, taps_ref[:, cols], bias_ref[:, cols])
            s = sigmoid(v)
            slope[rows, cols] = s * (1.0 + v * (1.0 - s))
            signal_ref[rows, cols] = (v * s).astype(BF16)

    pad[EDGE : EDGE + BLK, :SIG] = sig_in[:BLK, :].astype(F32)
    pad[EDGE : EDGE + BLK, SIG:] = map_in[:BLK, :].astype(F32)
    keep = jnp.where(me == 0, 0.0, 1.0).astype(F32)

    def before(cols):
        mine_then = tail_own[:, cols].astype(F32)
        pad[:EDGE, cols] = keep * jnp.where(me == n - 1, mine_then, tail_got[:, cols].astype(F32))

    dt_copy.wait()
    own, got = dt_in[...], dt_got[...]
    own = jnp.where(odd == 0, own, turned(own))
    got = jnp.where(odd == 0, turned(got), got)
    logits = jnp.where(lane < BLK, own, got) + in_rows(dtb_ref)
    rate = -jnp.exp(in_rows(alog_ref))
    step = jnp.maximum(logits, 0.0) + log1p_small(jnp.exp(-jnp.abs(logits)))
    ds = nt(step * rate, lower_f, HIGH)
    end_low = jnp.exp(ds[:, BLK - 1 : BLK])
    end_high = jnp.exp(ds[:, ROWS - 1 : ROWS])
    end = jnp.where(lane < BLK, ds[:, BLK - 1 : BLK], ds[:, ROWS - 1 : ROWS])
    to_end = jnp.exp(end - ds)
    col4 = nt(eye, jnp.concatenate([step, to_end, jnp.exp(ds), ds], axis=0), HIGH)
    ds_col = col4[:, 3 * HERE :]
    wide3[:, 2 * SIG :] = nn(col4[:, 2 * HERE : 3 * HERE], spread1, HIGH)
    end_low8 = jnp.broadcast_to(end_low, (HERE, STATE))
    end_high8 = jnp.broadcast_to(end_high, (HERE, STATE))
    both_ends = end_low8 * end_high8
    for h in range(HERE):
        es[h] = both_ends[h : h + 1]

    def e_copy(d):
        return remote(es.at[d // per_head], er.at[me], es_sem.at[d], er_sem.at[me], ctx=d)

    def send_ends(i, _):
        e_copy(other(me, i, n)).start()
        return 0

    lax.fori_loop(1, n, send_ends, 0)
    er[me] = es[me // per_head]

    for k in range(2):

        @pl.when(group + k * half != f)
        def _():
            remote(
                tap_row, gtaps_ref.at[k], tap_send.at[k], tap_recv.at[k], fsdp=group + k * half
            ).wait_recv()

        @pl.when(first + k != f)
        def _():
            remote(
                tap_row, gtaps_ref.at[slot], tap_send.at[k], tap_recv.at[slot], fsdp=first + k
            ).wait_send()

    out_tail.wait()
    before(out_cols)
    def map_rows(k, out, r, count):
        cols = slice(SIG + k * STATE, SIG + (k + 1) * STATE)
        v = preact(r, count, cols, gtaps_ref[k, :KSIZE], gtaps_ref[k, KSIZE : KSIZE + 1])
        out[r : r + count, :] = (v * sigmoid(v)).astype(BF16)

    def sgrad_rows(rows):
        for q in range(QUADS):
            cols3 = slice(2 * SIG + q * STATE, 2 * SIG + (q + 1) * STATE)
            grad = dout_ref[rows, third(q)].astype(F32) * wide3[rows, cols3]
            sgrad_ref[rows, third(q)] = grad.astype(BF16)
        return tn(sgrad_ref[rows, :], omap_ref[rows, :])

    def mine(d):
        return pl.ds(pl.multiple_of(d * share, share), share)

    def x_copy(d):
        return remote(xs.at[mine(d)], xr.at[me], xs_sem.at[d], xr_sem.at[me], ctx=d)

    def g_copy(d):
        return remote(gs.at[d], gr.at[me], gs_sem.at[d], gr_sem.at[me], ctx=d)

    def h_copy(d):
        return remote(yh.at[d], lh.at[mine(me)], hs_sem.at[d], hr_sem.at[me], ctx=d)

    def c_copy(d):
        return remote(yc.at[d], lc.at[me], cs_sem.at[d], cr_sem.at[me], ctx=d)

    def send_g(i, _):
        g_copy(other(me, i, n)).start()
        return 0

    def send_x(i, _):
        x_copy(other(me, i, n)).start()
        return 0

    low, high = slice(0, BLK), slice(BLK, ROWS)
    map_rows(1, omap_ref, 0, BLK)
    first_sg[...] = sgrad_rows(low)
    out_copy.wait()
    pad[EDGE + BLK :, out_cols] = map_in[BLK:, third(1)].astype(F32)
    map_rows(1, omap_ref, BLK, BLK)
    dout_copy.wait()
    second_sg[...] = sgrad_rows(high)
    for h in range(HERE):
        at = slice(h * HDIM, (h + 1) * HDIM)
        link = first_sg[at, :] + end_low8[h : h + 1] * second_sg[at, :]
        top, rest = pack(link.reshape(per_head, share, STATE))
        gs[h * per_head : (h + 1) * per_head, :share, :] = top
        gs[h * per_head : (h + 1) * per_head, share:, :] = rest
    lax.fori_loop(1, n, send_g, 0)
    gr[me] = gs[me]

    wide3[:, : 2 * SIG] = nn(col4[:, : 2 * HERE], spread3[: 2 * HERE, : 2 * SIG], HIGH)
    for copy in tails + map_copies:
        copy.wait()
    for cols in (slice(0, SIG + STATE), slice(SIG + 2 * STATE, WIDE)):
        before(cols)
    pad[EDGE + BLK :, SIG : SIG + STATE] = map_in[BLK:, third(0)].astype(F32)
    pad[EDGE + BLK :, SIG + 2 * STATE :] = map_in[BLK:, third(2)].astype(F32)
    map_rows(0, imap_ref, 0, ROWS)
    v = preact(0, ROWS, slice(SIG + 2 * STATE, WIDE), mtaps_ref[...], mbias_ref[...])
    s = sigmoid(v)
    slope[:, SIG:] = s * (1.0 + v * (1.0 - s))
    sig_copy.wait()
    pad[EDGE + BLK :, :SIG] = sig_in[BLK:, :].astype(F32)
    sig_rows(0, ROWS)
    for q in range(QUADS):
        cols = third(q)
        cols2 = slice(SIG + q * STATE, SIG + (q + 1) * STATE)
        scaled_b = (signal_ref[:, cols].astype(F32) * wide3[:, cols]).astype(BF16)
        scaled_ref[:, cols] = scaled_b
        weighted_ref[:, cols] = (scaled_b.astype(F32) * wide3[:, cols2]).astype(BF16)
    first_local[...] = tn(weighted_ref[low, :], imap_ref[low, :])
    second_local = tn(weighted_ref[high, :], imap_ref[high, :])
    for h in range(HERE):
        at = slice(h * HDIM, (h + 1) * HDIM)
        xs[at, :] = (end_high8[h : h + 1] * first_local[at, :] + second_local[at, :]).astype(BF16)
    lax.fori_loop(1, n, send_x, 0)
    xr[me] = xs[mine(me)]

    score = nt(omap_ref[...], imap_ref[...])
    lane_row = lax.broadcasted_iota(jnp.int32, (ROWS, STATE), 1)
    grad_score = jnp.zeros((ROWS, ROWS), F32)
    for q in range(HERE // 2):
        cols = third(q)
        d_pair = dout_ref[:, cols].astype(F32)
        d_two = jnp.concatenate(
            [jnp.where(lane_row < HDIM, d_pair, 0.0), jnp.where(lane_row < HDIM, 0.0, d_pair)],
            axis=0,
        ).astype(BF16)
        grad_mix2 = nt(d_two, scaled_ref[:, cols])
        mixes = []
        for k in range(2):
            h = 2 * q + k
            grad_mix = grad_mix2[k * ROWS : (k + 1) * ROWS]
            gap = jnp.minimum(ds_col[:, h : h + 1] - ds[h : h + 1, :], 0.0)
            decay = jnp.where(lower, jnp.exp(gap), 0.0)
            mix = score * decay
            mixes.append(mix.astype(BF16))
            grad_score = grad_score + grad_mix * decay
            product = grad_mix * mix
            drow[h : h + 1, :] = nt(ones8, product, HIGH)[0:1] - jnp.sum(
                product, axis=0, keepdims=True
            )
        intra[:, cols] = tn(jnp.concatenate(mixes, axis=0), d_two)
    grad_score = grad_score.astype(BF16)
    mg[0] = tn(grad_score, omap_ref[...])
    mg[1] = nn(grad_score, imap_ref[...])

    def holder(i):
        return jnp.where(i < n // 2, 2 * i, 2 * (n - 1 - i) + 1)

    zero = jnp.zeros((share, STATE), F32)

    def g_arrived(i, _):
        s = other(me, i, n)
        remote(es.at[s // per_head], er.at[s], es_sem.at[s], er_sem.at[s], ctx=s).wait_recv()
        remote(gs.at[s], gr.at[s], gs_sem.at[s], gr_sem.at[s], ctx=s).wait_recv()
        return 0

    def to_front(i, g):
        at = holder(n - 1 - i)
        top, rest = pack(g[None])
        yc[at, :share, :] = top[0]
        yc[at, share:, :] = rest[0]
        got = gr[at]
        return er[at] * g + unpack(got[:share], got[share:])

    def send_c(i, _):
        c_copy(other(me, i, n)).start()
        return 0

    def x_arrived(i, _):
        s = other(me, i, n)
        remote(xs.at[mine(s)], xr.at[s], xs_sem.at[s], xr_sem.at[s], ctx=s).wait_recv()
        return 0

    def to_back(i, h):
        at = holder(i)
        yh[at] = h.astype(BF16)
        return er[at] * h + xr[at].astype(F32)

    def send_h(i, _):
        h_copy(other(me, i, n)).start()
        return 0

    lax.fori_loop(1, n, g_arrived, 0)
    lax.fori_loop(0, n, to_front, zero, unroll=4)
    lax.fori_loop(1, n, send_c, 0)
    lax.fori_loop(1, n, x_arrived, 0)
    lax.fori_loop(0, n, to_back, zero, unroll=4)
    lax.fori_loop(1, n, send_h, 0)
    lh[mine(me)] = yh[me]
    lc[me] = yc[me]
    step_w = wide3[:, :SIG]
    end_w = wide3[:, SIG : 2 * SIG]
    exp_w = wide3[:, 2 * SIG :]
    d_f = dout_ref[...].astype(F32)
    signal_f = signal_ref[...].astype(F32)
    skip_w = nn(jnp.broadcast_to(skip_ref[...], (HERE, HERE)), spread1, HIGH)[0:1]
    part[(KSIZE + 1) * QUADS :] = jnp.zeros((SUMS - (KSIZE + 1) * QUADS, STATE), F32)

    def small(at, row):
        at = KSIZE + 1 + at
        part_b[at : at + 1] = jnp.concatenate([row, jnp.zeros((1, STATE - HERE), F32)], axis=1)

    small(2, nt(ones8, per_row(d_f * signal_f), HIGH)[0:1])

    def m_copy(k):
        return remote(
            m_out.at[k], mgot.at[side], ms_sem.at[k], mr_sem.at[side], fsdp=group + k * half
        )

    def to_owner(k):
        m_out[k] = mg[k].astype(BF16)

        @pl.when(group + k * half != f)
        def _():
            m_copy(k).start()

        @pl.when(group + k * half == f)
        def _():
            mgot[side] = m_out[k]

    def c_in(i, _):
        d = other(me, i, n)
        g_copy(d).wait_send()
        e_copy(d).wait_send()
        remote(yc.at[d], lc.at[d], cs_sem.at[d], cr_sem.at[d], ctx=d).wait_recv()
        return 0

    lax.fori_loop(1, n, c_in, 0)
    for h in range(HERE):
        at = slice(h * HDIM, (h + 1) * HDIM)
        got = lc[h * per_head : (h + 1) * per_head]
        state = unpack(got[:, :share], got[:, share:]).reshape(HDIM, STATE)
        lk[3, at, :] = state.astype(BF16)
        lk[2, at, :] = (second_sg[at, :] + end_high8[h : h + 1] * state).astype(BF16)
    for b, rows in enumerate((low, high)):
        mg[0, rows, :] = mg[0, rows, :] + nn(weighted_ref[rows, :], lk[2 + b])
    to_owner(0)
    for b, rows in enumerate((low, high)):
        gw[rows, :] = nt(imap_ref[rows, :], lk[2 + b])
    gw_v = gw[...]
    back_row = per_row(gw_v * scaled_ref[...].astype(F32)) * to_end
    back_low = jnp.sum(jnp.where(lane < BLK, back_row, 0.0), axis=1, keepdims=True)
    back_high = jnp.sum(jnp.where(lane < BLK, 0.0, back_row), axis=1, keepdims=True)
    grad_scaled = gw_v * end_w + intra[...]
    own_step = per_row(grad_scaled * signal_f)
    gpad[:ROWS, :SIG] = (skip_w * d_f + grad_scaled * step_w) * slope[:, :SIG]

    def sums(cols, source, into, every, at):
        g = gpad[:ROWS, cols]
        for k in range(KSIZE):
            start = EDGE - RIM + k
            row = k * every + at
            into[row : row + 1] = jnp.sum(
                g * pad[start : start + ROWS, source], axis=0, keepdims=True
            )
        row = KSIZE * every + at
        into[row : row + 1] = jnp.sum(g, axis=0, keepdims=True)

    earlier = jnp.where(
        odd == 0, lax.rem(me + n - 2, n), jnp.where(me == n - 1, n - 2, lax.rem(me + 2, n))
    )
    earlier = jnp.where(me == 0, 1, earlier)

    def rim(i, cols):
        copy = remote(
            gpad.at[0:RIMS, cols], rims.at[:, cols], r_sem.at[2 * i], r_sem.at[2 * i + 1],
            ctx=earlier,
        )
        copy.start()
        return copy

    sig_cols, map_cols = slice(0, SIG), slice(SIG, OWN)
    sig_rim = rim(0, sig_cols)
    for q in range(QUADS):
        sums(third(q), third(q), part, QUADS, q)

    planes = n // 2
    y = me // planes
    z = me - y * planes
    z_high = z // 4
    z_low = z - 4 * z_high
    here = 4 * y + z_low
    sent = []

    def to_near(src, dst, at, recv_sem):
        for k in range(1, 8):
            s = lax.rem(here + k, 8)
            d = s // 4 * planes + z_high * 4 + s - s // 4 * 4
            copy = remote(src, dst.at[here], q_send.at[at + k], recv_sem.at[here], ctx=d)
            copy.start()
            sent.append(copy)
        dst[here] = src[...]

    def near_in(src, dst, recv_sem):
        for k in range(1, 8):
            s = lax.rem(here + k, 8)
            remote(src, dst.at[s], q_send.at[k], recv_sem.at[s], ctx=mate).wait_recv()

    def to_far(src, dst, at, recv_sem):
        for k in range(1, 4):
            s = lax.rem(z_high + k, 4)
            d = y * planes + 4 * s + z_low
            copy = remote(src, dst.at[z_high], q_send.at[at + k], recv_sem.at[z_high], ctx=d)
            copy.start()
            sent.append(copy)
        dst[z_high] = src[...]

    def far_in(src, dst, recv_sem):
        for k in range(1, 4):
            s = lax.rem(z_high + k, 4)
            remote(src, dst.at[s], q_send.at[k], recv_sem.at[s], ctx=mate).wait_recv()

    low_part[...] = part[...].astype(BF16)
    to_near(low_part, near, 0, q_near)

    def raw(r, out, taps, cols):
        acc = taps[RIM : RIM + 1] * gpad[r : r + BLK, cols]
        for k in range(RIM):
            acc = acc + taps[k : k + 1] * gpad[r + RIM - k : r + RIM - k + BLK, cols]
        out[:, cols] = acc

    def transposed(i, rim_copy, taps, cols, out):
        rim_copy.wait()
        gpad[ROWS:, cols] = jnp.where(me == 1, 0.0, rims[:, cols])
        raw(BLK, swap, taps, cols)
        away = remote(
            swap.at[:, cols], out.at[pl.ds(kept, BLK)], w_sem.at[2 * i], w_sem.at[2 * i + 1],
            ctx=mate,
        )
        away.start()
        raw(0, stay, taps, cols)
        return away, fetch(i, stay.at[:, cols], out.at[pl.ds(kept, BLK)])

    def h_in(i, _):
        d = other(me, i, n)
        x_copy(d).wait_send()
        remote(yh.at[d], lh.at[mine(d)], hs_sem.at[d], hr_sem.at[d], ctx=d).wait_recv()
        return 0

    lax.fori_loop(1, n, h_in, 0)
    lk[0] = lh[...]
    for h in range(HERE):
        at = slice(h * HDIM, (h + 1) * HDIM)
        lk[1, at, :] = (end_low8[h : h + 1] * lh[at, :].astype(F32) + first_local[at, :]).astype(
            BF16
        )
    for b, rows in enumerate((low, high)):
        mg[1, rows, :] = mg[1, rows, :] + nn(sgrad_ref[rows, :], lk[b])
    to_owner(1)
    end_terms = []
    for b, rows in enumerate((low, high)):
        oh[rows, :] = nt(omap_ref[rows, :], lk[b])
        both = lk[b].astype(F32) * lk[2 + b].astype(F32)
        both = jnp.sum(both.reshape(HERE, HDIM, STATE), axis=1)
        end_terms.append(jnp.sum(both, axis=1, keepdims=True))
    grad_sum = per_row(d_f * exp_w * oh[...]) - back_row + drow[...]
    last_low = back_low + end_low * end_terms[0]
    last_high = back_high + end_high * end_terms[1]
    grad_sum = grad_sum + jnp.where(
        lane == BLK - 1, last_low, jnp.where(lane == ROWS - 1, last_high, 0.0)
    )
    grad_log = nn(grad_sum, lower_f, HIGH)
    grad_step = grad_log * rate + own_step
    grad_dt = grad_step * sigmoid(logits)
    ddt_mine[...] = grad_dt
    ddt_copy = remote(ddt_mine, ddt_got, w_sem.at[0], w_sem.at[1], ctx=mate)
    ddt_copy.start()
    small(0, nt(ones8, grad_log * step, HIGH)[0:1] * (-jnp.exp(alog_ref[...])))
    small(1, nt(ones8, grad_dt, HIGH)[0:1])
    near_in(low_part, near, q_near)
    low_near[...] = jnp.sum(near[...].astype(F32), axis=0).astype(BF16)
    to_far(low_near, far, 7, q_far)

    for k in range(2):

        @pl.when(first + k != f)
        def _():
            remote(
                m_out.at[k], mgot.at[k], ms_sem.at[k], mr_sem.at[k], fsdp=first + k
            ).wait_recv()

    gpad[:ROWS, SIG:] = (mgot[0].astype(F32) + mgot[1].astype(F32)) * slope[:, SIG:]
    map_rim = rim(1, map_cols)
    sums(map_cols, slice(SIG + 2 * STATE, WIDE), part_b, 1, 0)
    to_near(part_b, near_b, 10, q_near_b)
    sig_out = transposed(1, sig_rim, taps_ref, sig_cols, dsig_hbm)
    map_out = transposed(2, map_rim, mtaps_ref, map_cols, dmap_hbm)
    near_in(part_b, near_b, q_near_b)
    sum_b[...] = jnp.sum(near_b[...], axis=0)
    to_far(sum_b, far_b, 17, q_far_b)
    ddt_copy.wait()
    own, got = ddt_mine[...], ddt_got[...]
    ddt_low = jnp.where(odd == 0, own, turned(got))
    ddt_high = jnp.where(odd == 0, got, turned(own))
    ddt_ref[...] = jnp.where(lane < BLK, ddt_low, ddt_high)
    ddt_out = fetch(3, ddt_ref, ddt_hbm)
    far_in(low_near, far, q_far)
    total[...] = jnp.sum(far[...].astype(F32), axis=0)
    sums_out = fetch(4, total, sums_hbm)

    def done(i, _):
        d = other(me, i, n)
        h_copy(d).wait_send()
        c_copy(d).wait_send()
        return 0

    lax.fori_loop(1, n, done, 0)
    for k in range(2):

        @pl.when(group + k * half != f)
        def _():
            m_copy(k).wait_send()

    far_in(sum_b, far_b, q_far_b)
    total_b[...] = jnp.sum(far_b[...], axis=0)
    small_out = fetch(5, total_b, small_hbm)
    for copy in sent:
        copy.wait_send()
    for copy in sig_out + map_out + (ddt_out, sums_out, small_out):
        copy.wait()


def main(*operands):
    n = lax.axis_size("ctx")
    half = lax.axis_size("fsdp") // 2
    share = SIG // n
    dma = pltpu.SemaphoreType.DMA
    vm = pltpu.VMEM
    return pl.pallas_call(
        functools.partial(main_kernel, n, half),
        out_shape=(
            jax.ShapeDtypeStruct((ROWS, SIG), F32),
            jax.ShapeDtypeStruct((ROWS, STATE), F32),
            jax.ShapeDtypeStruct((SUMS, STATE), F32),
            jax.ShapeDtypeStruct((8, STATE), F32),
            jax.ShapeDtypeStruct((HERE, ROWS), F32),
        ),
        in_specs=[pl.BlockSpec(memory_space=pl.ANY)] * len(operands),
        out_specs=(HBM,) * 5,
        scratch_shapes=[
            vm((ROWS, SIG), BF16),
            vm((ROWS, 3 * STATE), BF16),
            vm((ROWS, SIG), BF16),
            vm((HERE, ROWS), F32),
            vm((HERE, ROWS), F32),
            vm((KSIZE, SIG), F32),
            vm((1, SIG), F32),
            vm((KSIZE, STATE), F32),
            vm((1, STATE), F32),
            vm((1, HERE), F32),
            vm((1, HERE), F32),
            vm((1, HERE), F32),
            vm((EDGE, WIDE), BF16),
            vm((EDGE, WIDE), BF16),
            vm((8, STATE), F32),
            vm((2, 8, STATE), F32),
            vm((EDGE + ROWS, WIDE), F32),
            vm((ROWS, OWN), F32),
            vm((ROWS, SIG), BF16),
            vm((ROWS, SIG), BF16),
            vm((ROWS, SIG), BF16),
            vm((ROWS, SIG), BF16),
            vm((ROWS, STATE), BF16),
            vm((ROWS, STATE), BF16),
            vm((ROWS, 3 * SIG), F32),
            vm((ROWS, SIG), F32),
            vm((ROWS, SIG), F32),
            vm((ROWS, SIG), F32),
            vm((HERE, ROWS), F32),
            vm((2, ROWS, STATE), BF16),
            vm((SIG, STATE), BF16),
            vm((n, 3 * share // 2, STATE), BF16),
            vm((HERE, 1, STATE), F32),
            vm((n, share, STATE), BF16),
            vm((n, 3 * share // 2, STATE), BF16),
            vm((n, 1, STATE), F32),
            vm((n, share, STATE), BF16),
            vm((n, 3 * share // 2, STATE), BF16),
            vm((SIG, STATE), BF16),
            vm((n, 3 * share // 2, STATE), BF16),
            vm((SIG, STATE), F32),
            vm((SIG, STATE), F32),
            vm((SIG, STATE), F32),
            vm((4, SIG, STATE), BF16),
            vm((2, ROWS, STATE), F32),
            vm((2, ROWS, STATE), BF16),
            vm((ROWS + RIMS, OWN), F32),
            vm((RIMS, OWN), F32),
            vm((BLK, OWN), F32),
            vm((BLK, OWN), F32),
            vm((HERE, ROWS), F32),
            vm((HERE, ROWS), F32),
            vm((HERE, ROWS), F32),
            vm((SUMS, STATE), F32),
            vm((SUMS, STATE), BF16),
            vm((8, SUMS, STATE), BF16),
            vm((SUMS, STATE), BF16),
            vm((4, SUMS, STATE), BF16),
            vm((SUMS, STATE), F32),
            vm((8, STATE), F32),
            vm((8, 8, STATE), F32),
            vm((8, STATE), F32),
            vm((4, 8, STATE), F32),
            vm((8, STATE), F32),
        ]
        + [dma((17,)), dma((6,)), dma((6,)), dma((3,)), dma((3,)), dma((2,)), dma((2,))]
        + [dma((n,))] * 10
        + [dma((2,)), dma((2,)), dma((4,)), dma((6,)), dma((21,)), dma((8,)), dma((4,)), dma((8,)), dma((4,))],
        compiler_params=pltpu.CompilerParams(
            collective_id=0, has_side_effects=True, vmem_limit_bytes=56 * 1024 * 1024
        ),
        name="main",
    )(*operands)


def last_kernel(
    scale, dsig_in, dmap_in, sums_in, small_in, ddt_in,
    dsig, dmap, ddt, dtaps, dmtaps, dbias, dmbias, dalog, ddtb, dskip
):
    dsig[...] = dsig_in[...]
    dmap[...] = dmap_in[...]
    ddt[...] = ddt_in[...]
    for k in range(KSIZE + 1):
        for q in range(QUADS):
            at = k * QUADS + q
            cols = slice(q * STATE, (q + 1) * STATE)
            row = sums_in[at : at + 1] * scale
            if k < KSIZE:
                dtaps[k : k + 1, cols] = row
            else:
                dbias[:, cols] = row
    dmtaps[...] = small_in[:KSIZE] * scale
    dmbias[...] = small_in[KSIZE : KSIZE + 1] * scale
    for k, out in enumerate((dalog, ddtb, dskip)):
        at = KSIZE + 1 + k
        out[...] = small_in[at : at + 1, :HERE] * scale


def last(*operands):
    scale = 1.0 / math.sqrt(float(lax.axis_size("ctx") * ROWS))
    shapes = (
        (ROWS, SIG), (ROWS, STATE), (HERE, ROWS), (KSIZE, SIG), (KSIZE, STATE),
        (1, SIG), (1, STATE), (1, HERE), (1, HERE), (1, HERE),
    )
    return pl.pallas_call(
        functools.partial(last_kernel, scale),
        out_shape=tuple(jax.ShapeDtypeStruct(s, F32) for s in shapes),
        in_specs=[VM] * 5,
        out_specs=(VM,) * len(shapes),
        compiler_params=pltpu.CompilerParams(vmem_limit_bytes=60 * 1024 * 1024),
        name="last",
    )(*operands)


def shards(
    sig_raw,
    map_raw,
    step_size_logits,
    d_out,
    sig_taps,
    map_taps,
    sig_bias,
    map_bias,
    a_log,
    dt_bias,
    skip_gain,
):
    found = main(
        sig_raw, map_raw, step_size_logits.T, d_out, sig_taps, sig_bias[None, :], map_taps,
        map_bias[None, :], a_log[None, :], dt_bias[None, :], skip_gain[None, :],
    )
    out = last(*found)
    return out[:2] + (out[2].T,) + out[3:5] + tuple(a.reshape(-1) for a in out[5:])


def solution(mesh):
    return jax.shard_map(
        shards,
        mesh=mesh,
        in_specs=(
            P("ctx", "fsdp"),
            P("ctx", None),
            P("ctx", "fsdp"),
            P("ctx", "fsdp"),
            P(None, "fsdp"),
            P(None, "fsdp"),
            P("fsdp"),
            P("fsdp"),
            P("fsdp"),
            P("fsdp"),
            P("fsdp"),
        ),
        out_specs=(
            P("ctx", "fsdp"),
            P("ctx", "fsdp"),
            P("ctx", "fsdp"),
            P(None, "fsdp"),
            P(None, "fsdp"),
            P("fsdp"),
            P("fsdp"),
            P("fsdp"),
            P("fsdp"),
            P("fsdp"),
        ),
        check_vma=False,
    )
```

```python
import functools
import math

import jax
import jax.numpy as jnp
from jax import lax
from jax.experimental import pallas as pl
from jax.experimental.pallas import tpu as pltpu
from jax.sharding import PartitionSpec as P

HEADS = 128
HDIM = 64
STATE = 128
GROUPS = 8
HERE = 8
KSIZE = 4
RIM = KSIZE - 1
BLK = 64
ROWS = 2 * BLK
SIG = HERE * HDIM
WIDE = SIG + 3 * STATE
OWN = SIG + STATE
EDGE = 16
RIMS = 8
QUADS = SIG // STATE
SUMS = 24
FINE = 10
MESH = pl.DeviceIdType.MESH
VM = pl.BlockSpec(memory_space=pltpu.VMEM)
HBM = pl.BlockSpec(memory_space=pltpu.HBM)
HIGH = lax.Precision.HIGHEST
F32 = jnp.float32
BF16 = jnp.bfloat16


def signal(sem, **where):
    pl.semaphore_signal(sem, inc=1, device_id=where, device_id_type=MESH)


def remote(src, dst, send_sem, recv_sem, **where):
    return pltpu.make_async_remote_copy(
        src_ref=src,
        dst_ref=dst,
        send_sem=send_sem,
        recv_sem=recv_sem,
        device_id=where,
        device_id_type=MESH,
    )


def other(me, i, n):
    off = jnp.where(lax.rem(i, 2) == 1, (i + 1) // 2, n - i // 2)
    return lax.rem(me + off, n)


def columns(start):
    return pl.ds(pl.multiple_of(start * STATE, STATE), STATE)


def nn(a, b, precision=None):
    return lax.dot_general(
        a, b, (((1,), (0,)), ((), ())), precision=precision, preferred_element_type=F32
    )


def nt(a, b, precision=None):
    return lax.dot_general(
        a, b, (((1,), (1,)), ((), ())), precision=precision, preferred_element_type=F32
    )


def tn(a, b):
    return lax.dot_general(a, b, (((0,), (0,)), ((), ())), preferred_element_type=F32)


def sigmoid(v):
    return 1.0 / (1.0 + jnp.exp(-v))


def log1p_small(e):
    series = e * (
        1.0 + e * (-1.0 / 2 + e * (1.0 / 3 + e * (-1.0 / 4 + e * (1.0 / 5 + e * (-1.0 / 6)))))
    )
    return jnp.where(e < 0.03, series, jnp.log(1.0 + e))


def pack(v):
    n, rows, _ = v.shape
    high = v.astype(BF16)
    value = high.astype(F32)
    tiny = jnp.abs(value) < 1e-30
    ratio = jnp.where(tiny, 0.0, (v - value) / jnp.where(tiny, 1.0, value))
    steps = jnp.clip(jnp.round(ratio * (256.0 * FINE)), -FINE, FINE)
    both = steps[:, : rows // 2] * (2.0 * FINE + 1.0) + steps[:, rows // 2 :]
    return high, both.astype(BF16)


def unpack(high, both):
    value = high.astype(F32)
    both = both.astype(F32)
    first = jnp.floor((both + (FINE + 0.5)) * (1.0 / (2.0 * FINE + 1.0)))
    second = both - first * (2.0 * FINE + 1.0)
    steps = jnp.concatenate([first, second], axis=-2)
    return value + value * steps * (1.0 / (256.0 * FINE))


def main_kernel(
    n, half, sig_hbm, map_hbm, dt_hbm, dout_hbm, taps_hbm, bias_hbm, mtaps_hbm, mbias_hbm,
    alog_hbm, dtb_hbm, skip_hbm,
    dsig_hbm, dmap_hbm, sums_hbm, small_hbm, ddt_hbm,
    sig_in, map_in, dout_ref, dt_in, dt_got, taps_ref, bias_ref, mtaps_ref, mbias_ref,
    alog_ref, dtb_ref, skip_ref, tail_own, tail_got, tap_row, gtaps_ref,
    pad, slope, signal_ref, scaled_ref, weighted_ref, sgrad_ref, imap_ref, omap_ref, wide3, intra,
    oh, gw, drow, m_out, xs, gs, es, xr, gr, er, yh, yc, lh, lc, first_local, first_sg, second_sg, lk,
    mg, mgot, gpad, rims, swap, stay, ddt_mine, ddt_got, ddt_ref,
    part, low_part, near, low_near, far, total, part_b, near_b, sum_b, far_b, total_b,
    l_sem, n_send, n_recv, b_send, b_recv, tap_send, tap_recv,
    xs_sem, xr_sem, gs_sem, gr_sem, es_sem, er_sem, hs_sem, hr_sem, cs_sem, cr_sem,
    ms_sem, mr_sem, r_sem, w_sem, q_send, q_near, q_far, q_near_b, q_far_b
):
    me = lax.axis_index("ctx")
    f = lax.axis_index("fsdp")
    odd = lax.rem(me, 2)
    mate = me + 1 - 2 * odd
    side_ctx = lax.rem(me + n - 1 + 2 * odd, n)
    slot = f // half
    first = 2 * (f - slot * half)
    group = f // 2
    side = f - 2 * group
    share = SIG // n
    per_head = n // HERE
    kept = pl.multiple_of(odd * BLK, BLK)
    given = pl.multiple_of((1 - odd) * BLK, BLK)
    ending = pl.multiple_of((1 - odd) * BLK + BLK - EDGE, EDGE)
    starts = (group, GROUPS + group, f)
    barrier = pltpu.get_barrier_semaphore()

    for i in range(1, n):
        signal(barrier, ctx=lax.rem(me + (i + 1) // 2 if i % 2 else me + n - i // 2, n))
    for k in range(2):

        @pl.when(group + k * half != f)
        def _():
            signal(barrier, fsdp=group + k * half)

        @pl.when(first + k != f)
        def _():
            signal(barrier, fsdp=first + k)

    def fetch(i, src, dst):
        copy = pltpu.make_async_copy(src, dst, l_sem.at[i])
        copy.start()
        return copy

    def third(k):
        return slice(k * STATE, (k + 1) * STATE)

    local = [
        fetch(0, mtaps_hbm, mtaps_ref),
        fetch(1, mbias_hbm, mbias_ref),
        fetch(2, dt_hbm, dt_in),
        fetch(3, alog_hbm, alog_ref),
        fetch(4, dtb_hbm, dtb_ref),
        fetch(5, skip_hbm, skip_ref),
        fetch(6, taps_hbm, taps_ref),
        fetch(7, bias_hbm, bias_ref),
        fetch(8, sig_hbm.at[pl.ds(kept, BLK)], sig_in.at[0:BLK]),
        fetch(9, dout_hbm.at[pl.ds(kept, BLK)], dout_ref.at[0:BLK]),
        fetch(10, sig_hbm.at[pl.ds(ending, EDGE)], tail_own.at[:, 0:SIG]),
    ]
    for k, start in enumerate(starts):
        local.append(
            fetch(
                11 + k,
                map_hbm.at[pl.ds(kept, BLK), columns(start)],
                map_in.at[0:BLK, third(k)],
            )
        )
        local.append(
            fetch(
                14 + k,
                map_hbm.at[pl.ds(ending, EDGE), columns(start)],
                tail_own.at[:, SIG + k * STATE : SIG + (k + 1) * STATE],
            )
        )

    tap_row[KSIZE + 1 :] = jnp.zeros((8 - KSIZE - 1, STATE), F32)
    selves = jnp.where(group == f, 1, 0) + jnp.where(group + half == f, 1, 0)
    pl.semaphore_wait(barrier, n - 1 + 4 - 2 * selves)

    def to_mate(i, src, dst):
        copy = remote(src, dst, n_send.at[i], n_recv.at[i], ctx=mate)
        copy.start()
        return copy

    def map_copy(k):
        return to_mate(
            1 + k, map_hbm.at[pl.ds(given, BLK), columns(starts[k])], map_in.at[BLK:ROWS, third(k)]
        )

    dt_copy = to_mate(0, dt_hbm, dt_got)
    out_copy = map_copy(1)
    dout_copy = to_mate(5, dout_hbm.at[pl.ds(given, BLK)], dout_ref.at[BLK:ROWS])
    for copy in local:
        copy.wait()
    tap_row[0:KSIZE] = mtaps_ref[...]
    tap_row[KSIZE : KSIZE + 1] = mbias_ref[...]
    for k in range(2):

        @pl.when(first + k != f)
        def _():
            remote(
                tap_row, gtaps_ref.at[slot], tap_send.at[k], tap_recv.at[slot], fsdp=first + k
            ).start()

        @pl.when(group + k * half == f)
        def _():
            gtaps_ref[k] = tap_row[...]

    def to_side(i, dst_cols):
        copy = remote(
            tail_own.at[:, dst_cols], tail_got.at[:, dst_cols], b_send.at[i], b_recv.at[i],
            ctx=side_ctx,
        )
        copy.start()
        return copy

    out_cols = slice(SIG + STATE, SIG + 2 * STATE)
    out_tail = to_side(0, out_cols)
    tails = [to_side(1, slice(0, SIG + STATE)), to_side(2, slice(SIG + 2 * STATE, WIDE))]
    map_copies = [map_copy(0), map_copy(2)]
    sig_copy = to_mate(4, sig_hbm.at[pl.ds(given, BLK)], sig_in.at[BLK:ROWS])

    lane = lax.broadcasted_iota(jnp.int32, (HERE, ROWS), 1)
    row_id = lax.broadcasted_iota(jnp.int32, (ROWS, ROWS), 0)
    col_id = lax.broadcasted_iota(jnp.int32, (ROWS, ROWS), 1)
    lower = ((row_id >= BLK) == (col_id >= BLK)) & (col_id <= row_id)
    lower_f = jnp.where(lower, 1.0, 0.0).astype(F32)
    eye = jnp.where(row_id == col_id, 1.0, 0.0).astype(F32)
    eye8 = eye[:HERE, :HERE]
    ones8 = jnp.ones((HERE, ROWS), F32)
    head1 = lax.broadcasted_iota(jnp.int32, (HERE, SIG), 0)
    spread1 = jnp.where(
        lax.broadcasted_iota(jnp.int32, (HERE, SIG), 1) // HDIM == head1, 1.0, 0.0
    ).astype(F32)

    def in_rows(ref):
        return nt(eye8, jnp.broadcast_to(ref[...], (ROWS, HERE)), HIGH)

    spread_low = spread1.astype(BF16)

    def halves(y):
        top = y.astype(BF16)
        return top, (y - top.astype(F32)).astype(BF16)

    def per_row(y):
        top, rest = halves(y)
        return nt(spread_low, top) + nt(spread_low, rest)

    def widened(x):
        top, rest = halves(x)
        return nn(top, spread_low) + nn(rest, spread_low)

    def turned(x):
        return pltpu.roll(x, BLK, 1)

    def preact(r, rows, cols, taps, bias):
        acc = bias
        for k in range(KSIZE):
            start = EDGE - RIM + k + r
            acc = acc + taps[k : k + 1] * pad[start : start + rows, cols]
        return acc

    def sig_rows(r, count):
        rows = slice(r, r + count)
        for q in range(SIG // STATE):
            cols = third(q)
            v = preact(r, count, cols, taps_ref[:, cols], bias_ref[:, cols])
            s = sigmoid(v)
            slope[rows, cols] = s * (1.0 + v * (1.0 - s))
            signal_ref[rows, cols] = (v * s).astype(BF16)

    pad[EDGE : EDGE + BLK, :SIG] = sig_in[:BLK, :].astype(F32)
    pad[EDGE : EDGE + BLK, SIG:] = map_in[:BLK, :].astype(F32)
    keep = jnp.where(me == 0, 0.0, 1.0).astype(F32)

    def before(cols):
        mine_then = tail_own[:, cols].astype(F32)
        pad[:EDGE, cols] = keep * jnp.where(me == n - 1, mine_then, tail_got[:, cols].astype(F32))

    dt_copy.wait()
    own, got = dt_in[...], dt_got[...]
    own = jnp.where(odd == 0, own, turned(own))
    got = jnp.where(odd == 0, turned(got), got)
    logits = jnp.where(lane < BLK, own, got) + in_rows(dtb_ref)
    rate = -jnp.exp(in_rows(alog_ref))
    step = jnp.maximum(logits, 0.0) + log1p_small(jnp.exp(-jnp.abs(logits)))
    ds = nt(step * rate, lower_f, HIGH)
    end_low = jnp.exp(ds[:, BLK - 1 : BLK])
    end_high = jnp.exp(ds[:, ROWS - 1 : ROWS])
    end = jnp.where(lane < BLK, ds[:, BLK - 1 : BLK], ds[:, ROWS - 1 : ROWS])
    to_end = jnp.exp(end - ds)
    col4 = nt(eye, jnp.concatenate([step, to_end, jnp.exp(ds), ds], axis=0), HIGH)
    ds_col = col4[:, 3 * HERE :]
    wide3[:, 2 * SIG :] = widened(col4[:, 2 * HERE : 3 * HERE])
    end_low8 = jnp.broadcast_to(end_low, (HERE, STATE))
    end_high8 = jnp.broadcast_to(end_high, (HERE, STATE))
    both_ends = end_low8 * end_high8
    for h in range(HERE):
        es[h] = both_ends[h : h + 1]

    def e_copy(d):
        return remote(es.at[d // per_head], er.at[me], es_sem.at[d], er_sem.at[me], ctx=d)

    def send_ends(i, _):
        e_copy(other(me, i, n)).start()
        return 0

    lax.fori_loop(1, n, send_ends, 0)
    er[me] = es[me // per_head]

    for k in range(2):

        @pl.when(group + k * half != f)
        def _():
            remote(
                tap_row, gtaps_ref.at[k], tap_send.at[k], tap_recv.at[k], fsdp=group + k * half
            ).wait_recv()

        @pl.when(first + k != f)
        def _():
            remote(
                tap_row, gtaps_ref.at[slot], tap_send.at[k], tap_recv.at[slot], fsdp=first + k
            ).wait_send()

    out_tail.wait()
    before(out_cols)
    def map_rows(k, out, r, count):
        cols = slice(SIG + k * STATE, SIG + (k + 1) * STATE)
        v = preact(r, count, cols, gtaps_ref[k, :KSIZE], gtaps_ref[k, KSIZE : KSIZE + 1])
        out[r : r + count, :] = (v * sigmoid(v)).astype(BF16)

    def sgrad_rows(rows):
        for q in range(QUADS):
            cols3 = slice(2 * SIG + q * STATE, 2 * SIG + (q + 1) * STATE)
            grad = dout_ref[rows, third(q)].astype(F32) * wide3[rows, cols3]
            sgrad_ref[rows, third(q)] = grad.astype(BF16)
        return tn(sgrad_ref[rows, :], omap_ref[rows, :])

    def mine(d):
        return pl.ds(pl.multiple_of(d * share, share), share)

    def x_copy(d):
        return remote(xs.at[mine(d)], xr.at[me], xs_sem.at[d], xr_sem.at[me], ctx=d)

    def g_copy(d):
        return remote(gs.at[d], gr.at[me], gs_sem.at[d], gr_sem.at[me], ctx=d)

    def h_copy(d):
        return remote(yh.at[d], lh.at[mine(me)], hs_sem.at[d], hr_sem.at[me], ctx=d)

    def c_copy(d):
        return remote(yc.at[d], lc.at[me], cs_sem.at[d], cr_sem.at[me], ctx=d)

    def send_g(i, _):
        g_copy(other(me, i, n)).start()
        return 0

    def send_x(i, _):
        x_copy(other(me, i, n)).start()
        return 0

    low, high = slice(0, BLK), slice(BLK, ROWS)
    map_rows(1, omap_ref, 0, BLK)
    first_sg[...] = sgrad_rows(low)
    out_copy.wait()
    pad[EDGE + BLK :, out_cols] = map_in[BLK:, third(1)].astype(F32)
    map_rows(1, omap_ref, BLK, BLK)
    dout_copy.wait()
    second_sg[...] = sgrad_rows(high)
    for h in range(HERE):
        at = slice(h * HDIM, (h + 1) * HDIM)
        link = first_sg[at, :] + end_low8[h : h + 1] * second_sg[at, :]
        top, rest = pack(link.reshape(per_head, share, STATE))
        gs[h * per_head : (h + 1) * per_head, :share, :] = top
        gs[h * per_head : (h + 1) * per_head, share:, :] = rest
    lax.fori_loop(1, n, send_g, 0)
    gr[me] = gs[me]

    wide3[:, :SIG] = widened(col4[:, :HERE])
    wide3[:, SIG : 2 * SIG] = widened(col4[:, HERE : 2 * HERE])
    for copy in tails + map_copies:
        copy.wait()
    for cols in (slice(0, SIG + STATE), slice(SIG + 2 * STATE, WIDE)):
        before(cols)
    pad[EDGE + BLK :, SIG : SIG + STATE] = map_in[BLK:, third(0)].astype(F32)
    pad[EDGE + BLK :, SIG + 2 * STATE :] = map_in[BLK:, third(2)].astype(F32)
    map_rows(0, imap_ref, 0, ROWS)
    v = preact(0, ROWS, slice(SIG + 2 * STATE, WIDE), mtaps_ref[...], mbias_ref[...])
    s = sigmoid(v)
    slope[:, SIG:] = s * (1.0 + v * (1.0 - s))
    sig_copy.wait()
    pad[EDGE + BLK :, :SIG] = sig_in[BLK:, :].astype(F32)
    sig_rows(0, ROWS)
    for q in range(QUADS):
        cols = third(q)
        cols2 = slice(SIG + q * STATE, SIG + (q + 1) * STATE)
        scaled_b = (signal_ref[:, cols].astype(F32) * wide3[:, cols]).astype(BF16)
        scaled_ref[:, cols] = scaled_b
        weighted_ref[:, cols] = (scaled_b.astype(F32) * wide3[:, cols2]).astype(BF16)
    first_local[...] = tn(weighted_ref[low, :], imap_ref[low, :])
    second_local = tn(weighted_ref[high, :], imap_ref[high, :])
    for h in range(HERE):
        at = slice(h * HDIM, (h + 1) * HDIM)
        xs[at, :] = (end_high8[h : h + 1] * first_local[at, :] + second_local[at, :]).astype(BF16)
    lax.fori_loop(1, n, send_x, 0)
    xr[me] = xs[mine(me)]

    score = nt(omap_ref[...], imap_ref[...])
    lane_row = lax.broadcasted_iota(jnp.int32, (ROWS, STATE), 1)
    grad_score = jnp.zeros((ROWS, ROWS), F32)
    for q in range(HERE // 2):
        cols = third(q)
        d_pair = dout_ref[:, cols].astype(F32)
        d_two = jnp.concatenate(
            [jnp.where(lane_row < HDIM, d_pair, 0.0), jnp.where(lane_row < HDIM, 0.0, d_pair)],
            axis=0,
        ).astype(BF16)
        grad_mix2 = nt(d_two, scaled_ref[:, cols])
        mixes = []
        for k in range(2):
            h = 2 * q + k
            grad_mix = grad_mix2[k * ROWS : (k + 1) * ROWS]
            gap = jnp.minimum(ds_col[:, h : h + 1] - ds[h : h + 1, :], 0.0)
            decay = jnp.where(lower, jnp.exp(gap), 0.0)
            mix = score * decay
            mixes.append(mix.astype(BF16))
            grad_score = grad_score + grad_mix * decay
            product = grad_mix * mix
            drow[h : h + 1, :] = nt(ones8, product, HIGH)[0:1] - jnp.sum(
                product, axis=0, keepdims=True
            )
        intra[:, cols] = tn(jnp.concatenate(mixes, axis=0), d_two)
    grad_score = grad_score.astype(BF16)
    mg[0] = tn(grad_score, omap_ref[...])
    mg[1] = nn(grad_score, imap_ref[...])

    def holder(i):
        return jnp.where(i < n // 2, 2 * i, 2 * (n - 1 - i) + 1)

    zero = jnp.zeros((share, STATE), F32)

    def g_arrived(i, _):
        s = other(me, i, n)
        remote(es.at[s // per_head], er.at[s], es_sem.at[s], er_sem.at[s], ctx=s).wait_recv()
        remote(gs.at[s], gr.at[s], gs_sem.at[s], gr_sem.at[s], ctx=s).wait_recv()
        return 0

    def to_front(i, g):
        at = holder(n - 1 - i)
        top, rest = pack(g[None])
        yc[at, :share, :] = top[0]
        yc[at, share:, :] = rest[0]
        got = gr[at]
        return er[at] * g + unpack(got[:share], got[share:])

    def send_c(i, _):
        c_copy(other(me, i, n)).start()
        return 0

    def x_arrived(i, _):
        s = other(me, i, n)
        remote(xs.at[mine(s)], xr.at[s], xs_sem.at[s], xr_sem.at[s], ctx=s).wait_recv()
        return 0

    def to_back(i, h):
        at = holder(i)
        yh[at] = h.astype(BF16)
        return er[at] * h + xr[at].astype(F32)

    def send_h(i, _):
        h_copy(other(me, i, n)).start()
        return 0

    lax.fori_loop(1, n, g_arrived, 0)
    lax.fori_loop(0, n, to_front, zero, unroll=4)
    lax.fori_loop(1, n, send_c, 0)
    lax.fori_loop(1, n, x_arrived, 0)
    lax.fori_loop(0, n, to_back, zero, unroll=4)
    lax.fori_loop(1, n, send_h, 0)
    lh[mine(me)] = yh[me]
    lc[me] = yc[me]
    step_w = wide3[:, :SIG]
    end_w = wide3[:, SIG : 2 * SIG]
    exp_w = wide3[:, 2 * SIG :]
    d_f = dout_ref[...].astype(F32)
    signal_f = signal_ref[...].astype(F32)
    skip_w = nn(jnp.broadcast_to(skip_ref[...], (HERE, HERE)), spread1, HIGH)[0:1]
    part[(KSIZE + 1) * QUADS :] = jnp.zeros((SUMS - (KSIZE + 1) * QUADS, STATE), F32)

    def small(at, row):
        at = KSIZE + 1 + at
        part_b[at : at + 1] = jnp.concatenate([row, jnp.zeros((1, STATE - HERE), F32)], axis=1)

    small(2, nt(ones8, per_row(d_f * signal_f), HIGH)[0:1])

    def m_copy(k):
        return remote(
            m_out.at[k], mgot.at[side], ms_sem.at[k], mr_sem.at[side], fsdp=group + k * half
        )

    def to_owner(k):
        m_out[k] = mg[k].astype(BF16)

        @pl.when(group + k * half != f)
        def _():
            m_copy(k).start()

        @pl.when(group + k * half == f)
        def _():
            mgot[side] = m_out[k]

    def c_in(i, _):
        d = other(me, i, n)
        g_copy(d).wait_send()
        e_copy(d).wait_send()
        remote(yc.at[d], lc.at[d], cs_sem.at[d], cr_sem.at[d], ctx=d).wait_recv()
        return 0

    lax.fori_loop(1, n, c_in, 0)
    for h in range(HERE):
        at = slice(h * HDIM, (h + 1) * HDIM)
        got = lc[h * per_head : (h + 1) * per_head]
        state = unpack(got[:, :share], got[:, share:]).reshape(HDIM, STATE)
        lk[3, at, :] = state.astype(BF16)
        lk[2, at, :] = (second_sg[at, :] + end_high8[h : h + 1] * state).astype(BF16)
    for b, rows in enumerate((low, high)):
        mg[0, rows, :] = mg[0, rows, :] + nn(weighted_ref[rows, :], lk[2 + b])
    to_owner(0)
    for b, rows in enumerate((low, high)):
        gw[rows, :] = nt(imap_ref[rows, :], lk[2 + b])
    gw_v = gw[...]
    back_row = per_row(gw_v * scaled_ref[...].astype(F32)) * to_end
    back_low = jnp.sum(jnp.where(lane < BLK, back_row, 0.0), axis=1, keepdims=True)
    back_high = jnp.sum(jnp.where(lane < BLK, 0.0, back_row), axis=1, keepdims=True)
    grad_scaled = gw_v * end_w + intra[...]
    own_step = per_row(grad_scaled * signal_f)
    gpad[:ROWS, :SIG] = (skip_w * d_f + grad_scaled * step_w) * slope[:, :SIG]

    def sums(cols, source, into, every, at):
        g = gpad[:ROWS, cols]
        for k in range(KSIZE):
            start = EDGE - RIM + k
            row = k * every + at
            into[row : row + 1] = jnp.sum(
                g * pad[start : start + ROWS, source], axis=0, keepdims=True
            )
        row = KSIZE * every + at
        into[row : row + 1] = jnp.sum(g, axis=0, keepdims=True)

    earlier = jnp.where(
        odd == 0, lax.rem(me + n - 2, n), jnp.where(me == n - 1, n - 2, lax.rem(me + 2, n))
    )
    earlier = jnp.where(me == 0, 1, earlier)

    def rim(i, cols):
        copy = remote(
            gpad.at[0:RIMS, cols], rims.at[:, cols], r_sem.at[2 * i], r_sem.at[2 * i + 1],
            ctx=earlier,
        )
        copy.start()
        return copy

    sig_cols, map_cols = slice(0, SIG), slice(SIG, OWN)
    sig_rim = rim(0, sig_cols)
    planes = n // 2
    y = me // planes
    z = me - y * planes
    z_high = z // 4
    z_low = z - 4 * z_high
    here = 4 * y + z_low
    sent = []

    def to_near(src, dst, at, recv_sem):
        for k in range(1, 8):
            s = lax.rem(here + k, 8)
            d = s // 4 * planes + z_high * 4 + s - s // 4 * 4
            copy = remote(src, dst.at[here], q_send.at[at + k], recv_sem.at[here], ctx=d)
            copy.start()
            sent.append(copy)
        dst[here] = src[...]

    def near_in(src, dst, recv_sem):
        for k in range(1, 8):
            s = lax.rem(here + k, 8)
            remote(src, dst.at[s], q_send.at[k], recv_sem.at[s], ctx=mate).wait_recv()

    def to_far(src, dst, at, recv_sem):
        for k in range(1, 4):
            s = lax.rem(z_high + k, 4)
            d = y * planes + 4 * s + z_low
            copy = remote(src, dst.at[z_high], q_send.at[at + k], recv_sem.at[z_high], ctx=d)
            copy.start()
            sent.append(copy)
        dst[z_high] = src[...]

    def far_in(src, dst, recv_sem):
        for k in range(1, 4):
            s = lax.rem(z_high + k, 4)
            remote(src, dst.at[s], q_send.at[k], recv_sem.at[s], ctx=mate).wait_recv()

    def raw(r, out, taps, cols):
        acc = taps[RIM : RIM + 1] * gpad[r : r + BLK, cols]
        for k in range(RIM):
            acc = acc + taps[k : k + 1] * gpad[r + RIM - k : r + RIM - k + BLK, cols]
        out[:, cols] = acc

    def transposed(i, rim_copy, taps, cols, out):
        rim_copy.wait()
        gpad[ROWS:, cols] = jnp.where(me == 1, 0.0, rims[:, cols])
        raw(BLK, swap, taps, cols)
        away = remote(
            swap.at[:, cols], out.at[pl.ds(kept, BLK)], w_sem.at[2 * i], w_sem.at[2 * i + 1],
            ctx=mate,
        )
        away.start()
        raw(0, stay, taps, cols)
        return away, fetch(i, stay.at[:, cols], out.at[pl.ds(kept, BLK)])

    def h_in(i, _):
        d = other(me, i, n)
        x_copy(d).wait_send()
        remote(yh.at[d], lh.at[mine(d)], hs_sem.at[d], hr_sem.at[d], ctx=d).wait_recv()
        return 0

    lax.fori_loop(1, n, h_in, 0)
    lk[0] = lh[...]
    for h in range(HERE):
        at = slice(h * HDIM, (h + 1) * HDIM)
        lk[1, at, :] = (end_low8[h : h + 1] * lh[at, :].astype(F32) + first_local[at, :]).astype(
            BF16
        )
    for b, rows in enumerate((low, high)):
        mg[1, rows, :] = mg[1, rows, :] + nn(sgrad_ref[rows, :], lk[b])
    to_owner(1)
    for q in range(QUADS):
        sums(third(q), third(q), part, QUADS, q)
    low_part[...] = part[...].astype(BF16)
    to_near(low_part, near, 0, q_near)

    end_terms = []
    for b, rows in enumerate((low, high)):
        oh[rows, :] = nt(omap_ref[rows, :], lk[b])
        both = lk[b].astype(F32) * lk[2 + b].astype(F32)
        both = jnp.sum(both.reshape(HERE, HDIM, STATE), axis=1)
        end_terms.append(jnp.sum(both, axis=1, keepdims=True))
    grad_sum = per_row(d_f * exp_w * oh[...]) - back_row + drow[...]
    last_low = back_low + end_low * end_terms[0]
    last_high = back_high + end_high * end_terms[1]
    grad_sum = grad_sum + jnp.where(
        lane == BLK - 1, last_low, jnp.where(lane == ROWS - 1, last_high, 0.0)
    )
    grad_log = nn(grad_sum, lower_f, HIGH)
    grad_step = grad_log * rate + own_step
    grad_dt = grad_step * sigmoid(logits)
    ddt_mine[...] = grad_dt
    ddt_copy = remote(ddt_mine, ddt_got, w_sem.at[0], w_sem.at[1], ctx=mate)
    ddt_copy.start()
    small(0, nt(ones8, grad_log * step, HIGH)[0:1] * (-jnp.exp(alog_ref[...])))
    small(1, nt(ones8, grad_dt, HIGH)[0:1])
    for k in range(2):

        @pl.when(first + k != f)
        def _():
            remote(
                m_out.at[k], mgot.at[k], ms_sem.at[k], mr_sem.at[k], fsdp=first + k
            ).wait_recv()

    gpad[:ROWS, SIG:] = (mgot[0].astype(F32) + mgot[1].astype(F32)) * slope[:, SIG:]
    map_rim = rim(1, map_cols)
    sums(map_cols, slice(SIG + 2 * STATE, WIDE), part_b, 1, 0)
    to_near(part_b, near_b, 10, q_near_b)
    sig_out = transposed(1, sig_rim, taps_ref, sig_cols, dsig_hbm)
    near_in(low_part, near, q_near)
    low_near[...] = jnp.sum(near[...].astype(F32), axis=0).astype(BF16)
    to_far(low_near, far, 7, q_far)
    map_out = transposed(2, map_rim, mtaps_ref, map_cols, dmap_hbm)
    near_in(part_b, near_b, q_near_b)
    sum_b[...] = jnp.sum(near_b[...], axis=0)
    to_far(sum_b, far_b, 17, q_far_b)
    ddt_copy.wait()
    own, got = ddt_mine[...], ddt_got[...]
    ddt_low = jnp.where(odd == 0, own, turned(got))
    ddt_high = jnp.where(odd == 0, got, turned(own))
    ddt_ref[...] = jnp.where(lane < BLK, ddt_low, ddt_high)
    ddt_out = fetch(3, ddt_ref, ddt_hbm)
    far_in(low_near, far, q_far)
    total[...] = jnp.sum(far[...].astype(F32), axis=0)
    sums_out = fetch(4, total, sums_hbm)

    def done(i, _):
        d = other(me, i, n)
        h_copy(d).wait_send()
        c_copy(d).wait_send()
        return 0

    lax.fori_loop(1, n, done, 0)
    for k in range(2):

        @pl.when(group + k * half != f)
        def _():
            m_copy(k).wait_send()

    far_in(sum_b, far_b, q_far_b)
    total_b[...] = jnp.sum(far_b[...], axis=0)
    small_out = fetch(5, total_b, small_hbm)
    for copy in sent:
        copy.wait_send()
    for copy in sig_out + map_out + (ddt_out, sums_out, small_out):
        copy.wait()


def main(*operands):
    n = lax.axis_size("ctx")
    half = lax.axis_size("fsdp") // 2
    share = SIG // n
    dma = pltpu.SemaphoreType.DMA
    vm = pltpu.VMEM
    return pl.pallas_call(
        functools.partial(main_kernel, n, half),
        out_shape=(
            jax.ShapeDtypeStruct((ROWS, SIG), F32),
            jax.ShapeDtypeStruct((ROWS, STATE), F32),
            jax.ShapeDtypeStruct((SUMS, STATE), F32),
            jax.ShapeDtypeStruct((8, STATE), F32),
            jax.ShapeDtypeStruct((HERE, ROWS), F32),
        ),
        in_specs=[pl.BlockSpec(memory_space=pl.ANY)] * len(operands),
        out_specs=(HBM,) * 5,
        scratch_shapes=[
            vm((ROWS, SIG), BF16),
            vm((ROWS, 3 * STATE), BF16),
            vm((ROWS, SIG), BF16),
            vm((HERE, ROWS), F32),
            vm((HERE, ROWS), F32),
            vm((KSIZE, SIG), F32),
            vm((1, SIG), F32),
            vm((KSIZE, STATE), F32),
            vm((1, STATE), F32),
            vm((1, HERE), F32),
            vm((1, HERE), F32),
            vm((1, HERE), F32),
            vm((EDGE, WIDE), BF16),
            vm((EDGE, WIDE), BF16),
            vm((8, STATE), F32),
            vm((2, 8, STATE), F32),
            vm((EDGE + ROWS, WIDE), F32),
            vm((ROWS, OWN), F32),
            vm((ROWS, SIG), BF16),
            vm((ROWS, SIG), BF16),
            vm((ROWS, SIG), BF16),
            vm((ROWS, SIG), BF16),
            vm((ROWS, STATE), BF16),
            vm((ROWS, STATE), BF16),
            vm((ROWS, 3 * SIG), F32),
            vm((ROWS, SIG), F32),
            vm((ROWS, SIG), F32),
            vm((ROWS, SIG), F32),
            vm((HERE, ROWS), F32),
            vm((2, ROWS, STATE), BF16),
            vm((SIG, STATE), BF16),
            vm((n, 3 * share // 2, STATE), BF16),
            vm((HERE, 1, STATE), F32),
            vm((n, share, STATE), BF16),
            vm((n, 3 * share // 2, STATE), BF16),
            vm((n, 1, STATE), F32),
            vm((n, share, STATE), BF16),
            vm((n, 3 * share // 2, STATE), BF16),
            vm((SIG, STATE), BF16),
            vm((n, 3 * share // 2, STATE), BF16),
            vm((SIG, STATE), F32),
            vm((SIG, STATE), F32),
            vm((SIG, STATE), F32),
            vm((4, SIG, STATE), BF16),
            vm((2, ROWS, STATE), F32),
            vm((2, ROWS, STATE), BF16),
            vm((ROWS + RIMS, OWN), F32),
            vm((RIMS, OWN), F32),
            vm((BLK, OWN), F32),
            vm((BLK, OWN), F32),
            vm((HERE, ROWS), F32),
            vm((HERE, ROWS), F32),
            vm((HERE, ROWS), F32),
            vm((SUMS, STATE), F32),
            vm((SUMS, STATE), BF16),
            vm((8, SUMS, STATE), BF16),
            vm((SUMS, STATE), BF16),
            vm((4, SUMS, STATE), BF16),
            vm((SUMS, STATE), F32),
            vm((8, STATE), F32),
            vm((8, 8, STATE), F32),
            vm((8, STATE), F32),
            vm((4, 8, STATE), F32),
            vm((8, STATE), F32),
        ]
        + [dma((17,)), dma((6,)), dma((6,)), dma((3,)), dma((3,)), dma((2,)), dma((2,))]
        + [dma((n,))] * 10
        + [dma((2,)), dma((2,)), dma((4,)), dma((6,)), dma((21,)), dma((8,)), dma((4,)), dma((8,)), dma((4,))],
        compiler_params=pltpu.CompilerParams(
            collective_id=0, has_side_effects=True, vmem_limit_bytes=56 * 1024 * 1024
        ),
        name="main",
    )(*operands)


def last_kernel(
    scale, dsig_in, dmap_in, sums_in, small_in, ddt_in,
    dsig, dmap, ddt, dtaps, dmtaps, dbias, dmbias, dalog, ddtb, dskip
):
    dsig[...] = dsig_in[...]
    dmap[...] = dmap_in[...]
    ddt[...] = ddt_in[...]
    for k in range(KSIZE + 1):
        for q in range(QUADS):
            at = k * QUADS + q
            cols = slice(q * STATE, (q + 1) * STATE)
            row = sums_in[at : at + 1] * scale
            if k < KSIZE:
                dtaps[k : k + 1, cols] = row
            else:
                dbias[:, cols] = row
    dmtaps[...] = small_in[:KSIZE] * scale
    dmbias[...] = small_in[KSIZE : KSIZE + 1] * scale
    for k, out in enumerate((dalog, ddtb, dskip)):
        at = KSIZE + 1 + k
        out[...] = small_in[at : at + 1, :HERE] * scale


def last(*operands):
    scale = 1.0 / math.sqrt(float(lax.axis_size("ctx") * ROWS))
    shapes = (
        (ROWS, SIG), (ROWS, STATE), (HERE, ROWS), (KSIZE, SIG), (KSIZE, STATE),
        (1, SIG), (1, STATE), (1, HERE), (1, HERE), (1, HERE),
    )
    return pl.pallas_call(
        functools.partial(last_kernel, scale),
        out_shape=tuple(jax.ShapeDtypeStruct(s, F32) for s in shapes),
        in_specs=[VM] * 5,
        out_specs=(VM,) * len(shapes),
        compiler_params=pltpu.CompilerParams(vmem_limit_bytes=60 * 1024 * 1024),
        name="last",
    )(*operands)


def shards(
    sig_raw,
    map_raw,
    step_size_logits,
    d_out,
    sig_taps,
    map_taps,
    sig_bias,
    map_bias,
    a_log,
    dt_bias,
    skip_gain,
):
    found = main(
        sig_raw, map_raw, step_size_logits.T, d_out, sig_taps, sig_bias[None, :], map_taps,
        map_bias[None, :], a_log[None, :], dt_bias[None, :], skip_gain[None, :],
    )
    out = last(*found)
    return out[:2] + (out[2].T,) + out[3:5] + tuple(a.reshape(-1) for a in out[5:])


def solution(mesh):
    return jax.shard_map(
        shards,
        mesh=mesh,
        in_specs=(
            P("ctx", "fsdp"),
            P("ctx", None),
            P("ctx", "fsdp"),
            P("ctx", "fsdp"),
            P(None, "fsdp"),
            P(None, "fsdp"),
            P("fsdp"),
            P("fsdp"),
            P("fsdp"),
            P("fsdp"),
            P("fsdp"),
        ),
        out_specs=(
            P("ctx", "fsdp"),
            P("ctx", "fsdp"),
            P("ctx", "fsdp"),
            P(None, "fsdp"),
            P(None, "fsdp"),
            P("fsdp"),
            P("fsdp"),
            P("fsdp"),
            P("fsdp"),
            P("fsdp"),
        ),
        check_vma=False,
    )
```

```python
import functools
import math

import jax
import jax.numpy as jnp
from jax import lax
from jax.experimental import pallas as pl
from jax.experimental.pallas import tpu as pltpu
from jax.sharding import PartitionSpec as P

HEADS = 128
HDIM = 64
STATE = 128
GROUPS = 8
HERE = 8
KSIZE = 4
RIM = KSIZE - 1
BLK = 64
ROWS = 2 * BLK
SIG = HERE * HDIM
WIDE = SIG + 3 * STATE
OWN = SIG + STATE
EDGE = 16
RIMS = 8
QUADS = SIG // STATE
SUMS = 24
FINE = 10
MESH = pl.DeviceIdType.MESH
VM = pl.BlockSpec(memory_space=pltpu.VMEM)
HBM = pl.BlockSpec(memory_space=pltpu.HBM)
HIGH = lax.Precision.HIGHEST
F32 = jnp.float32
BF16 = jnp.bfloat16


def signal(sem, **where):
    pl.semaphore_signal(sem, inc=1, device_id=where, device_id_type=MESH)


def remote(src, dst, send_sem, recv_sem, **where):
    return pltpu.make_async_remote_copy(
        src_ref=src,
        dst_ref=dst,
        send_sem=send_sem,
        recv_sem=recv_sem,
        device_id=where,
        device_id_type=MESH,
    )


def other(me, i, n):
    off = jnp.where(lax.rem(i, 2) == 1, (i + 1) // 2, n - i // 2)
    return lax.rem(me + off, n)


def columns(start):
    return pl.ds(pl.multiple_of(start * STATE, STATE), STATE)


def nn(a, b, precision=None):
    return lax.dot_general(
        a, b, (((1,), (0,)), ((), ())), precision=precision, preferred_element_type=F32
    )


def nt(a, b, precision=None):
    return lax.dot_general(
        a, b, (((1,), (1,)), ((), ())), precision=precision, preferred_element_type=F32
    )


def tn(a, b):
    return lax.dot_general(a, b, (((0,), (0,)), ((), ())), preferred_element_type=F32)


def sigmoid(v):
    return 1.0 / (1.0 + jnp.exp(-v))


def log1p_small(e):
    series = e * (
        1.0 + e * (-1.0 / 2 + e * (1.0 / 3 + e * (-1.0 / 4 + e * (1.0 / 5 + e * (-1.0 / 6)))))
    )
    return jnp.where(e < 0.03, series, jnp.log(1.0 + e))


def pack(v):
    n, rows, _ = v.shape
    high = v.astype(BF16)
    value = high.astype(F32)
    tiny = jnp.abs(value) < 1e-30
    ratio = jnp.where(tiny, 0.0, (v - value) / jnp.where(tiny, 1.0, value))
    steps = jnp.clip(jnp.round(ratio * (256.0 * FINE)), -FINE, FINE)
    both = steps[:, : rows // 2] * (2.0 * FINE + 1.0) + steps[:, rows // 2 :]
    return high, both.astype(BF16)


def unpack(high, both):
    value = high.astype(F32)
    both = both.astype(F32)
    first = jnp.floor((both + (FINE + 0.5)) * (1.0 / (2.0 * FINE + 1.0)))
    second = both - first * (2.0 * FINE + 1.0)
    steps = jnp.concatenate([first, second], axis=-2)
    return value + value * steps * (1.0 / (256.0 * FINE))


def main_kernel(
    n, half, sig_hbm, map_hbm, dt_hbm, dout_hbm, taps_hbm, bias_hbm, mtaps_hbm, mbias_hbm,
    alog_hbm, dtb_hbm, skip_hbm,
    dsig_hbm, dmap_hbm, sums_hbm, small_hbm, ddt_hbm,
    sig_in, map_in, dout_ref, dt_in, dt_got, taps_ref, bias_ref, mtaps_ref, mbias_ref,
    alog_ref, dtb_ref, skip_ref, tail_own, tail_got, tap_row, gtaps_ref,
    pad, slope, signal_ref, scaled_ref, weighted_ref, sgrad_ref, imap_ref, omap_ref, wide3, intra,
    oh, gw, drow, m_out, xs, gs, es, xr, gr, er, yh, yc, lh, lc, first_local, first_sg, second_sg, lk,
    mg, mgot, gpad, rims, swap, stay, ddt_mine, ddt_got, ddt_ref,
    part, low_part, near, low_near, far, total, part_b, near_b, sum_b, far_b, total_b,
    l_sem, n_send, n_recv, b_send, b_recv, tap_send, tap_recv,
    xs_sem, xr_sem, gs_sem, gr_sem, es_sem, er_sem, hs_sem, hr_sem, cs_sem, cr_sem,
    ms_sem, mr_sem, r_sem, w_sem, q_send, q_near, q_far, q_near_b, q_far_b
):
    me = lax.axis_index("ctx")
    f = lax.axis_index("fsdp")
    odd = lax.rem(me, 2)
    mate = me + 1 - 2 * odd
    side_ctx = lax.rem(me + n - 1 + 2 * odd, n)
    slot = f // half
    first = 2 * (f - slot * half)
    group = f // 2
    side = f - 2 * group
    share = SIG // n
    per_head = n // HERE
    kept = pl.multiple_of(odd * BLK, BLK)
    given = pl.multiple_of((1 - odd) * BLK, BLK)
    ending = pl.multiple_of((1 - odd) * BLK + BLK - EDGE, EDGE)
    starts = (group, GROUPS + group, f)
    barrier = pltpu.get_barrier_semaphore()

    for i in range(1, n):
        signal(barrier, ctx=lax.rem(me + (i + 1) // 2 if i % 2 else me + n - i // 2, n))
    for k in range(2):

        @pl.when(group + k * half != f)
        def _():
            signal(barrier, fsdp=group + k * half)

        @pl.when(first + k != f)
        def _():
            signal(barrier, fsdp=first + k)

    def fetch(i, src, dst):
        copy = pltpu.make_async_copy(src, dst, l_sem.at[i])
        copy.start()
        return copy

    def third(k):
        return slice(k * STATE, (k + 1) * STATE)

    local = [
        fetch(0, mtaps_hbm, mtaps_ref),
        fetch(1, mbias_hbm, mbias_ref),
        fetch(2, dt_hbm, dt_in),
        fetch(3, alog_hbm, alog_ref),
        fetch(4, dtb_hbm, dtb_ref),
        fetch(5, skip_hbm, skip_ref),
        fetch(6, taps_hbm, taps_ref),
        fetch(7, bias_hbm, bias_ref),
        fetch(8, sig_hbm.at[pl.ds(kept, BLK)], sig_in.at[0:BLK]),
        fetch(9, dout_hbm.at[pl.ds(kept, BLK)], dout_ref.at[0:BLK]),
        fetch(10, sig_hbm.at[pl.ds(ending, EDGE)], tail_own.at[:, 0:SIG]),
    ]
    for k, start in enumerate(starts):
        local.append(
            fetch(
                11 + k,
                map_hbm.at[pl.ds(kept, BLK), columns(start)],
                map_in.at[0:BLK, third(k)],
            )
        )
        local.append(
            fetch(
                14 + k,
                map_hbm.at[pl.ds(ending, EDGE), columns(start)],
                tail_own.at[:, SIG + k * STATE : SIG + (k + 1) * STATE],
            )
        )

    tap_row[KSIZE + 1 :] = jnp.zeros((8 - KSIZE - 1, STATE), F32)
    selves = jnp.where(group == f, 1, 0) + jnp.where(group + half == f, 1, 0)
    pl.semaphore_wait(barrier, n - 1 + 4 - 2 * selves)

    def to_mate(i, src, dst):
        copy = remote(src, dst, n_send.at[i], n_recv.at[i], ctx=mate)
        copy.start()
        return copy

    def map_copy(k):
        return to_mate(
            1 + k, map_hbm.at[pl.ds(given, BLK), columns(starts[k])], map_in.at[BLK:ROWS, third(k)]
        )

    dt_copy = to_mate(0, dt_hbm, dt_got)
    out_copy = map_copy(1)
    dout_copy = to_mate(5, dout_hbm.at[pl.ds(given, BLK)], dout_ref.at[BLK:ROWS])
    for copy in local:
        copy.wait()
    tap_row[0:KSIZE] = mtaps_ref[...]
    tap_row[KSIZE : KSIZE + 1] = mbias_ref[...]
    for k in range(2):

        @pl.when(first + k != f)
        def _():
            remote(
                tap_row, gtaps_ref.at[slot], tap_send.at[k], tap_recv.at[slot], fsdp=first + k
            ).start()

        @pl.when(group + k * half == f)
        def _():
            gtaps_ref[k] = tap_row[...]

    def to_side(i, dst_cols):
        copy = remote(
            tail_own.at[:, dst_cols], tail_got.at[:, dst_cols], b_send.at[i], b_recv.at[i],
            ctx=side_ctx,
        )
        copy.start()
        return copy

    out_cols = slice(SIG + STATE, SIG + 2 * STATE)
    out_tail = to_side(0, out_cols)
    tails = [to_side(1, slice(0, SIG + STATE)), to_side(2, slice(SIG + 2 * STATE, WIDE))]
    map_copies = [map_copy(0), map_copy(2)]
    sig_copy = to_mate(4, sig_hbm.at[pl.ds(given, BLK)], sig_in.at[BLK:ROWS])

    lane = lax.broadcasted_iota(jnp.int32, (HERE, ROWS), 1)
    row_id = lax.broadcasted_iota(jnp.int32, (ROWS, ROWS), 0)
    col_id = lax.broadcasted_iota(jnp.int32, (ROWS, ROWS), 1)
    lower = ((row_id >= BLK) == (col_id >= BLK)) & (col_id <= row_id)
    lower_f = jnp.where(lower, 1.0, 0.0).astype(F32)
    eye = jnp.where(row_id == col_id, 1.0, 0.0).astype(F32)
    eye8 = eye[:HERE, :HERE]
    ones8 = jnp.ones((HERE, ROWS), F32)
    head1 = lax.broadcasted_iota(jnp.int32, (HERE, SIG), 0)
    spread1 = jnp.where(
        lax.broadcasted_iota(jnp.int32, (HERE, SIG), 1) // HDIM == head1, 1.0, 0.0
    ).astype(F32)

    def in_rows(ref):
        return nt(eye8, jnp.broadcast_to(ref[...], (ROWS, HERE)), HIGH)

    spread_low = spread1.astype(BF16)

    def halves(y):
        top = y.astype(BF16)
        return top, (y - top.astype(F32)).astype(BF16)

    def per_row(y):
        top, rest = halves(y)
        return nt(spread_low, top) + nt(spread_low, rest)

    def widened(x):
        top, rest = halves(x)
        return nn(top, spread_low) + nn(rest, spread_low)

    def turned(x):
        return pltpu.roll(x, BLK, 1)

    def preact(r, rows, cols, taps, bias):
        acc = bias
        for k in range(KSIZE):
            start = EDGE - RIM + k + r
            acc = acc + taps[k : k + 1] * pad[start : start + rows, cols]
        return acc

    def sig_rows(r, count):
        rows = slice(r, r + count)
        for q in range(SIG // STATE):
            cols = third(q)
            v = preact(r, count, cols, taps_ref[:, cols], bias_ref[:, cols])
            s = sigmoid(v)
            slope[rows, cols] = s * (1.0 + v * (1.0 - s))
            signal_ref[rows, cols] = (v * s).astype(BF16)

    pad[EDGE : EDGE + BLK, :SIG] = sig_in[:BLK, :].astype(F32)
    pad[EDGE : EDGE + BLK, SIG:] = map_in[:BLK, :].astype(F32)
    keep = jnp.where(me == 0, 0.0, 1.0).astype(F32)

    def before(cols):
        mine_then = tail_own[:, cols].astype(F32)
        pad[:EDGE, cols] = keep * jnp.where(me == n - 1, mine_then, tail_got[:, cols].astype(F32))

    dt_copy.wait()
    own, got = dt_in[...], dt_got[...]
    own = jnp.where(odd == 0, own, turned(own))
    got = jnp.where(odd == 0, turned(got), got)
    logits = jnp.where(lane < BLK, own, got) + in_rows(dtb_ref)
    rate = -jnp.exp(in_rows(alog_ref))
    step = jnp.maximum(logits, 0.0) + log1p_small(jnp.exp(-jnp.abs(logits)))
    ds = nt(step * rate, lower_f, HIGH)
    end_low = jnp.exp(ds[:, BLK - 1 : BLK])
    end_high = jnp.exp(ds[:, ROWS - 1 : ROWS])
    end = jnp.where(lane < BLK, ds[:, BLK - 1 : BLK], ds[:, ROWS - 1 : ROWS])
    to_end = jnp.exp(end - ds)
    col4 = nt(eye, jnp.concatenate([step, to_end, jnp.exp(ds), ds], axis=0), HIGH)
    ds_col = col4[:, 3 * HERE :]
    wide3[:, 2 * SIG :] = widened(col4[:, 2 * HERE : 3 * HERE])
    end_low8 = jnp.broadcast_to(end_low, (HERE, STATE))
    end_high8 = jnp.broadcast_to(end_high, (HERE, STATE))
    both_ends = end_low8 * end_high8
    for h in range(HERE):
        es[h] = both_ends[h : h + 1]

    def e_copy(d):
        return remote(es.at[d // per_head], er.at[me], es_sem.at[d], er_sem.at[me], ctx=d)

    def send_ends(i, _):
        e_copy(other(me, i, n)).start()
        return 0

    lax.fori_loop(1, n, send_ends, 0)
    er[me] = es[me // per_head]

    for k in range(2):

        @pl.when(group + k * half != f)
        def _():
            remote(
                tap_row, gtaps_ref.at[k], tap_send.at[k], tap_recv.at[k], fsdp=group + k * half
            ).wait_recv()

        @pl.when(first + k != f)
        def _():
            remote(
                tap_row, gtaps_ref.at[slot], tap_send.at[k], tap_recv.at[slot], fsdp=first + k
            ).wait_send()

    out_tail.wait()
    before(out_cols)
    def map_rows(k, out, r, count):
        cols = slice(SIG + k * STATE, SIG + (k + 1) * STATE)
        v = preact(r, count, cols, gtaps_ref[k, :KSIZE], gtaps_ref[k, KSIZE : KSIZE + 1])
        out[r : r + count, :] = (v * sigmoid(v)).astype(BF16)

    def sgrad_rows(rows):
        for q in range(QUADS):
            cols3 = slice(2 * SIG + q * STATE, 2 * SIG + (q + 1) * STATE)
            grad = dout_ref[rows, third(q)].astype(F32) * wide3[rows, cols3]
            sgrad_ref[rows, third(q)] = grad.astype(BF16)
        return tn(sgrad_ref[rows, :], omap_ref[rows, :])

    def mine(d):
        return pl.ds(pl.multiple_of(d * share, share), share)

    def x_copy(d):
        return remote(xs.at[mine(d)], xr.at[me], xs_sem.at[d], xr_sem.at[me], ctx=d)

    def g_copy(d):
        return remote(gs.at[d], gr.at[me], gs_sem.at[d], gr_sem.at[me], ctx=d)

    def h_copy(d):
        return remote(yh.at[d], lh.at[mine(me)], hs_sem.at[d], hr_sem.at[me], ctx=d)

    def c_copy(d):
        return remote(yc.at[d], lc.at[me], cs_sem.at[d], cr_sem.at[me], ctx=d)

    def send_g(i, _):
        g_copy(other(me, i, n)).start()
        return 0

    def send_x(i, _):
        x_copy(other(me, i, n)).start()
        return 0

    low, high = slice(0, BLK), slice(BLK, ROWS)
    map_rows(1, omap_ref, 0, BLK)
    first_sg[...] = sgrad_rows(low)
    out_copy.wait()
    pad[EDGE + BLK :, out_cols] = map_in[BLK:, third(1)].astype(F32)
    map_rows(1, omap_ref, BLK, BLK)
    dout_copy.wait()
    second_sg[...] = sgrad_rows(high)
    for h in range(HERE):
        at = slice(h * HDIM, (h + 1) * HDIM)
        link = first_sg[at, :] + end_low8[h : h + 1] * second_sg[at, :]
        top, rest = pack(link.reshape(per_head, share, STATE))
        gs[h * per_head : (h + 1) * per_head, :share, :] = top
        gs[h * per_head : (h + 1) * per_head, share:, :] = rest
    lax.fori_loop(1, n, send_g, 0)
    gr[me] = gs[me]

    wide3[:, :SIG] = widened(col4[:, :HERE])
    wide3[:, SIG : 2 * SIG] = widened(col4[:, HERE : 2 * HERE])
    for copy in tails + map_copies:
        copy.wait()
    for cols in (slice(0, SIG + STATE), slice(SIG + 2 * STATE, WIDE)):
        before(cols)
    pad[EDGE + BLK :, SIG : SIG + STATE] = map_in[BLK:, third(0)].astype(F32)
    pad[EDGE + BLK :, SIG + 2 * STATE :] = map_in[BLK:, third(2)].astype(F32)
    map_rows(0, imap_ref, 0, ROWS)
    v = preact(0, ROWS, slice(SIG + 2 * STATE, WIDE), mtaps_ref[...], mbias_ref[...])
    s = sigmoid(v)
    slope[:, SIG:] = s * (1.0 + v * (1.0 - s))
    sig_copy.wait()
    pad[EDGE + BLK :, :SIG] = sig_in[BLK:, :].astype(F32)
    sig_rows(0, ROWS)
    for q in range(QUADS):
        cols = third(q)
        cols2 = slice(SIG + q * STATE, SIG + (q + 1) * STATE)
        scaled_b = (signal_ref[:, cols].astype(F32) * wide3[:, cols]).astype(BF16)
        scaled_ref[:, cols] = scaled_b
        weighted_ref[:, cols] = (scaled_b.astype(F32) * wide3[:, cols2]).astype(BF16)
    first_local[...] = tn(weighted_ref[low, :], imap_ref[low, :])
    second_local = tn(weighted_ref[high, :], imap_ref[high, :])
    for h in range(HERE):
        at = slice(h * HDIM, (h + 1) * HDIM)
        xs[at, :] = (end_high8[h : h + 1] * first_local[at, :] + second_local[at, :]).astype(BF16)
    lax.fori_loop(1, n, send_x, 0)
    xr[me] = xs[mine(me)]

    score = nt(omap_ref[...], imap_ref[...])
    lane_row = lax.broadcasted_iota(jnp.int32, (ROWS, STATE), 1)
    grad_score = jnp.zeros((ROWS, ROWS), F32)
    for q in range(HERE // 2):
        cols = third(q)
        d_pair = dout_ref[:, cols].astype(F32)
        d_two = jnp.concatenate(
            [jnp.where(lane_row < HDIM, d_pair, 0.0), jnp.where(lane_row < HDIM, 0.0, d_pair)],
            axis=0,
        ).astype(BF16)
        grad_mix2 = nt(d_two, scaled_ref[:, cols])
        mixes = []
        for k in range(2):
            h = 2 * q + k
            grad_mix = grad_mix2[k * ROWS : (k + 1) * ROWS]
            gap = jnp.minimum(ds_col[:, h : h + 1] - ds[h : h + 1, :], 0.0)
            decay = jnp.where(lower, jnp.exp(gap), 0.0)
            mix = score * decay
            mixes.append(mix.astype(BF16))
            grad_score = grad_score + grad_mix * decay
            product = grad_mix * mix
            drow[h : h + 1, :] = nt(ones8, product, HIGH)[0:1] - jnp.sum(
                product, axis=0, keepdims=True
            )
        intra[:, cols] = tn(jnp.concatenate(mixes, axis=0), d_two)
    grad_score = grad_score.astype(BF16)
    mg[0] = tn(grad_score, omap_ref[...])
    mg[1] = nn(grad_score, imap_ref[...])

    def holder(i):
        return jnp.where(i < n // 2, 2 * i, 2 * (n - 1 - i) + 1)

    zero = jnp.zeros((share, STATE), F32)

    def g_arrived(i, _):
        s = other(me, i, n)
        remote(es.at[s // per_head], er.at[s], es_sem.at[s], er_sem.at[s], ctx=s).wait_recv()
        remote(gs.at[s], gr.at[s], gs_sem.at[s], gr_sem.at[s], ctx=s).wait_recv()
        return 0

    def to_front(i, g):
        at = holder(n - 1 - i)
        top, rest = pack(g[None])
        yc[at, :share, :] = top[0]
        yc[at, share:, :] = rest[0]
        got = gr[at]
        return er[at] * g + unpack(got[:share], got[share:])

    def send_c(i, _):
        c_copy(other(me, i, n)).start()
        return 0

    def x_arrived(i, _):
        s = other(me, i, n)
        remote(xs.at[mine(s)], xr.at[s], xs_sem.at[s], xr_sem.at[s], ctx=s).wait_recv()
        return 0

    def to_back(i, h):
        at = holder(i)
        yh[at] = h.astype(BF16)
        return er[at] * h + xr[at].astype(F32)

    def send_h(i, _):
        h_copy(other(me, i, n)).start()
        return 0

    lax.fori_loop(1, n, g_arrived, 0)
    lax.fori_loop(0, n, to_front, zero, unroll=4)
    lax.fori_loop(1, n, send_c, 0)
    lax.fori_loop(1, n, x_arrived, 0)
    lax.fori_loop(0, n, to_back, zero, unroll=4)
    lax.fori_loop(1, n, send_h, 0)
    lh[mine(me)] = yh[me]
    lc[me] = yc[me]
    step_w = wide3[:, :SIG]
    end_w = wide3[:, SIG : 2 * SIG]
    exp_w = wide3[:, 2 * SIG :]
    d_f = dout_ref[...].astype(F32)
    signal_f = signal_ref[...].astype(F32)
    skip_w = nn(jnp.broadcast_to(skip_ref[...], (HERE, HERE)), spread1, HIGH)[0:1]
    part[(KSIZE + 1) * QUADS :] = jnp.zeros((SUMS - (KSIZE + 1) * QUADS, STATE), F32)

    def small(at, row):
        at = KSIZE + 1 + at
        part_b[at : at + 1] = jnp.concatenate([row, jnp.zeros((1, STATE - HERE), F32)], axis=1)

    small(2, nt(ones8, per_row(d_f * signal_f), HIGH)[0:1])

    def m_copy(k):
        return remote(
            m_out.at[k], mgot.at[side], ms_sem.at[k], mr_sem.at[side], fsdp=group + k * half
        )

    def to_owner(k):
        m_out[k] = mg[k].astype(BF16)

        @pl.when(group + k * half != f)
        def _():
            m_copy(k).start()

        @pl.when(group + k * half == f)
        def _():
            mgot[side] = m_out[k]

    def c_in(i, _):
        d = other(me, i, n)
        g_copy(d).wait_send()
        e_copy(d).wait_send()
        remote(yc.at[d], lc.at[d], cs_sem.at[d], cr_sem.at[d], ctx=d).wait_recv()
        return 0

    lax.fori_loop(1, n, c_in, 0)
    for h in range(HERE):
        at = slice(h * HDIM, (h + 1) * HDIM)
        got = lc[h * per_head : (h + 1) * per_head]
        state = unpack(got[:, :share], got[:, share:]).reshape(HDIM, STATE)
        lk[3, at, :] = state.astype(BF16)
        lk[2, at, :] = (second_sg[at, :] + end_high8[h : h + 1] * state).astype(BF16)
    for b, rows in enumerate((low, high)):
        mg[0, rows, :] = mg[0, rows, :] + nn(weighted_ref[rows, :], lk[2 + b])
    to_owner(0)
    for b, rows in enumerate((low, high)):
        gw[rows, :] = nt(imap_ref[rows, :], lk[2 + b])
    gw_v = gw[...]
    back_row = per_row(gw_v * scaled_ref[...].astype(F32)) * to_end
    back_low = jnp.sum(jnp.where(lane < BLK, back_row, 0.0), axis=1, keepdims=True)
    back_high = jnp.sum(jnp.where(lane < BLK, 0.0, back_row), axis=1, keepdims=True)
    grad_scaled = gw_v * end_w + intra[...]
    own_step = per_row(grad_scaled * signal_f)
    gpad[:ROWS, :SIG] = (skip_w * d_f + grad_scaled * step_w) * slope[:, :SIG]

    def sums(cols, source, into, every, at):
        g = gpad[:ROWS, cols]
        for k in range(KSIZE):
            start = EDGE - RIM + k
            row = k * every + at
            into[row : row + 1] = jnp.sum(
                g * pad[start : start + ROWS, source], axis=0, keepdims=True
            )
        row = KSIZE * every + at
        into[row : row + 1] = jnp.sum(g, axis=0, keepdims=True)

    earlier = jnp.where(
        odd == 0, lax.rem(me + n - 2, n), jnp.where(me == n - 1, n - 2, lax.rem(me + 2, n))
    )
    earlier = jnp.where(me == 0, 1, earlier)

    def rim(i, cols):
        copy = remote(
            gpad.at[0:RIMS, cols], rims.at[:, cols], r_sem.at[2 * i], r_sem.at[2 * i + 1],
            ctx=earlier,
        )
        copy.start()
        return copy

    sig_cols, map_cols = slice(0, SIG), slice(SIG, OWN)
    sig_rim = rim(0, sig_cols)
    for q in range(QUADS):
        sums(third(q), third(q), part, QUADS, q)

    planes = n // 2
    y = me // planes
    z = me - y * planes
    z_high = z // 4
    z_low = z - 4 * z_high
    here = 4 * y + z_low
    sent = []

    def to_near(src, dst, at, recv_sem):
        for k in range(1, 8):
            s = lax.rem(here + k, 8)
            d = s // 4 * planes + z_high * 4 + s - s // 4 * 4
            copy = remote(src, dst.at[here], q_send.at[at + k], recv_sem.at[here], ctx=d)
            copy.start()
            sent.append(copy)
        dst[here] = src[...]

    def near_in(src, dst, recv_sem):
        for k in range(1, 8):
            s = lax.rem(here + k, 8)
            remote(src, dst.at[s], q_send.at[k], recv_sem.at[s], ctx=mate).wait_recv()

    def to_far(src, dst, at, recv_sem):
        for k in range(1, 4):
            s = lax.rem(z_high + k, 4)
            d = y * planes + 4 * s + z_low
            copy = remote(src, dst.at[z_high], q_send.at[at + k], recv_sem.at[z_high], ctx=d)
            copy.start()
            sent.append(copy)
        dst[z_high] = src[...]

    def far_in(src, dst, recv_sem):
        for k in range(1, 4):
            s = lax.rem(z_high + k, 4)
            remote(src, dst.at[s], q_send.at[k], recv_sem.at[s], ctx=mate).wait_recv()

    low_part[...] = part[...].astype(BF16)
    to_near(low_part, near, 0, q_near)

    def raw(r, out, taps, cols):
        acc = taps[RIM : RIM + 1] * gpad[r : r + BLK, cols]
        for k in range(RIM):
            acc = acc + taps[k : k + 1] * gpad[r + RIM - k : r + RIM - k + BLK, cols]
        out[:, cols] = acc

    def transposed(i, rim_copy, taps, cols, out):
        rim_copy.wait()
        gpad[ROWS:, cols] = jnp.where(me == 1, 0.0, rims[:, cols])
        raw(BLK, swap, taps, cols)
        away = remote(
            swap.at[:, cols], out.at[pl.ds(kept, BLK)], w_sem.at[2 * i], w_sem.at[2 * i + 1],
            ctx=mate,
        )
        away.start()
        raw(0, stay, taps, cols)
        return away, fetch(i, stay.at[:, cols], out.at[pl.ds(kept, BLK)])

    def h_in(i, _):
        d = other(me, i, n)
        x_copy(d).wait_send()
        remote(yh.at[d], lh.at[mine(d)], hs_sem.at[d], hr_sem.at[d], ctx=d).wait_recv()
        return 0

    lax.fori_loop(1, n, h_in, 0)
    lk[0] = lh[...]
    for h in range(HERE):
        at = slice(h * HDIM, (h + 1) * HDIM)
        lk[1, at, :] = (end_low8[h : h + 1] * lh[at, :].astype(F32) + first_local[at, :]).astype(
            BF16
        )
    for b, rows in enumerate((low, high)):
        mg[1, rows, :] = mg[1, rows, :] + nn(sgrad_ref[rows, :], lk[b])
    to_owner(1)
    end_terms = []
    for b, rows in enumerate((low, high)):
        oh[rows, :] = nt(omap_ref[rows, :], lk[b])
        both = lk[b].astype(F32) * lk[2 + b].astype(F32)
        both = jnp.sum(both.reshape(HERE, HDIM, STATE), axis=1)
        end_terms.append(jnp.sum(both, axis=1, keepdims=True))
    grad_sum = per_row(d_f * exp_w * oh[...]) - back_row + drow[...]
    last_low = back_low + end_low * end_terms[0]
    last_high = back_high + end_high * end_terms[1]
    grad_sum = grad_sum + jnp.where(
        lane == BLK - 1, last_low, jnp.where(lane == ROWS - 1, last_high, 0.0)
    )
    grad_log = nn(grad_sum, lower_f, HIGH)
    grad_step = grad_log * rate + own_step
    grad_dt = grad_step * sigmoid(logits)
    ddt_mine[...] = grad_dt
    ddt_copy = remote(ddt_mine, ddt_got, w_sem.at[0], w_sem.at[1], ctx=mate)
    ddt_copy.start()
    small(0, nt(ones8, grad_log * step, HIGH)[0:1] * (-jnp.exp(alog_ref[...])))
    small(1, nt(ones8, grad_dt, HIGH)[0:1])
    near_in(low_part, near, q_near)
    low_near[...] = jnp.sum(near[...].astype(F32), axis=0).astype(BF16)
    to_far(low_near, far, 7, q_far)

    for k in range(2):

        @pl.when(first + k != f)
        def _():
            remote(
                m_out.at[k], mgot.at[k], ms_sem.at[k], mr_sem.at[k], fsdp=first + k
            ).wait_recv()

    gpad[:ROWS, SIG:] = (mgot[0].astype(F32) + mgot[1].astype(F32)) * slope[:, SIG:]
    map_rim = rim(1, map_cols)
    sums(map_cols, slice(SIG + 2 * STATE, WIDE), part_b, 1, 0)
    to_near(part_b, near_b, 10, q_near_b)
    sig_out = transposed(1, sig_rim, taps_ref, sig_cols, dsig_hbm)
    map_out = transposed(2, map_rim, mtaps_ref, map_cols, dmap_hbm)
    near_in(part_b, near_b, q_near_b)
    sum_b[...] = jnp.sum(near_b[...], axis=0)
    to_far(sum_b, far_b, 17, q_far_b)
    ddt_copy.wait()
    own, got = ddt_mine[...], ddt_got[...]
    ddt_low = jnp.where(odd == 0, own, turned(got))
    ddt_high = jnp.where(odd == 0, got, turned(own))
    ddt_ref[...] = jnp.where(lane < BLK, ddt_low, ddt_high)
    ddt_out = fetch(3, ddt_ref, ddt_hbm)
    far_in(low_near, far, q_far)
    total[...] = jnp.sum(far[...].astype(F32), axis=0)
    sums_out = fetch(4, total, sums_hbm)

    def done(i, _):
        d = other(me, i, n)
        h_copy(d).wait_send()
        c_copy(d).wait_send()
        return 0

    lax.fori_loop(1, n, done, 0)
    for k in range(2):

        @pl.when(group + k * half != f)
        def _():
            m_copy(k).wait_send()

    far_in(sum_b, far_b, q_far_b)
    total_b[...] = jnp.sum(far_b[...], axis=0)
    small_out = fetch(5, total_b, small_hbm)
    for copy in sent:
        copy.wait_send()
    for copy in sig_out + map_out + (ddt_out, sums_out, small_out):
        copy.wait()


def main(*operands):
    n = lax.axis_size("ctx")
    half = lax.axis_size("fsdp") // 2
    share = SIG // n
    dma = pltpu.SemaphoreType.DMA
    vm = pltpu.VMEM
    return pl.pallas_call(
        functools.partial(main_kernel, n, half),
        out_shape=(
            jax.ShapeDtypeStruct((ROWS, SIG), F32),
            jax.ShapeDtypeStruct((ROWS, STATE), F32),
            jax.ShapeDtypeStruct((SUMS, STATE), F32),
            jax.ShapeDtypeStruct((8, STATE), F32),
            jax.ShapeDtypeStruct((HERE, ROWS), F32),
        ),
        in_specs=[pl.BlockSpec(memory_space=pl.ANY)] * len(operands),
        out_specs=(HBM,) * 5,
        scratch_shapes=[
            vm((ROWS, SIG), BF16),
            vm((ROWS, 3 * STATE), BF16),
            vm((ROWS, SIG), BF16),
            vm((HERE, ROWS), F32),
            vm((HERE, ROWS), F32),
            vm((KSIZE, SIG), F32),
            vm((1, SIG), F32),
            vm((KSIZE, STATE), F32),
            vm((1, STATE), F32),
            vm((1, HERE), F32),
            vm((1, HERE), F32),
            vm((1, HERE), F32),
            vm((EDGE, WIDE), BF16),
            vm((EDGE, WIDE), BF16),
            vm((8, STATE), F32),
            vm((2, 8, STATE), F32),
            vm((EDGE + ROWS, WIDE), F32),
            vm((ROWS, OWN), F32),
            vm((ROWS, SIG), BF16),
            vm((ROWS, SIG), BF16),
            vm((ROWS, SIG), BF16),
            vm((ROWS, SIG), BF16),
            vm((ROWS, STATE), BF16),
            vm((ROWS, STATE), BF16),
            vm((ROWS, 3 * SIG), F32),
            vm((ROWS, SIG), F32),
            vm((ROWS, SIG), F32),
            vm((ROWS, SIG), F32),
            vm((HERE, ROWS), F32),
            vm((2, ROWS, STATE), BF16),
            vm((SIG, STATE), BF16),
            vm((n, 3 * share // 2, STATE), BF16),
            vm((HERE, 1, STATE), F32),
            vm((n, share, STATE), BF16),
            vm((n, 3 * share // 2, STATE), BF16),
            vm((n, 1, STATE), F32),
            vm((n, share, STATE), BF16),
            vm((n, 3 * share // 2, STATE), BF16),
            vm((SIG, STATE), BF16),
            vm((n, 3 * share // 2, STATE), BF16),
            vm((SIG, STATE), F32),
            vm((SIG, STATE), F32),
            vm((SIG, STATE), F32),
            vm((4, SIG, STATE), BF16),
            vm((2, ROWS, STATE), F32),
            vm((2, ROWS, STATE), BF16),
            vm((ROWS + RIMS, OWN), F32),
            vm((RIMS, OWN), F32),
            vm((BLK, OWN), F32),
            vm((BLK, OWN), F32),
            vm((HERE, ROWS), F32),
            vm((HERE, ROWS), F32),
            vm((HERE, ROWS), F32),
            vm((SUMS, STATE), F32),
            vm((SUMS, STATE), BF16),
            vm((8, SUMS, STATE), BF16),
            vm((SUMS, STATE), BF16),
            vm((4, SUMS, STATE), BF16),
            vm((SUMS, STATE), F32),
            vm((8, STATE), F32),
            vm((8, 8, STATE), F32),
            vm((8, STATE), F32),
            vm((4, 8, STATE), F32),
            vm((8, STATE), F32),
        ]
        + [dma((17,)), dma((6,)), dma((6,)), dma((3,)), dma((3,)), dma((2,)), dma((2,))]
        + [dma((n,))] * 10
        + [dma((2,)), dma((2,)), dma((4,)), dma((6,)), dma((21,)), dma((8,)), dma((4,)), dma((8,)), dma((4,))],
        compiler_params=pltpu.CompilerParams(
            collective_id=0, has_side_effects=True, vmem_limit_bytes=56 * 1024 * 1024
        ),
        name="main",
    )(*operands)


def last_kernel(
    scale, dsig_in, dmap_in, sums_in, small_in, ddt_in,
    dsig, dmap, ddt, dtaps, dmtaps, dbias, dmbias, dalog, ddtb, dskip
):
    dsig[...] = dsig_in[...]
    dmap[...] = dmap_in[...]
    ddt[...] = ddt_in[...]
    for k in range(KSIZE + 1):
        for q in range(QUADS):
            at = k * QUADS + q
            cols = slice(q * STATE, (q + 1) * STATE)
            row = sums_in[at : at + 1] * scale
            if k < KSIZE:
                dtaps[k : k + 1, cols] = row
            else:
                dbias[:, cols] = row
    dmtaps[...] = small_in[:KSIZE] * scale
    dmbias[...] = small_in[KSIZE : KSIZE + 1] * scale
    for k, out in enumerate((dalog, ddtb, dskip)):
        at = KSIZE + 1 + k
        out[...] = small_in[at : at + 1, :HERE] * scale


def last(*operands):
    scale = 1.0 / math.sqrt(float(lax.axis_size("ctx") * ROWS))
    shapes = (
        (ROWS, SIG), (ROWS, STATE), (HERE, ROWS), (KSIZE, SIG), (KSIZE, STATE),
        (1, SIG), (1, STATE), (1, HERE), (1, HERE), (1, HERE),
    )
    return pl.pallas_call(
        functools.partial(last_kernel, scale),
        out_shape=tuple(jax.ShapeDtypeStruct(s, F32) for s in shapes),
        in_specs=[VM] * 5,
        out_specs=(VM,) * len(shapes),
        compiler_params=pltpu.CompilerParams(vmem_limit_bytes=60 * 1024 * 1024),
        name="last",
    )(*operands)


def shards(
    sig_raw,
    map_raw,
    step_size_logits,
    d_out,
    sig_taps,
    map_taps,
    sig_bias,
    map_bias,
    a_log,
    dt_bias,
    skip_gain,
):
    found = main(
        sig_raw, map_raw, step_size_logits.T, d_out, sig_taps, sig_bias[None, :], map_taps,
        map_bias[None, :], a_log[None, :], dt_bias[None, :], skip_gain[None, :],
    )
    out = last(*found)
    return out[:2] + (out[2].T,) + out[3:5] + tuple(a.reshape(-1) for a in out[5:])


def solution(mesh):
    return jax.shard_map(
        shards,
        mesh=mesh,
        in_specs=(
            P("ctx", "fsdp"),
            P("ctx", None),
            P("ctx", "fsdp"),
            P("ctx", "fsdp"),
            P(None, "fsdp"),
            P(None, "fsdp"),
            P("fsdp"),
            P("fsdp"),
            P("fsdp"),
            P("fsdp"),
            P("fsdp"),
        ),
        out_specs=(
            P("ctx", "fsdp"),
            P("ctx", "fsdp"),
            P("ctx", "fsdp"),
            P(None, "fsdp"),
            P(None, "fsdp"),
            P("fsdp"),
            P("fsdp"),
            P("fsdp"),
            P("fsdp"),
            P("fsdp"),
        ),
        check_vma=False,
    )
```
